32 devices in a mesh: dp: 2 (over x), row: 4 (over y, core), col: 4 (over z).
Axes of the slice: x: 2, y: 2, z: 4, core: 2. Of those that a mesh axis runs over, the one named last changes fastest.
Arguments:
- block_input: bfloat16 [2, 6304, 384], P(None, ('dp', 'row', 'col')), may hold values from -6 to 6
- first_gain: bfloat16 [384], P('col'), may hold values from 0.25 to 1.75
- first_bias: bfloat16 [384], P('col'), may hold values from -2.5 to 2.5
- project_in: bfloat16 [384, 1152], P('col', 'row'), may hold values from -0.3125 to 0.3125
- project_out: bfloat16 [384, 384], P('row', 'col'), may hold values from -1.5 to 1.5
- second_gain: bfloat16 [384], P('col'), may hold values from 0.25 to 1.75
- second_bias: bfloat16 [384], P('col'), may hold values from -2.5 to 2.5
- router_weight: bfloat16 [384, 32], P('col', 'row'), may hold values from -0.15625 to 0.15625
- expert_up: bfloat16 [32, 384, 1536], P(None, 'col', 'row'), may hold values from -0.3125 to 0.3125
- expert_down: bfloat16 [32, 384, 1536], P(None, 'col', 'row'), may hold values from -0.3125 to 0.3125
- routes: int32 [2, 6304, 2], P(None, 'dp'), may hold values from 0 to 31, all different within a row; in each aligned block of 3152 rows (0 to 3151, 3152 to 6303, ..., all dimensions but the last counted through in order) at most 246 rows name the same one
- out_grad: bfloat16 [2, 6304, 384], P(None, ('dp', 'row', 'col')), may hold values from -6 to 6
Outputs:
- block_output: bfloat16 [2, 6304, 384], P(None, ('dp', 'row', 'col'))
- input_grad: float32 [2, 6304, 384], P(None, ('dp', 'row', 'col'))
- first_gain_grad: float32 [384], P('col')
- first_bias_grad: float32 [384], P('col')
- project_in_grad: float32 [384, 1152], P('col', 'row')
- project_out_grad: float32 [384, 384], P('row', 'col')
- second_gain_grad: float32 [384], P('col')
- second_bias_grad: float32 [384], P('col')
- router_grad: float32 [384, 32], P('col', 'row')
- expert_up_grad: float32 [32, 384, 1536], P('dp', 'col', 'row')
- expert_down_grad: float32 [32, 384, 1536], P('dp', 'col', 'row')
The draws below stay inside these ranges and needn't reach their ends.
Inputs may be any that keep to these rules, and one draw needn't show every extreme that they name: `routes`: within each micro-batch, the 3152 consecutive tokens that begin at a multiple of 3152 name each expert at most 246 times, and in some of these blocks one expert exactly 246 times. The 2 experts of a token differ.
All inputs are finite; a program needn't handle non-finite values.
Results may differ from the reference program's by a relative error of at most 0.013.
Values may be sent and summed in bfloat16 or wider, within the bound.
A program may use at most 192 MiB of HBM per device.

```python
import math
import jax
import jax.numpy as jnp
import numpy as np
from jax import lax

D = 384
HEADS = 6
HEAD = 64
FF = 1536
EXPERTS = 32
TOP = 2
SEQ = 197
MICRO = 2
T_GROUP = 3152
TOK_MB = 6304
CAP = 246


def steps_of(rng, extent, split, smallest, high):
    def one(dim, blocks):
        draws = jax.random.uniform(jax.random.fold_in(jax.random.fold_in(rng, 6), dim), (blocks,), jnp.float32, smallest / len(split), high / len(split))
        return jnp.repeat(jnp.exp(draws), extent[dim] // blocks).reshape((-1,) + (1,) * (len(extent) - dim - 1))

    loudness = one(*split[0])
    for cut in split[1:]:
        loudness = loudness * one(*cut)
    return loudness


def routed_block(key, own, number, rows, number_of, top, limit, slope):
    sequence = jax.random.permutation(key, number_of)
    heavy_load, common = load_shares(number_of, rows * top, limit, slope, True), load_shares(number_of, rows * top, limit, slope, False)
    places = jnp.arange(number_of)

    def named(lengths, turn):
        used = int((lengths > 0).sum())
        fixed = max(1, used // 4)
        shifted = fixed + (places - fixed + turn * (used - fixed)) % max(1, number_of - fixed)
        return jnp.zeros((number_of,), jnp.int32).at[sequence[jnp.where(places < fixed, places, shifted)]].set(jnp.asarray(lengths, jnp.int32))

    lengths = jnp.where(number % 4 == 0, named(heavy_load, number // 4), named(common, number - number // 4 - 1))
    mixed = jax.random.permutation(jax.random.fold_in(own, 3), number_of)
    donor, receiver = mixed[0:number_of // 2 * 2:2], mixed[1:number_of // 2 * 2:2]
    margin = jnp.minimum(lengths[donor] - 1, limit - lengths[receiver]) // 2
    margin = jnp.where((donor == sequence[0]) | (receiver == sequence[0]) | (lengths[receiver] == 0), 0, jnp.maximum(margin, 0))
    shifted = jax.random.randint(jax.random.fold_in(own, 4), (number_of // 2,), 0, 1 << 20) % (margin + 1)
    lengths = lengths.at[donor].add(-shifted).at[receiver].add(shifted)
    members = jnp.searchsorted(jnp.cumsum(lengths), jnp.arange(rows * top), side="right").astype(jnp.int32)
    grid = members.reshape(top, rows).T
    grid = grid[jax.random.permutation(jax.random.fold_in(own, 1), rows)]
    turn = jax.random.randint(jax.random.fold_in(own, 2), (rows, 1), 0, top)
    return jnp.take_along_axis(grid, (jnp.arange(top)[None, :] + turn) % top, axis=1)


def load_shares(amount, total, limit, skew, full):
    portions = [(1 << 20) // math.isqrt(grade ** skew) + 1 for grade in range(1, amount + 1)]
    largest = limit if full else min(limit, max(-(-total // amount), total * portions[0] // sum(portions)))
    least = 1 if total - largest >= amount - 1 else 0
    holding, spare = [largest] + [least] * (amount - 1), total - largest - least * (amount - 1)
    while spare > 0:
        candidates = [i for i in range(1, amount) if holding[i] < largest] or [i for i in range(1, amount) if holding[i] < limit]
        pool, left = sum([portions[i] for i in candidates]), spare
        for i in candidates:
            more = min(limit - holding[i], max(1, left * portions[i] // pool), spare)
            holding[i] = holding[i] + more
            spare = spare - more
    return np.array(holding)


def noise(key, dims, width, bound, cuts=(), kind=jnp.bfloat16):
    loudness = steps_of(key, dims, cuts, -0.22, 0.18) if cuts else 1.0
    array = jax.random.normal(key, dims, jnp.float32) * width * loudness
    return jnp.minimum(jnp.maximum(array, -bound), bound).astype(kind)


def setup_inputs(seed: int = 0) -> dict:
    keys = jax.random.split(jax.random.key(seed), 13)
    block_input = noise(keys[0], (MICRO, TOK_MB, D), 1.0, 6.0, ((1, 32),))
    first_gain = jnp.clip(1.0 + 0.15 * jax.random.normal(keys[1], (D,), jnp.float32), 0.25, 1.75).astype(jnp.bfloat16)
    first_bias = noise(keys[2], (D,), 0.3, 2.5, ((0, 4),))
    project_in = noise(keys[3], (D, 3 * D), D ** -0.5, 0.3125, ((0, 4), (1, 4)))
    project_out = noise(keys[4], (D, D), (D // 24) ** -0.5, 1.5, ((0, 4), (1, 4)))
    second_gain = jnp.clip(1.0 + 0.15 * jax.random.normal(keys[5], (D,), jnp.float32), 0.25, 1.75).astype(jnp.bfloat16)
    second_bias = noise(keys[6], (D,), 0.3, 2.5, ((0, 4),))
    router_weight = noise(keys[7], (D, EXPERTS), (4 * D) ** -0.5, 0.15625, ((0, 4), (1, 4)))
    expert_up = noise(keys[8], (EXPERTS, D, FF), D ** -0.5, 0.3125, ((1, 4), (2, 4)))
    expert_down = noise(keys[9], (EXPERTS, D, FF), (FF // 4) ** -0.5, 0.3125, ((1, 4), (2, 4)))
    routes_keys = jax.random.split(jax.random.fold_in(keys[10], 1), MICRO * TOK_MB // T_GROUP)
    routes_turns = jax.random.permutation(jax.random.fold_in(keys[10], 3), MICRO * TOK_MB // T_GROUP)
    routes = jax.vmap(lambda own, number: routed_block(jax.random.fold_in(keys[10], 2), own, number, T_GROUP, EXPERTS, TOP, CAP, 1))(routes_keys, routes_turns).reshape((MICRO, TOK_MB, TOP))
    out_grad = noise(keys[11], (MICRO, TOK_MB, D), 1.0, 6.0, ((1, 32),))
    return dict(block_input=block_input, first_gain=first_gain, first_bias=first_bias, project_in=project_in, project_out=project_out, second_gain=second_gain, second_bias=second_bias, router_weight=router_weight, expert_up=expert_up, expert_down=expert_down, routes=routes, out_grad=out_grad)


@jax.custom_vjp
def low(v):
    return lax.optimization_barrier(v.astype(jnp.bfloat16)).astype(jnp.float32)

@jax.custom_vjp
def low_back(v):
    return v

def low_keep(v):
    return (low(v), None)

def low_pass(kept, grad):
    return (grad,)

def back_keep(v):
    return (v, None)

def back_low(kept, grad):
    return (low(grad),)
low.defvjp(low_keep, low_pass)
low_back.defvjp(back_keep, back_low)
highest = lax.Precision.HIGHEST

def norm_rows(stream, gain_vec, bias_vec):
    mean_val = lax.optimization_barrier(jnp.mean(stream, axis=-1, keepdims=True))
    spread = lax.optimization_barrier(jnp.mean(stream * stream, axis=-1, keepdims=True)) - mean_val * mean_val
    return (stream - mean_val) * lax.rsqrt(spread + 1e-06) * gain_vec + bias_vec

def route_tables(route_rows):
    pair_ids = route_rows.reshape(-1).astype(jnp.int32)
    pair_total = pair_ids.shape[0]
    onehot = (pair_ids[:, None] == jnp.arange(EXPERTS, dtype=jnp.int32)[None, :]).astype(jnp.int32)
    earlier = jnp.cumsum(onehot, axis=0) - onehot
    position = lax.optimization_barrier(jnp.sum(earlier * onehot, axis=1))
    slot_of_pair = (pair_ids * CAP + position).astype(jnp.int32)
    source = jnp.full((EXPERTS * CAP,), pair_total, jnp.int32).at[slot_of_pair].set(jnp.arange(pair_total, dtype=jnp.int32))
    return (slot_of_pair, source)

def group_layer(stream, route_rows, params):
    first_gain, first_bias, project_in, project_out, second_gain, second_bias, router_weight, expert_up, expert_down = params
    token_count = stream.shape[0]
    normed_one = low(norm_rows(stream, first_gain, first_bias))
    triple = low_back(low(jnp.dot(normed_one, project_in, precision=highest)))
    pieces = triple.reshape(token_count // SEQ, SEQ, 3, HEADS, HEAD)
    queries, key_vecs, values = (pieces[:, :, 0], pieces[:, :, 1], pieces[:, :, 2])
    scores = low_back(jnp.einsum('ishd,ithd->ihst', queries, key_vecs, precision=highest) * HEAD ** (-0.5))
    attn_weights = low(jax.nn.softmax(scores, axis=-1))
    mixed_rows = low_back(low(jnp.einsum('ihst,ithd->ishd', attn_weights, values, precision=highest))).reshape(token_count, D)
    hidden_one = stream + low_back(jnp.dot(mixed_rows, project_out, precision=highest))
    normed_two = low(norm_rows(hidden_one, second_gain, second_bias))
    logits = jnp.dot(normed_two, router_weight, precision=highest)
    gate_vals = jax.nn.softmax(jnp.take_along_axis(logits, route_rows, axis=1), axis=-1)
    slot_of_pair, source = route_tables(route_rows)
    padded_in = jnp.concatenate([normed_two, jnp.zeros((1, D), jnp.float32)], axis=0)
    slot_inputs = padded_in[source // TOP].reshape(EXPERTS, CAP, D)
    hidden_slots = jnp.einsum('ecd,edf->ecf', slot_inputs, expert_up, precision=highest).reshape(EXPERTS * CAP, FF)
    pre_act = low_back(hidden_slots[slot_of_pair].reshape(token_count, TOP, FF))
    scaled = low(gate_vals[:, :, None] * jax.nn.gelu(pre_act, approximate=False))
    padded_scaled = jnp.concatenate([scaled.reshape(token_count * TOP, FF), jnp.zeros((1, FF), jnp.float32)], axis=0)
    down_inputs = padded_scaled[source].reshape(EXPERTS, CAP, FF)
    out_slots = jnp.einsum('ecf,edf->ecd', down_inputs, expert_down, precision=highest).reshape(EXPERTS * CAP, D)
    branch = low_back(lax.optimization_barrier(jnp.sum(out_slots[slot_of_pair].reshape(token_count, TOP, D), axis=1)))
    return hidden_one + branch

def reference(block_input, first_gain, first_bias, project_in, project_out, second_gain, second_bias, router_weight, expert_up, expert_down, routes, out_grad):
    floats = tuple((argument.astype(jnp.float32) for argument in (block_input, first_gain, first_bias, project_in, project_out, second_gain, second_bias, router_weight, expert_up, expert_down)))
    route_groups = routes.reshape(-1, T_GROUP, TOP)

    def forward(stream, *params):
        groups = stream.reshape(-1, T_GROUP, D)
        step_fn = jax.checkpoint(lambda group_pair: group_layer(group_pair[0], group_pair[1], params))
        return lax.map(step_fn, (groups, route_groups)).reshape(stream.shape)
    result, pullback = jax.vjp(forward, *floats)
    grads = pullback(out_grad.astype(jnp.float32))
    return (result.astype(jnp.bfloat16), grads[0], grads[1], grads[2], grads[3], grads[4], grads[5], grads[6], grads[7], grads[8], grads[9])
```

```python
import jax
import jax.numpy as jnp
from jax import lax
from jax.sharding import PartitionSpec as P

D = 384
HEADS = 6
HEAD = 64
TOP = 2
SEQ = 197
ROWS = 208
SLOTS = 256

sqrt_half = 0.7071067811865476
inv_root_tau = 0.3989422804014327
plane = ("row", "col")
bf16 = jnp.bfloat16
f32 = jnp.float32


def mm(spec, left, right):
    return jnp.einsum(spec, left, right, preferred_element_type=f32)


def norm_forward(stream, gain_vec, bias_vec):
    mean_val = jnp.mean(stream, axis=-1, keepdims=True)
    spread = jnp.mean(stream * stream, axis=-1, keepdims=True) - mean_val * mean_val
    inverse = lax.rsqrt(spread + 1e-06)
    normal = (stream - mean_val) * inverse
    return (normal, inverse, (normal * gain_vec + bias_vec).astype(bf16))


def norm_backward(grad_out, normal, inverse, gain_vec):
    scaled = grad_out * gain_vec
    grad_in = inverse * (
        scaled
        - jnp.mean(scaled, axis=-1, keepdims=True)
        - normal * jnp.mean(scaled * normal, axis=-1, keepdims=True)
    )
    return (grad_in, jnp.sum(grad_out * normal, axis=(0, 1)), jnp.sum(grad_out, axis=(0, 1)))


def split_heads(triple):
    images = triple.shape[0]
    pieces = triple.reshape(images, SEQ, 3, HEADS, HEAD)
    return (pieces[:, :, 0], pieces[:, :, 1], pieces[:, :, 2])


def on_device(
    block_input,
    first_gain,
    first_bias,
    project_in,
    project_out,
    second_gain,
    second_bias,
    router_weight,
    expert_up,
    expert_down,
    routes,
    out_grad,
):
    micro = block_input.shape[0]
    row_count = lax.axis_size("row")
    col_count = lax.axis_size("col")
    shares = row_count * col_count
    experts = expert_up.shape[0]
    own = experts // shares
    rank = lax.axis_index("row") * col_count + lax.axis_index("col")
    d_part = D // col_count
    f_part = expert_up.shape[2]

    small = jnp.concatenate(
        [
            v.reshape(-1)
            for v in (
                project_in,
                project_out,
                router_weight,
                first_gain,
                first_bias,
                second_gain,
                second_bias,
            )
        ]
    )
    gathered = lax.all_gather(small, plane, axis=0).reshape(row_count, col_count, -1)
    offset = 0

    def take(v):
        nonlocal offset
        piece = gathered[:, :, offset : offset + v.size].reshape((row_count, col_count) + v.shape)
        offset += v.size
        return piece

    w_in = take(project_in).transpose(1, 2, 0, 3).reshape(D, -1)
    w_out = take(project_out).transpose(0, 2, 1, 3).reshape(D, -1)
    w_router = take(router_weight).transpose(1, 2, 0, 3).reshape(D, -1)
    gain_one, bias_one, gain_two, bias_two = (
        take(v)[0].reshape(-1).astype(f32) for v in (first_gain, first_bias, second_gain, second_bias)
    )

    def fetch(weight):
        parts = weight.reshape(own, shares, d_part, f_part)
        got = lax.all_to_all(parts, plane, split_axis=1, concat_axis=1, tiled=True)
        got = got.reshape(own, row_count, col_count, d_part, f_part)
        return got.transpose(0, 2, 3, 1, 4).reshape(own, D, row_count * f_part)

    up = fetch(expert_up)
    down = fetch(expert_down)

    def to_plane(rows):
        padded = jnp.pad(rows, ((0, 0), (0, ROWS - SEQ), (0, 0)))
        return lax.all_gather(padded, plane, axis=1, tiled=True)

    grad_rows = to_plane(out_grad)

    stream = block_input.astype(f32)
    normal_one, inverse_one, normed_one = norm_forward(stream, gain_one, bias_one)
    triple = mm("isd,df->isf", normed_one, w_in).astype(bf16)
    queries, key_vecs, values = split_heads(triple)
    scores = mm("ishd,ithd->ihst", queries, key_vecs) * HEAD ** (-0.5)
    prob = jax.nn.softmax(scores, axis=-1)
    attn_weights = prob.astype(bf16)
    mixed = mm("ihst,ithd->ishd", attn_weights, values).astype(bf16).reshape(micro, SEQ, D)
    hidden_one = stream + mm("isd,df->isf", mixed, w_out)
    normal_two, inverse_two, normed_two = norm_forward(hidden_one, gain_two, bias_two)

    token_rows = to_plane(normed_two)

    places = routes.reshape(micro, shares, SEQ, TOP)
    places = jnp.pad(places, ((0, 0), (0, 0), (0, ROWS - SEQ), (0, 0)), constant_values=-1)
    places = places.reshape(micro, shares * ROWS, TOP)
    logits = mm("itd,de->ite", token_rows, w_router)
    picked = places[..., None] == jnp.arange(experts, dtype=jnp.int32)
    pair_logits = jnp.sum(jnp.where(picked, logits[:, :, None, :], 0.0), axis=-1)
    gates = jax.nn.softmax(pair_logits, axis=-1)
    own_ids = rank + shares * jnp.arange(own, dtype=jnp.int32)
    own_mask = places[:, None, :, :] == own_ids[None, :, None, None]
    routed = jnp.any(own_mask, axis=-1)
    gate_row = jnp.sum(jnp.where(own_mask, gates[:, None], 0.0), axis=-1)
    position = jnp.cumsum(routed.astype(jnp.int32), axis=-1) - 1
    position = jnp.where(routed, position, -1)
    pick = (position[:, :, None, :] == jnp.arange(SLOTS, dtype=jnp.int32)[:, None]).astype(bf16)
    slot_gate = jnp.sum(pick.astype(f32) * gate_row[:, :, None, :], axis=-1, keepdims=True)

    slot_x = mm("iest,itd->iesd", pick, token_rows).astype(bf16)
    slot_g = mm("iest,itd->iesd", pick, grad_rows).astype(bf16)
    pre_act = mm("iesd,edf->iesf", slot_x, up)
    cdf = 0.5 * (1.0 + lax.erf(pre_act * sqrt_half))
    act = pre_act * cdf
    scaled = (slot_gate * act).astype(bf16)
    out_slots = mm("iesf,edf->iesd", scaled, down).astype(bf16)
    grad_scaled = mm("iesd,edf->iesf", slot_g, down)
    grad_gate_slot = jnp.sum(grad_scaled * act, axis=-1)
    slope = cdf + pre_act * jnp.exp(-0.5 * pre_act * pre_act) * inv_root_tau
    grad_pre = (slot_gate * grad_scaled * slope).astype(bf16)
    back_slots = mm("iesf,edf->iesd", grad_pre, up).astype(bf16)
    up_grad = mm("iesd,iesf->edf", slot_x, grad_pre)
    down_grad = mm("iesd,iesf->edf", slot_g, scaled)
    branch_part = mm("iest,iesd->itd", pick, out_slots)
    back_part = mm("iest,iesd->itd", pick, back_slots)
    gate_token = jnp.sum(pick.astype(f32) * grad_gate_slot[..., None], axis=2)
    gate_part = jnp.sum(jnp.where(own_mask, gate_token[..., None], 0.0), axis=1)

    def to_owner(part):
        pieces = part.astype(bf16).reshape(micro, shares, ROWS, -1)
        got = lax.all_to_all(pieces, plane, split_axis=1, concat_axis=1, tiled=True)
        return jnp.sum(got.astype(f32), axis=1)[:, :SEQ]

    grad_norm_two = to_owner(back_part)
    branch = to_owner(branch_part)
    grad_gate = lax.psum(gate_part, plane)
    start = rank * ROWS
    grad_gate = lax.dynamic_slice_in_dim(grad_gate, start, SEQ, axis=1)
    gate_own = lax.dynamic_slice_in_dim(gates, start, SEQ, axis=1)
    route_own = lax.dynamic_slice_in_dim(places, start, SEQ, axis=1)
    block_output = (hidden_one + branch).astype(bf16)

    grad_logit = gate_own * (grad_gate - jnp.sum(gate_own * grad_gate, axis=-1, keepdims=True))
    dense_logit = jnp.sum(
        jnp.where(
            route_own[..., None] == jnp.arange(experts, dtype=jnp.int32), grad_logit[..., None], 0.0
        ),
        axis=2,
    )
    exact = lax.Precision.HIGHEST
    router_grad = jnp.einsum("isd,ise->de", normed_two.astype(f32), dense_logit, precision=exact)
    grad_norm_two = grad_norm_two + jnp.einsum(
        "ise,de->isd", dense_logit, w_router.astype(f32), precision=exact
    )
    grad_part, gain_two_grad, bias_two_grad = norm_backward(
        grad_norm_two, normal_two, inverse_two, gain_two
    )
    grad_hidden = out_grad.astype(f32) + grad_part
    grad_attn = grad_hidden.astype(bf16)
    out_weight_grad = mm("isd,isf->df", mixed, grad_attn)
    grad_mixed = mm("isf,df->isd", grad_attn, w_out).astype(bf16)
    grad_heads = grad_mixed.reshape(micro, SEQ, HEADS, HEAD)
    grad_values = mm("ihst,ishd->ithd", attn_weights, grad_heads)
    grad_prob = mm("ishd,ithd->ihst", grad_heads, values)
    grad_scores = (prob * (grad_prob - jnp.sum(prob * grad_prob, axis=-1, keepdims=True))).astype(bf16)
    grad_queries = mm("ihst,ithd->ishd", grad_scores, key_vecs) * HEAD ** (-0.5)
    grad_keys = mm("ihst,ishd->ithd", grad_scores, queries) * HEAD ** (-0.5)
    grad_triple = jnp.stack([grad_queries, grad_keys, grad_values], axis=2).astype(bf16)
    grad_triple = grad_triple.reshape(micro, SEQ, 3 * HEADS * HEAD)
    in_weight_grad = mm("isd,isf->df", normed_one, grad_triple)
    grad_norm_one = mm("isf,df->isd", grad_triple, w_in)
    grad_part, gain_one_grad, bias_one_grad = norm_backward(
        grad_norm_one, normal_one, inverse_one, gain_one
    )
    input_grad = grad_hidden + grad_part

    def give(grad):
        parts = grad.astype(bf16).reshape(own, col_count, d_part, row_count, f_part)
        parts = parts.transpose(0, 3, 1, 2, 4).reshape(own, shares, d_part, f_part)
        got = lax.all_to_all(parts, plane, split_axis=1, concat_axis=1, tiled=True)
        got = got.reshape(experts, d_part, f_part)
        return lax.psum_scatter(got, "dp", scatter_dimension=0, tiled=True).astype(f32)

    expert_up_grad = give(up_grad)
    expert_down_grad = give(down_grad)

    def blocks(grad, row_axis):
        if row_axis is None:
            piece = grad.reshape(1, col_count, -1)
            return jnp.broadcast_to(piece, (row_count, col_count, piece.shape[2]))
        if row_axis == 1:
            piece = grad.reshape(col_count, D // col_count, row_count, -1).transpose(2, 0, 1, 3)
        else:
            piece = grad.reshape(row_count, D // row_count, col_count, -1).transpose(0, 2, 1, 3)
        return piece.reshape(row_count, col_count, -1)

    packed = jnp.concatenate(
        [
            blocks(in_weight_grad, 1),
            blocks(out_weight_grad, 0),
            blocks(router_grad, 1),
            blocks(gain_one_grad, None),
            blocks(bias_one_grad, None),
            blocks(gain_two_grad, None),
            blocks(bias_two_grad, None),
        ],
        axis=2,
    ).reshape(shares, -1)
    got = lax.all_to_all(packed.astype(bf16), plane, split_axis=0, concat_axis=0, tiled=True)
    total = lax.psum(jnp.sum(got.astype(f32), axis=0), "dp")
    results = []
    offset = 0
    for v in (
        project_in,
        project_out,
        router_weight,
        first_gain,
        first_bias,
        second_gain,
        second_bias,
    ):
        results.append(total[offset : offset + v.size].reshape(v.shape))
        offset += v.size
    g_in, g_out, g_router, g_gain_one, g_bias_one, g_gain_two, g_bias_two = results
    return (
        block_output,
        input_grad,
        g_gain_one,
        g_bias_one,
        g_in,
        g_out,
        g_gain_two,
        g_bias_two,
        g_router,
        expert_up_grad,
        expert_down_grad,
    )


def solution(mesh):
    in_specs = (
        P(None, ("dp", "row", "col"), None),
        P("col"),
        P("col"),
        P("col", "row"),
        P("row", "col"),
        P("col"),
        P("col"),
        P("col", "row"),
        P(None, "col", "row"),
        P(None, "col", "row"),
        P(None, "dp", None),
        P(None, ("dp", "row", "col"), None),
    )
    out_specs = (
        P(None, ("dp", "row", "col"), None),
        P(None, ("dp", "row", "col"), None),
        P("col"),
        P("col"),
        P("col", "row"),
        P("row", "col"),
        P("col"),
        P("col"),
        P("col", "row"),
        P("dp", "col", "row"),
        P("dp", "col", "row"),
    )
    return jax.shard_map(
        on_device, mesh=mesh, in_specs=in_specs, out_specs=out_specs, check_vma=False
    )
```

```python
import functools

import jax
import jax.numpy as jnp
from jax import lax
from jax.experimental import pallas as pl
from jax.experimental.pallas import tpu as pltpu
from jax.sharding import PartitionSpec as P

D = 384
HEADS = 6
HEAD = 64
TOP = 2
SEQ = 197
ROWS = 208
SLOTS = 256
SIDE = 4
SHARES = SIDE * SIDE
OWN = 2
PART = D // SIDE
WIDE = 3 * D
FPART = 384
PACK = PART + 16

sqrt_half = 0.7071067811865476
inv_root_tau = 0.3989422804014327
bf16 = jnp.bfloat16
f32 = jnp.float32
MESH = pl.DeviceIdType.MESH
ANY = pl.BlockSpec(memory_space=pl.ANY)
VMEM = pl.BlockSpec(memory_space=pltpu.VMEM)
DMA = pltpu.SemaphoreType.DMA


def dot(left, right, dims):
    return lax.dot_general(left, right, (dims, ((), ())), preferred_element_type=f32)


def position():
    row = lax.axis_index("row")
    col = lax.axis_index("col")
    across = lax.rem(row + 2, SIDE)
    beside = row + 1 - 2 * lax.rem(row, 2)
    return (row, col, across, beside)


def remote(src, dst, send, recv, **target):
    return pltpu.make_async_remote_copy(
        src_ref=src,
        dst_ref=dst,
        send_sem=send,
        recv_sem=recv,
        device_id=target,
        device_id_type=MESH,
    )


def greet(partner):
    row, col, _, _ = position()
    rank = row * SIDE + col
    barrier = pltpu.get_barrier_semaphore()

    @pl.loop(1, SHARES)
    def _(step):
        other = lax.rem(rank + step, SHARES)
        pl.semaphore_signal(
            barrier,
            inc=1,
            device_id={"row": other // SIDE, "col": lax.rem(other, SIDE)},
            device_id_type=MESH,
        )

    if partner is not None:
        pl.semaphore_signal(barrier, inc=1, device_id={"dp": partner}, device_id_type=MESH)
    pl.semaphore_wait(barrier, SHARES if partner is not None else SHARES - 1)


class Spread:
    UP, DOWN, LINE, ACROSS, CROSSED, BESIDE, PASSED, KEEP = 0, 4, 8, 12, 16, 20, 28, 36
    COUNT = 37

    def __init__(self, source, slot, sems):
        self.source, self.slot, self.sems = source, slot, sems
        self.row, self.col, self.across, self.beside = position()
        self.corner = lax.rem(self.beside + 2, SIDE)

    def hop(self, block, send, recv, src=None, **target):
        src = block if src is None else src
        return remote(src, block, self.sems.at[send], self.sems.at[recv], **target)

    def line(self, row, at, toward, src=None):
        base = self.UP if toward > 0 else self.DOWN
        return self.hop(
            self.slot(row, at), base + at, self.LINE + at, src, row=self.row, col=self.col + toward
        )

    def over(self, at, src=None):
        return self.hop(
            self.slot(self.row, at),
            self.ACROSS + at,
            self.CROSSED + at,
            src,
            row=self.across,
            col=self.col,
        )

    def side(self, row, at, shift, src=None):
        return self.hop(
            self.slot(row, at),
            self.BESIDE + shift + at,
            self.PASSED + shift + at,
            src,
            row=self.beside,
            col=self.col,
        )

    def keep(self):
        return pltpu.make_async_copy(
            self.source, self.slot(self.row, self.col), self.sems.at[self.KEEP]
        )

    def start(self):
        @pl.when(self.col < SIDE - 1)
        def _():
            self.line(self.row, self.col, 1, self.source).start()

        @pl.when(self.col > 0)
        def _():
            self.line(self.row, self.col, -1, self.source).start()

        self.over(self.col, self.source).start()
        self.side(self.row, self.col, 0, self.source).start()
        self.keep().start()

    def each(self, distance, body):
        for sign in (-1, 1):
            at = self.col + sign * distance

            @pl.when((at >= 0) & (at < SIDE))
            def _(at=at, sign=sign):
                body(at, sign)

    def relay(self, distance):
        def body(at, sign):
            self.line(self.row, at, sign).wait_recv()
            onward = self.col - sign

            @pl.when((onward >= 0) & (onward < SIDE))
            def _():
                self.line(self.row, at, -sign).start()

            self.over(at).start()
            self.side(self.row, at, 0).start()

        self.each(distance, body)

    def cross(self, distance):
        def body(at, sign):
            block = self.slot(self.across, at)
            self.hop(
                block, self.ACROSS + at, self.CROSSED + at, row=self.across, col=self.col
            ).wait_recv()
            self.side(self.across, at, SIDE).start()

        if distance == 0:
            body(self.col, 0)
        else:
            self.each(distance, body)

    def finish(self):
        for at in range(SIDE):
            self.side(self.beside, at, 0).wait_recv()
            self.side(self.corner, at, SIDE).wait_recv()
        for at in range(SIDE):

            @pl.when((at <= self.col) & (self.col < SIDE - 1))
            def _(at=at):
                self.line(self.row, at, 1).wait_send()

            @pl.when((at >= self.col) & (self.col > 0))
            def _(at=at):
                self.line(self.row, at, -1).wait_send()

            self.over(at).wait_send()
            self.side(self.row, at, 0).wait_send()
            self.side(self.across, at, SIDE).wait_send()
        self.keep().wait()


def normalize(stream):
    mean_val = jnp.mean(stream, axis=-1, keepdims=True)
    spread = jnp.mean(stream * stream, axis=-1, keepdims=True) - mean_val * mean_val
    inverse = lax.rsqrt(spread + 1e-06)
    return ((stream - mean_val) * inverse, inverse)


def half_lanes(width):
    return lax.broadcasted_iota(jnp.int32, (ROWS, width), 1) < HEAD


def one_half(pair, low, which):
    keep = low if which == 0 else jnp.logical_not(low)
    return jnp.where(keep, pair.astype(f32), 0.0).astype(bf16)


def softmax_rows(queries, keys):
    scores = dot(queries, keys, ((1,), (1,))) * HEAD ** (-0.5)
    place = lax.broadcasted_iota(jnp.int32, scores.shape, 1)
    scores = jnp.where(place < SEQ, scores, -1e30)
    top = jnp.max(scores, axis=-1, keepdims=True)
    grown = jnp.exp(scores - top)
    return grown / jnp.sum(grown, axis=-1, keepdims=True)


def attend_kernel(
    paired,
    x_ref,
    dy_ref,
    pack_ref,
    eup_ref,
    edown_ref,
    x_all,
    dy_all,
    up_ref,
    down_ref,
    w_in,
    w_out,
    w_route,
    vecs,
    normed_one,
    triple,
    mixed,
    hidden,
    normed_two,
    packs,
    spread_sems,
    fetch_send,
    fetch_recv,
    pass_send,
    pass_recv,
    keep_sems,
):
    row, col, _, _ = position()
    rank = row * SIDE + col
    half = lax.axis_index("dp") if paired else None
    partner = 1 - half if paired else None
    greet(partner)

    pack = Spread(pack_ref, lambda r, c: packs.at[r * SIDE + c], spread_sems.at[0])
    cots = Spread(dy_ref, lambda r, c: dy_all.at[:, r * SIDE + c], spread_sems.at[1])
    pack.start()
    cots.start()
    for distance in range(1, SIDE):
        pack.relay(distance)
    for distance in range(SIDE):
        pack.cross(distance)
    pack.finish()

    for r in range(SIDE):
        for c in range(SIDE):
            at = r * SIDE + c
            w_in[c * PART : (c + 1) * PART, r * 288 : (r + 1) * 288] = packs[at, :PART, :288]
            w_out[r * PART : (r + 1) * PART, c * PART : (c + 1) * PART] = packs[at, :PART, 288:]
            tail = packs[at, PART:, :PART].astype(f32)
            w_route[r * 8 : (r + 1) * 8, c * PART : (c + 1) * PART] = tail[:8]
            if r == 0:
                vecs[:, c * PART : (c + 1) * PART] = tail[8:]

    low = half_lanes(2 * HEAD)

    def image(m):
        stream = x_ref[m].astype(f32)
        normal, _ = normalize(stream)
        first = (normal * vecs[0:1] + vecs[1:2]).astype(bf16)
        normed_one[m] = first
        triple[m] = dot(first, w_in[...], ((1,), (0,))).astype(bf16)
        for pair in range(HEADS // 2):
            lanes = 2 * HEAD * pair
            queries = triple[m, :, lanes : lanes + 128]
            keys = triple[m, :, D + lanes : D + lanes + 128]
            values = triple[m, :, 2 * D + lanes : 2 * D + lanes + 128]
            parts = []
            for which in range(2):
                prob = softmax_rows(queries, one_half(keys, low, which)).astype(bf16)
                parts.append(dot(prob, values, ((1,), (0,))))
            mixed[m, :, lanes : lanes + 128] = jnp.where(low, parts[0], parts[1]).astype(bf16)
        after = stream + dot(mixed[m], w_out[...], ((1,), (0,)))
        hidden[m] = after
        normal, _ = normalize(after)
        normed_two[m] = (normal * vecs[2:3] + vecs[3:4]).astype(bf16)

    tokens = [
        Spread(
            normed_two.at[m],
            lambda r, c, m=m: x_all.at[m, r * SIDE + c],
            spread_sems.at[2 + m],
        )
        for m in range(2)
    ]
    image(0)
    tokens[0].start()
    for distance in range(1, SIDE):
        cots.relay(distance)
    image(1)
    tokens[1].start()

    mats = ((eup_ref, up_ref), (edown_ref, down_ref))
    shares = (half,) if paired else (0, 1)

    def into(whole, own, owner):
        return whole.at[own, owner // SIDE, pl.ds(lax.rem(owner, SIDE) * PART, PART), :]

    def fetch(number, mat, own, step):
        blocks, whole = mats[mat]
        to = lax.rem(rank + step, SHARES)
        return remote(
            blocks.at[own * SHARES + to],
            into(whole, own, rank),
            fetch_send.at[number, mat, step],
            fetch_recv.at[number, mat, step],
            row=to // SIDE,
            col=lax.rem(to, SIDE),
        )

    def arrival(number, mat, own, step):
        whole = mats[mat][1]
        source = lax.rem(rank + SHARES - step, SHARES)
        block = into(whole, own, source)
        return remote(
            block,
            block,
            fetch_send.at[number, mat, step],
            fetch_recv.at[number, mat, step],
            row=source // SIDE,
            col=lax.rem(source, SIDE),
        )

    def hand(mat, step):
        blocks, whole = mats[mat]
        source = lax.rem(rank + SHARES - step, SHARES)
        block = into(whole, half, source)
        src = blocks.at[half * SHARES + rank] if isinstance(step, int) else block
        return remote(src, block, pass_send.at[mat, step], pass_recv.at[mat, step], dp=partner)

    def keep(number, mat, own):
        blocks, whole = mats[mat]
        return pltpu.make_async_copy(
            blocks.at[own * SHARES + rank], into(whole, own, rank), keep_sems.at[number, mat]
        )

    for number, own in enumerate(shares):
        for mat in range(2):
            keep(number, mat, own).start()
            if paired:
                hand(mat, 0).start()

        @pl.loop(1, SHARES)
        def _(step):
            for mat in range(2):
                fetch(number, mat, own, step).start()

    for distance in range(SIDE):
        cots.cross(distance)
    for distance in range(1, SIDE):
        tokens[0].relay(distance)
    for distance in range(1, SIDE):
        tokens[1].relay(distance)
    for distance in range(SIDE):
        tokens[0].cross(distance)
    for distance in range(SIDE):
        tokens[1].cross(distance)

    for number, own in enumerate(shares):

        @pl.loop(1, SHARES)
        def _(step):
            for mat in range(2):
                arrival(number, mat, own, step).wait_recv()
                if paired:
                    hand(mat, step).start()

    tokens[0].finish()
    tokens[1].finish()
    cots.finish()
    for number, own in enumerate(shares):
        for mat in range(2):
            keep(number, mat, own).wait()

        @pl.loop(1, SHARES)
        def _(step):
            for mat in range(2):
                fetch(number, mat, own, step).wait_send()

    if paired:

        @pl.loop(0, SHARES)
        def _(step):
            for mat in range(2):
                copy = hand(mat, step)
                copy.wait_send()
                copy.wait_recv()


def attend_call(paired, x_rows, dy_rows, pack, expert_up, expert_down):
    sizes = [
        ((2, SHARES, ROWS, D), bf16, ANY),
        ((2, SHARES, ROWS, D), bf16, ANY),
        ((OWN, SIDE, D, FPART), bf16, ANY),
        ((OWN, SIDE, D, FPART), bf16, ANY),
        ((D, WIDE), bf16, VMEM),
        ((D, D), bf16, VMEM),
        ((32, D), f32, VMEM),
        ((8, D), f32, VMEM),
        ((2, ROWS, D), bf16, VMEM),
        ((2, ROWS, WIDE), bf16, VMEM),
        ((2, ROWS, D), bf16, VMEM),
        ((2, ROWS, D), f32, VMEM),
        ((2, ROWS, D), bf16, VMEM),
    ]
    numbers = 1 if paired else 2
    return pl.pallas_call(
        functools.partial(attend_kernel, paired),
        out_shape=[jax.ShapeDtypeStruct(shape, kind) for shape, kind, _ in sizes],
        in_specs=[VMEM, VMEM, VMEM, ANY, ANY],
        out_specs=[space for _, _, space in sizes],
        scratch_shapes=[
            pltpu.VMEM((SHARES, PACK, D), bf16),
            DMA((4, Spread.COUNT)),
            DMA((numbers, 2, SHARES)),
            DMA((numbers, 2, SHARES)),
            DMA((2, SHARES)),
            DMA((2, SHARES)),
            DMA((numbers, 2)),
        ],
        compiler_params=pltpu.CompilerParams(
            collective_id=0, has_side_effects=True, vmem_limit_bytes=40 << 20
        ),
        name="attend",
    )(x_rows, dy_rows, pack, expert_up, expert_down)

plane = ("row", "col")


def mm(spec, left, right):
    return jnp.einsum(spec, left, right, preferred_element_type=f32)


def norm_forward(stream, gain_vec, bias_vec):
    mean_val = jnp.mean(stream, axis=-1, keepdims=True)
    spread = jnp.mean(stream * stream, axis=-1, keepdims=True) - mean_val * mean_val
    inverse = lax.rsqrt(spread + 1e-06)
    normal = (stream - mean_val) * inverse
    return (normal, inverse, (normal * gain_vec + bias_vec).astype(bf16))


def norm_backward(grad_out, normal, inverse, gain_vec):
    scaled = grad_out * gain_vec
    grad_in = inverse * (
        scaled
        - jnp.mean(scaled, axis=-1, keepdims=True)
        - normal * jnp.mean(scaled * normal, axis=-1, keepdims=True)
    )
    return (grad_in, jnp.sum(grad_out * normal, axis=(0, 1)), jnp.sum(grad_out, axis=(0, 1)))


def split_heads(triple):
    images = triple.shape[0]
    pieces = triple.reshape(images, SEQ, 3, HEADS, HEAD)
    return (pieces[:, :, 0], pieces[:, :, 1], pieces[:, :, 2])


def on_device(
    block_input,
    first_gain,
    first_bias,
    project_in,
    project_out,
    second_gain,
    second_bias,
    router_weight,
    expert_up,
    expert_down,
    routes,
    out_grad,
):
    micro = block_input.shape[0]
    row_count = lax.axis_size("row")
    col_count = lax.axis_size("col")
    shares = row_count * col_count
    experts = expert_up.shape[0]
    own = experts // shares
    rank = lax.axis_index("row") * col_count + lax.axis_index("col")
    d_part = D // col_count
    f_part = expert_up.shape[2]

    paired = lax.axis_size("dp") == 2
    pad = ((0, 0), (0, ROWS - SEQ), (0, 0))
    vec_rows = jnp.stack([first_gain, first_bias, second_gain, second_bias])
    tail = jnp.concatenate([router_weight.T, vec_rows], axis=0)
    tail = jnp.pad(tail, ((0, 16 - tail.shape[0]), (0, D - d_part)))
    pack = jnp.concatenate([jnp.concatenate([project_in, project_out], axis=1), tail], axis=0)
    (token_rows, grad_rows, up, down, w_in, w_out, w_route, vecs, normed_one, triple, mixed, hidden_one,
     normed_two) = attend_call(paired, jnp.pad(block_input, pad), jnp.pad(out_grad, pad), pack, expert_up, expert_down)
    token_rows = token_rows.reshape(micro, -1, D)
    grad_rows = grad_rows.reshape(micro, -1, D)
    up = up.transpose(0, 2, 1, 3).reshape(own, D, -1)
    down = down.transpose(0, 2, 1, 3).reshape(own, D, -1)
    w_router = w_route.T.astype(bf16)
    gain_one, gain_two = vecs[0], vecs[2]
    stream = block_input.astype(f32)
    normal_one, inverse_one = normalize(stream)
    normed_one, triple, mixed, hidden_one, normed_two = (v[:, :SEQ] for v in (normed_one, triple, mixed, hidden_one, normed_two))
    normal_two, inverse_two = normalize(hidden_one)
    queries, key_vecs, values = split_heads(triple)
    scores = mm("ishd,ithd->ihst", queries, key_vecs) * HEAD ** (-0.5)
    prob = jax.nn.softmax(scores, axis=-1)
    attn_weights = prob.astype(bf16)

    places = routes.reshape(micro, shares, SEQ, TOP)
    places = jnp.pad(places, ((0, 0), (0, 0), (0, ROWS - SEQ), (0, 0)), constant_values=-1)
    places = places.reshape(micro, shares * ROWS, TOP)
    logits = mm("itd,de->ite", token_rows, w_router)
    picked = places[..., None] == jnp.arange(experts, dtype=jnp.int32)
    pair_logits = jnp.sum(jnp.where(picked, logits[:, :, None, :], 0.0), axis=-1)
    gates = jax.nn.softmax(pair_logits, axis=-1)
    own_ids = rank + shares * jnp.arange(own, dtype=jnp.int32)
    own_mask = places[:, None, :, :] == own_ids[None, :, None, None]
    routed = jnp.any(own_mask, axis=-1)
    gate_row = jnp.sum(jnp.where(own_mask, gates[:, None], 0.0), axis=-1)
    position = jnp.cumsum(routed.astype(jnp.int32), axis=-1) - 1
    position = jnp.where(routed, position, -1)
    pick = (position[:, :, None, :] == jnp.arange(SLOTS, dtype=jnp.int32)[:, None]).astype(bf16)
    slot_gate = jnp.sum(pick.astype(f32) * gate_row[:, :, None, :], axis=-1, keepdims=True)

    slot_x = mm("iest,itd->iesd", pick, token_rows).astype(bf16)
    slot_g = mm("iest,itd->iesd", pick, grad_rows).astype(bf16)
    pre_act = mm("iesd,edf->iesf", slot_x, up)
    cdf = 0.5 * (1.0 + lax.erf(pre_act * sqrt_half))
    act = pre_act * cdf
    scaled = (slot_gate * act).astype(bf16)
    out_slots = mm("iesf,edf->iesd", scaled, down).astype(bf16)
    grad_scaled = mm("iesd,edf->iesf", slot_g, down)
    grad_gate_slot = jnp.sum(grad_scaled * act, axis=-1)
    slope = cdf + pre_act * jnp.exp(-0.5 * pre_act * pre_act) * inv_root_tau
    grad_pre = (slot_gate * grad_scaled * slope).astype(bf16)
    back_slots = mm("iesf,edf->iesd", grad_pre, up).astype(bf16)
    up_grad = mm("iesd,iesf->edf", slot_x, grad_pre)
    down_grad = mm("iesd,iesf->edf", slot_g, scaled)
    branch_part = mm("iest,iesd->itd", pick, out_slots)
    back_part = mm("iest,iesd->itd", pick, back_slots)
    gate_token = jnp.sum(pick.astype(f32) * grad_gate_slot[..., None], axis=2)
    gate_part = jnp.sum(jnp.where(own_mask, gate_token[..., None], 0.0), axis=1)

    def to_owner(part):
        pieces = part.astype(bf16).reshape(micro, shares, ROWS, -1)
        got = lax.all_to_all(pieces, plane, split_axis=1, concat_axis=1, tiled=True)
        return jnp.sum(got.astype(f32), axis=1)[:, :SEQ]

    grad_norm_two = to_owner(back_part)
    branch = to_owner(branch_part)
    grad_gate = lax.psum(gate_part, plane)
    start = rank * ROWS
    grad_gate = lax.dynamic_slice_in_dim(grad_gate, start, SEQ, axis=1)
    gate_own = lax.dynamic_slice_in_dim(gates, start, SEQ, axis=1)
    route_own = lax.dynamic_slice_in_dim(places, start, SEQ, axis=1)
    block_output = (hidden_one + branch).astype(bf16)

    grad_logit = gate_own * (grad_gate - jnp.sum(gate_own * grad_gate, axis=-1, keepdims=True))
    dense_logit = jnp.sum(
        jnp.where(
            route_own[..., None] == jnp.arange(experts, dtype=jnp.int32), grad_logit[..., None], 0.0
        ),
        axis=2,
    )
    exact = lax.Precision.HIGHEST
    router_grad = jnp.einsum("isd,ise->de", normed_two.astype(f32), dense_logit, precision=exact)
    grad_norm_two = grad_norm_two + jnp.einsum(
        "ise,de->isd", dense_logit, w_router.astype(f32), precision=exact
    )
    grad_part, gain_two_grad, bias_two_grad = norm_backward(
        grad_norm_two, normal_two, inverse_two, gain_two
    )
    grad_hidden = out_grad.astype(f32) + grad_part
    grad_attn = grad_hidden.astype(bf16)
    out_weight_grad = mm("isd,isf->df", mixed, grad_attn)
    grad_mixed = mm("isf,df->isd", grad_attn, w_out).astype(bf16)
    grad_heads = grad_mixed.reshape(micro, SEQ, HEADS, HEAD)
    grad_values = mm("ihst,ishd->ithd", attn_weights, grad_heads)
    grad_prob = mm("ishd,ithd->ihst", grad_heads, values)
    grad_scores = (prob * (grad_prob - jnp.sum(prob * grad_prob, axis=-1, keepdims=True))).astype(bf16)
    grad_queries = mm("ihst,ithd->ishd", grad_scores, key_vecs) * HEAD ** (-0.5)
    grad_keys = mm("ihst,ishd->ithd", grad_scores, queries) * HEAD ** (-0.5)
    grad_triple = jnp.stack([grad_queries, grad_keys, grad_values], axis=2).astype(bf16)
    grad_triple = grad_triple.reshape(micro, SEQ, 3 * HEADS * HEAD)
    in_weight_grad = mm("isd,isf->df", normed_one, grad_triple)
    grad_norm_one = mm("isf,df->isd", grad_triple, w_in)
    grad_part, gain_one_grad, bias_one_grad = norm_backward(
        grad_norm_one, normal_one, inverse_one, gain_one
    )
    input_grad = grad_hidden + grad_part

    def give(grad):
        parts = grad.astype(bf16).reshape(own, col_count, d_part, row_count, f_part)
        parts = parts.transpose(0, 3, 1, 2, 4).reshape(own, shares, d_part, f_part)
        got = lax.all_to_all(parts, plane, split_axis=1, concat_axis=1, tiled=True)
        got = got.reshape(experts, d_part, f_part)
        return lax.psum_scatter(got, "dp", scatter_dimension=0, tiled=True).astype(f32)

    expert_up_grad = give(up_grad)
    expert_down_grad = give(down_grad)

    def blocks(grad, row_axis):
        if row_axis is None:
            piece = grad.reshape(1, col_count, -1)
            return jnp.broadcast_to(piece, (row_count, col_count, piece.shape[2]))
        if row_axis == 1:
            piece = grad.reshape(col_count, D // col_count, row_count, -1).transpose(2, 0, 1, 3)
        else:
            piece = grad.reshape(row_count, D // row_count, col_count, -1).transpose(0, 2, 1, 3)
        return piece.reshape(row_count, col_count, -1)

    packed = jnp.concatenate(
        [
            blocks(in_weight_grad, 1),
            blocks(out_weight_grad, 0),
            blocks(router_grad, 1),
            blocks(gain_one_grad, None),
            blocks(bias_one_grad, None),
            blocks(gain_two_grad, None),
            blocks(bias_two_grad, None),
        ],
        axis=2,
    ).reshape(shares, -1)
    got = lax.all_to_all(packed.astype(bf16), plane, split_axis=0, concat_axis=0, tiled=True)
    total = lax.psum(jnp.sum(got.astype(f32), axis=0), "dp")
    results = []
    offset = 0
    for v in (
        project_in,
        project_out,
        router_weight,
        first_gain,
        first_bias,
        second_gain,
        second_bias,
    ):
        results.append(total[offset : offset + v.size].reshape(v.shape))
        offset += v.size
    g_in, g_out, g_router, g_gain_one, g_bias_one, g_gain_two, g_bias_two = results
    return (
        block_output,
        input_grad,
        g_gain_one,
        g_bias_one,
        g_in,
        g_out,
        g_gain_two,
        g_bias_two,
        g_router,
        expert_up_grad,
        expert_down_grad,
    )


def solution(mesh):
    in_specs = (
        P(None, ("dp", "row", "col"), None),
        P("col"),
        P("col"),
        P("col", "row"),
        P("row", "col"),
        P("col"),
        P("col"),
        P("col", "row"),
        P(None, "col", "row"),
        P(None, "col", "row"),
        P(None, "dp", None),
        P(None, ("dp", "row", "col"), None),
    )
    out_specs = (
        P(None, ("dp", "row", "col"), None),
        P(None, ("dp", "row", "col"), None),
        P("col"),
        P("col"),
        P("col", "row"),
        P("row", "col"),
        P("col"),
        P("col"),
        P("col", "row"),
        P("dp", "col", "row"),
        P("dp", "col", "row"),
    )
    return jax.shard_map(
        on_device, mesh=mesh, in_specs=in_specs, out_specs=out_specs, check_vma=False
    )
```

```python
import functools

import jax
import jax.numpy as jnp
from jax import lax
from jax.experimental import pallas as pl
from jax.experimental.pallas import tpu as pltpu
from jax.sharding import PartitionSpec as P

D = 384
HEADS = 6
HEAD = 64
TOP = 2
SEQ = 197
ROWS = 208
SLOTS = 256
SIDE = 4
SHARES = SIDE * SIDE
OWN = 2
PART = D // SIDE
WIDE = 3 * D
FPART = 384
PACK = PART + 16

sqrt_half = 0.7071067811865476
inv_root_tau = 0.3989422804014327
bf16 = jnp.bfloat16
f32 = jnp.float32
MESH = pl.DeviceIdType.MESH
ANY = pl.BlockSpec(memory_space=pl.ANY)
VMEM = pl.BlockSpec(memory_space=pltpu.VMEM)
DMA = pltpu.SemaphoreType.DMA


def dot(left, right, dims):
    return lax.dot_general(left, right, (dims, ((), ())), preferred_element_type=f32)


def position():
    row = lax.axis_index("row")
    col = lax.axis_index("col")
    across = lax.rem(row + 2, SIDE)
    beside = row + 1 - 2 * lax.rem(row, 2)
    return (row, col, across, beside)


def remote(src, dst, send, recv, **target):
    return pltpu.make_async_remote_copy(
        src_ref=src,
        dst_ref=dst,
        send_sem=send,
        recv_sem=recv,
        device_id=target,
        device_id_type=MESH,
    )


def greet(partner):
    row, col, _, _ = position()
    rank = row * SIDE + col
    barrier = pltpu.get_barrier_semaphore()

    @pl.loop(1, SHARES)
    def _(step):
        other = lax.rem(rank + step, SHARES)
        pl.semaphore_signal(
            barrier,
            inc=1,
            device_id={"row": other // SIDE, "col": lax.rem(other, SIDE)},
            device_id_type=MESH,
        )

    if partner is not None:
        pl.semaphore_signal(barrier, inc=1, device_id={"dp": partner}, device_id_type=MESH)
    pl.semaphore_wait(barrier, SHARES if partner is not None else SHARES - 1)


class Spread:
    UP, DOWN, LINE, ACROSS, CROSSED, BESIDE, PASSED, KEEP = 0, 4, 8, 12, 16, 20, 28, 36
    COUNT = 37

    def __init__(self, source, slot, sems):
        self.source, self.slot, self.sems = source, slot, sems
        self.row, self.col, self.across, self.beside = position()
        self.corner = lax.rem(self.beside + 2, SIDE)

    def hop(self, block, send, recv, src=None, **target):
        src = block if src is None else src
        return remote(src, block, self.sems.at[send], self.sems.at[recv], **target)

    def line(self, row, at, toward, src=None):
        base = self.UP if toward > 0 else self.DOWN
        return self.hop(
            self.slot(row, at), base + at, self.LINE + at, src, row=self.row, col=self.col + toward
        )

    def over(self, at, src=None):
        return self.hop(
            self.slot(self.row, at),
            self.ACROSS + at,
            self.CROSSED + at,
            src,
            row=self.across,
            col=self.col,
        )

    def side(self, row, at, shift, src=None):
        return self.hop(
            self.slot(row, at),
            self.BESIDE + shift + at,
            self.PASSED + shift + at,
            src,
            row=self.beside,
            col=self.col,
        )

    def keep(self):
        return pltpu.make_async_copy(
            self.source, self.slot(self.row, self.col), self.sems.at[self.KEEP]
        )

    def start(self):
        @pl.when(self.col < SIDE - 1)
        def _():
            self.line(self.row, self.col, 1, self.source).start()

        @pl.when(self.col > 0)
        def _():
            self.line(self.row, self.col, -1, self.source).start()

        self.over(self.col, self.source).start()
        self.side(self.row, self.col, 0, self.source).start()
        self.keep().start()

    def each(self, distance, body):
        for sign in (-1, 1):
            at = self.col + sign * distance

            @pl.when((at >= 0) & (at < SIDE))
            def _(at=at, sign=sign):
                body(at, sign)

    def relay(self, distance):
        def body(at, sign):
            self.line(self.row, at, sign).wait_recv()
            onward = self.col - sign

            @pl.when((onward >= 0) & (onward < SIDE))
            def _():
                self.line(self.row, at, -sign).start()

            self.over(at).start()
            self.side(self.row, at, 0).start()

        self.each(distance, body)

    def cross(self, distance):
        def body(at, sign):
            block = self.slot(self.across, at)
            self.hop(
                block, self.ACROSS + at, self.CROSSED + at, row=self.across, col=self.col
            ).wait_recv()
            self.side(self.across, at, SIDE).start()

        if distance == 0:
            body(self.col, 0)
        else:
            self.each(distance, body)

    def finish(self):
        for at in range(SIDE):
            self.side(self.beside, at, 0).wait_recv()
            self.side(self.corner, at, SIDE).wait_recv()
        for at in range(SIDE):

            @pl.when((at <= self.col) & (self.col < SIDE - 1))
            def _(at=at):
                self.line(self.row, at, 1).wait_send()

            @pl.when((at >= self.col) & (self.col > 0))
            def _(at=at):
                self.line(self.row, at, -1).wait_send()

            self.over(at).wait_send()
            self.side(self.row, at, 0).wait_send()
            self.side(self.across, at, SIDE).wait_send()
        self.keep().wait()


def normalize(stream):
    mean_val = jnp.mean(stream, axis=-1, keepdims=True)
    spread = jnp.mean(stream * stream, axis=-1, keepdims=True) - mean_val * mean_val
    inverse = lax.rsqrt(spread + 1e-06)
    return ((stream - mean_val) * inverse, inverse)


def half_lanes(width):
    return lax.broadcasted_iota(jnp.int32, (ROWS, width), 1) < HEAD


def one_half(pair, low, which):
    keep = low if which == 0 else jnp.logical_not(low)
    return jnp.where(keep, pair.astype(f32), 0.0).astype(bf16)


def softmax_rows(queries, keys):
    scores = dot(queries, keys, ((1,), (1,))) * HEAD ** (-0.5)
    place = lax.broadcasted_iota(jnp.int32, scores.shape, 1)
    scores = jnp.where(place < SEQ, scores, -1e30)
    top = jnp.max(scores, axis=-1, keepdims=True)
    grown = jnp.exp(scores - top)
    return grown / jnp.sum(grown, axis=-1, keepdims=True)


def attend_kernel(
    paired,
    x_ref,
    dy_ref,
    pack_ref,
    eup_ref,
    edown_ref,
    x_all,
    dy_all,
    up_ref,
    down_ref,
    w_in,
    w_out,
    w_route,
    vecs,
    normed_one,
    triple,
    mixed,
    hidden,
    normed_two,
    packs,
    spread_sems,
    fetch_send,
    fetch_recv,
    pass_send,
    pass_recv,
    keep_sems,
):
    row, col, _, _ = position()
    rank = row * SIDE + col
    half = lax.axis_index("dp") if paired else None
    partner = 1 - half if paired else None
    greet(partner)

    pack = Spread(pack_ref, lambda r, c: packs.at[r * SIDE + c], spread_sems.at[0])
    cots = Spread(dy_ref, lambda r, c: dy_all.at[:, r * SIDE + c], spread_sems.at[1])
    pack.start()
    cots.start()
    for distance in range(1, SIDE):
        pack.relay(distance)
    for distance in range(SIDE):
        pack.cross(distance)
    pack.finish()

    for r in range(SIDE):
        for c in range(SIDE):
            at = r * SIDE + c
            w_in[c * PART : (c + 1) * PART, r * 288 : (r + 1) * 288] = packs[at, :PART, :288]
            w_out[r * PART : (r + 1) * PART, c * PART : (c + 1) * PART] = packs[at, :PART, 288:]
            tail = packs[at, PART:, :PART].astype(f32)
            w_route[r * 8 : (r + 1) * 8, c * PART : (c + 1) * PART] = tail[:8]
            if r == 0:
                vecs[:, c * PART : (c + 1) * PART] = tail[8:]

    low = half_lanes(2 * HEAD)

    def image(m):
        stream = x_ref[m].astype(f32)
        normal, _ = normalize(stream)
        first = (normal * vecs[0:1] + vecs[1:2]).astype(bf16)
        normed_one[m] = first
        triple[m] = dot(first, w_in[...], ((1,), (0,))).astype(bf16)
        for pair in range(HEADS // 2):
            lanes = 2 * HEAD * pair
            queries = triple[m, :, lanes : lanes + 128]
            keys = triple[m, :, D + lanes : D + lanes + 128]
            values = triple[m, :, 2 * D + lanes : 2 * D + lanes + 128]
            parts = []
            for which in range(2):
                prob = softmax_rows(queries, one_half(keys, low, which)).astype(bf16)
                parts.append(dot(prob, values, ((1,), (0,))))
            mixed[m, :, lanes : lanes + 128] = jnp.where(low, parts[0], parts[1]).astype(bf16)
        after = stream + dot(mixed[m], w_out[...], ((1,), (0,)))
        hidden[m] = after
        normal, _ = normalize(after)
        normed_two[m] = (normal * vecs[2:3] + vecs[3:4]).astype(bf16)

    tokens = [
        Spread(
            normed_two.at[m],
            lambda r, c, m=m: x_all.at[m, r * SIDE + c],
            spread_sems.at[2 + m],
        )
        for m in range(2)
    ]
    image(0)
    tokens[0].start()
    for distance in range(1, SIDE):
        cots.relay(distance)
    image(1)
    tokens[1].start()

    mats = ((eup_ref, up_ref), (edown_ref, down_ref))
    shares = (half,) if paired else (0, 1)

    def into(whole, own, owner):
        return whole.at[own, owner // SIDE, pl.ds(lax.rem(owner, SIDE) * PART, PART), :]

    def fetch(number, mat, own, step):
        blocks, whole = mats[mat]
        to = lax.rem(rank + step, SHARES)
        return remote(
            blocks.at[own * SHARES + to],
            into(whole, own, rank),
            fetch_send.at[number, mat, step],
            fetch_recv.at[number, mat, step],
            row=to // SIDE,
            col=lax.rem(to, SIDE),
        )

    def arrival(number, mat, own, step):
        whole = mats[mat][1]
        source = lax.rem(rank + SHARES - step, SHARES)
        block = into(whole, own, source)
        return remote(
            block,
            block,
            fetch_send.at[number, mat, step],
            fetch_recv.at[number, mat, step],
            row=source // SIDE,
            col=lax.rem(source, SIDE),
        )

    def hand(mat, step):
        blocks, whole = mats[mat]
        source = lax.rem(rank + SHARES - step, SHARES)
        block = into(whole, half, source)
        src = blocks.at[half * SHARES + rank] if isinstance(step, int) else block
        return remote(src, block, pass_send.at[mat, step], pass_recv.at[mat, step], dp=partner)

    def keep(number, mat, own):
        blocks, whole = mats[mat]
        return pltpu.make_async_copy(
            blocks.at[own * SHARES + rank], into(whole, own, rank), keep_sems.at[number, mat]
        )

    for number, own in enumerate(shares):
        for mat in range(2):
            keep(number, mat, own).start()
            if paired:
                hand(mat, 0).start()

        @pl.loop(1, SHARES)
        def _(step):
            for mat in range(2):
                fetch(number, mat, own, step).start()

    for distance in range(SIDE):
        cots.cross(distance)
    for distance in range(1, SIDE):
        tokens[0].relay(distance)
    for distance in range(1, SIDE):
        tokens[1].relay(distance)
    for distance in range(SIDE):
        tokens[0].cross(distance)
    for distance in range(SIDE):
        tokens[1].cross(distance)

    for number, own in enumerate(shares):

        @pl.loop(1, SHARES)
        def _(step):
            for mat in range(2):
                arrival(number, mat, own, step).wait_recv()
                if paired:
                    hand(mat, step).start()

    tokens[0].finish()
    tokens[1].finish()
    cots.finish()
    for number, own in enumerate(shares):
        for mat in range(2):
            keep(number, mat, own).wait()

        @pl.loop(1, SHARES)
        def _(step):
            for mat in range(2):
                fetch(number, mat, own, step).wait_send()

    if paired:

        @pl.loop(0, SHARES)
        def _(step):
            for mat in range(2):
                copy = hand(mat, step)
                copy.wait_send()
                copy.wait_recv()


def attend_call(paired, x_rows, dy_rows, pack, expert_up, expert_down):
    sizes = [
        ((2, SHARES, ROWS, D), bf16, ANY),
        ((2, SHARES, ROWS, D), bf16, ANY),
        ((OWN, SIDE, D, FPART), bf16, ANY),
        ((OWN, SIDE, D, FPART), bf16, ANY),
        ((D, WIDE), bf16, VMEM),
        ((D, D), bf16, VMEM),
        ((32, D), f32, VMEM),
        ((8, D), f32, VMEM),
        ((2, ROWS, D), bf16, VMEM),
        ((2, ROWS, WIDE), bf16, VMEM),
        ((2, ROWS, D), bf16, VMEM),
        ((2, ROWS, D), f32, VMEM),
        ((2, ROWS, D), bf16, VMEM),
    ]
    numbers = 1 if paired else 2
    return pl.pallas_call(
        functools.partial(attend_kernel, paired),
        out_shape=[jax.ShapeDtypeStruct(shape, kind) for shape, kind, _ in sizes],
        in_specs=[VMEM, VMEM, VMEM, ANY, ANY],
        out_specs=[space for _, _, space in sizes],
        scratch_shapes=[
            pltpu.VMEM((SHARES, PACK, D), bf16),
            DMA((4, Spread.COUNT)),
            DMA((numbers, 2, SHARES)),
            DMA((numbers, 2, SHARES)),
            DMA((2, SHARES)),
            DMA((2, SHARES)),
            DMA((numbers, 2)),
        ],
        compiler_params=pltpu.CompilerParams(
            collective_id=0, has_side_effects=True, vmem_limit_bytes=40 << 20
        ),
        name="attend",
    )(x_rows, dy_rows, pack, expert_up, expert_down)


CHUNKS = SHARES * ROWS // 128
LANES = 128


def expert_kernel(
    x_ref,
    dy_ref,
    up_ref,
    down_ref,
    w_route,
    places,
    branch,
    back,
    up_grad,
    down_grad,
    gate_out,
    pick,
    logit,
    gate_rows,
    own_gate,
    spots,
    slot_gate,
    slot_x,
    slot_g,
    out_sum,
    back_sum,
    gate_sum,
):
    row, col, _, _ = position()
    rank = row * SIDE + col
    slot_place = lax.broadcasted_iota(jnp.int32, (SLOTS, LANES), 0).astype(f32)
    upper = (
        lax.broadcasted_iota(jnp.int32, (LANES, LANES), 0)
        <= lax.broadcasted_iota(jnp.int32, (LANES, LANES), 1)
    )
    upper = jnp.where(upper, 1.0, 0.0).astype(bf16)
    above = (
        lax.broadcasted_iota(jnp.int32, (32, 32), 0) > lax.broadcasted_iota(jnp.int32, (32, 32), 1)
    )
    above = jnp.where(above, 1.0, 0.0).astype(bf16)
    ones = jnp.ones((LANES, LANES), bf16)
    names = lax.broadcasted_iota(jnp.int32, (32, LANES), 0)
    router = w_route[...].astype(bf16)

    for m in range(2):
        logit[...] = dot(router, x_ref[m], ((1,), (1,)))
        for k in range(TOP):
            gate_rows[k] = jnp.zeros((32, LANES), f32)
        for i in range(CHUNKS):
            piece = logit[:, i * LANES : (i + 1) * LANES]
            for k in range(TOP):
                chosen = places[m, k, i : i + 1, :] == names
                gate_rows[k, i : i + 1, :] = jnp.sum(
                    jnp.where(chosen, piece, 0.0), axis=0, keepdims=True
                )
        first, second = gate_rows[0], gate_rows[1]
        top = jnp.maximum(first, second)
        first, second = jnp.exp(first - top), jnp.exp(second - top)
        total = first + second
        first, second = first / total, second / total

        for q in range(OWN):
            mine = rank + SHARES * q
            one, two = places[m, 0] == mine, places[m, 1] == mine
            own_gate[q] = jnp.where(one, first, jnp.where(two, second, 0.0))
            routed = jnp.where(one | two, 1.0, 0.0).astype(bf16)
            within = dot(routed, upper, ((1,), (0,)))
            per_row = dot(routed, ones, ((1,), (0,))).astype(bf16)
            before = dot(above, per_row, ((1,), (0,)))
            spots[m, q] = jnp.where(one | two, within + before - 1.0, -1.0)
        for q in range(OWN):
            slot_gate[q, m * SLOTS : (m + 1) * SLOTS, :] = jnp.zeros((SLOTS, LANES), f32)

        for i in range(CHUNKS):
            lanes = slice(i * LANES, (i + 1) * LANES)
            for q in range(OWN):
                hit = spots[m, q, i : i + 1, :] == slot_place
                pick[m, q * SLOTS : (q + 1) * SLOTS, lanes] = jnp.where(hit, 1.0, 0.0).astype(bf16)
                slot_gate[q, m * SLOTS : (m + 1) * SLOTS, :] += jnp.where(
                    hit, own_gate[q, i : i + 1, :], 0.0
                )
        for q in range(OWN):
            rows = slice(m * SLOTS, (m + 1) * SLOTS)
            slot_gate[q, rows, :] = jnp.broadcast_to(
                jnp.sum(slot_gate[q, rows, :], axis=1, keepdims=True), (SLOTS, LANES)
            )
        for source, target in ((x_ref, slot_x), (dy_ref, slot_g)):
            found = dot(pick[m], source[m], ((1,), (0,))).astype(bf16)
            for q in range(OWN):
                target[q, m * SLOTS : (m + 1) * SLOTS, :] = found[q * SLOTS : (q + 1) * SLOTS]

    for q in range(OWN):
        out_sum[...] = jnp.zeros_like(out_sum)
        back_sum[...] = jnp.zeros_like(back_sum)
        gate_sum[q] = jnp.zeros_like(slot_gate[q])
        inputs, cots = slot_x[q], slot_g[q]

        @pl.loop(0, SIDE)
        def _(f):
            up, down = up_ref[q, f], down_ref[q, f]
            pre = dot(inputs, up, ((1,), (0,)))
            grad = dot(cots, down, ((1,), (0,)))
            cdf = 0.5 * (1.0 + lax.erf(pre * sqrt_half))
            act = pre * cdf
            gate = slot_gate[q, :, :1]
            scaled = (gate * act).astype(bf16)
            gate_sum[q] += jnp.broadcast_to(
                jnp.sum(grad * act, axis=1, keepdims=True), (2 * SLOTS, LANES)
            )
            slope = cdf + pre * jnp.exp(-0.5 * pre * pre) * inv_root_tau
            grad_pre = (gate * grad * slope).astype(bf16)
            out_sum[...] += dot(scaled, down, ((1,), (1,)))
            back_sum[...] += dot(grad_pre, up, ((1,), (1,)))
            up_grad[q, f] = dot(inputs, grad_pre, ((0,), (0,))).astype(bf16)
            down_grad[q, f] = dot(cots, scaled, ((0,), (0,))).astype(bf16)

        slot_x[q] = out_sum[...].astype(bf16)
        slot_g[q] = back_sum[...].astype(bf16)

    for m in range(2):
        rows = slice(m * SLOTS, (m + 1) * SLOTS)
        for source, target in ((slot_x, branch), (slot_g, back)):
            stacked = jnp.concatenate([source[0, rows, :], source[1, rows, :]], axis=0)

            @pl.loop(0, CHUNKS // 2)
            def _(i):
                start = pl.multiple_of(i * 2 * LANES, 2 * LANES)
                target[m, pl.ds(start, 2 * LANES), :] = dot(
                    pick[m, :, pl.ds(start, 2 * LANES)], stacked, ((0,), (0,))
                ).astype(bf16)

        for k in range(TOP):
            gate_out[m, k] = jnp.zeros((32, LANES), f32)
        for i in range(CHUNKS):
            for q in range(OWN):
                hit = spots[m, q, i : i + 1, :] == slot_place
                found = jnp.sum(jnp.where(hit, gate_sum[q, rows, :], 0.0), axis=0, keepdims=True)
                for k in range(TOP):
                    here = places[m, k, i : i + 1, :] == rank + SHARES * q
                    gate_out[m, k, i : i + 1, :] += jnp.where(here, found, 0.0)


def expert_call(x_all, dy_all, up, down, w_route, places):
    tokens = SHARES * ROWS
    sizes = [
        ((2, tokens, D), bf16),
        ((2, tokens, D), bf16),
        ((OWN, SIDE, D, FPART), bf16),
        ((OWN, SIDE, D, FPART), bf16),
        ((2, TOP, 32, LANES), f32),
    ]
    return pl.pallas_call(
        expert_kernel,
        out_shape=[jax.ShapeDtypeStruct(shape, kind) for shape, kind in sizes],
        in_specs=[VMEM] * 6,
        out_specs=[VMEM] * 5,
        scratch_shapes=[
            pltpu.VMEM((2, OWN * SLOTS, tokens), bf16),
            pltpu.VMEM((32, tokens), f32),
            pltpu.VMEM((TOP, 32, LANES), f32),
            pltpu.VMEM((OWN, 32, LANES), f32),
            pltpu.VMEM((2, OWN, 32, LANES), f32),
            pltpu.VMEM((OWN, 2 * SLOTS, LANES), f32),
            pltpu.VMEM((OWN, 2 * SLOTS, D), bf16),
            pltpu.VMEM((OWN, 2 * SLOTS, D), bf16),
            pltpu.VMEM((2 * SLOTS, D), f32),
            pltpu.VMEM((2 * SLOTS, D), f32),
            pltpu.VMEM((OWN, 2 * SLOTS, LANES), f32),
        ],
        compiler_params=pltpu.CompilerParams(vmem_limit_bytes=60 << 20),
        name="experts",
    )(x_all, dy_all, up, down, w_route, places)


class Fold:
    SIDE_SEND, SIDE_RECV, OVER_SEND, OVER_RECV, LINE_SEND, LINE_RECV, LOAD = 0, 8, 16, 20, 24, 28, 36
    COUNT = 38

    def __init__(self, part, own, beside, across, line, sems):
        self.part, self.own, self.from_beside = part, own, beside
        self.from_across, self.from_line, self.sems = across, line, sems
        self.row, self.col, self.across, self.beside = position()
        self.corner = lax.rem(self.beside + 2, SIDE)

    def load(self, far):
        row = self.across if far else self.row
        return pltpu.make_async_copy(
            self.part.at[pl.ds(row * SIDE, SIDE)], self.own.at[far], self.sems.at[self.LOAD + far]
        )

    def side(self, far, at):
        row = self.corner if far else self.beside
        return remote(
            self.part.at[row * SIDE + at],
            self.from_beside.at[far, at],
            self.sems.at[self.SIDE_SEND + 4 * far + at],
            self.sems.at[self.SIDE_RECV + 4 * far + at],
            row=self.beside,
            col=self.col,
        )

    def over(self, at):
        return remote(
            self.own.at[1, at],
            self.from_across.at[at],
            self.sems.at[self.OVER_SEND + at],
            self.sems.at[self.OVER_RECV + at],
            row=self.across,
            col=self.col,
        )

    def line(self, at, toward):
        return remote(
            self.own.at[0, at],
            self.from_line.at[at] if toward > 0 else self.from_line.at[SIDE + at],
            self.sems.at[self.LINE_SEND + at],
            self.sems.at[self.LINE_RECV + at if toward > 0 else self.LINE_RECV + SIDE + at],
            row=self.row,
            col=self.col + toward,
        )

    def add(self, far, at, other):
        self.own[far, at] = (self.own[far, at].astype(f32) + other[...].astype(f32)).astype(bf16)

    def start(self):
        for far in (1, 0):
            self.load(far).start()
            for at in (3, 0, 2, 1):
                self.side(far, at).start()

    def fold_side(self):
        self.load(1).wait()
        for at in (3, 0, 2, 1):
            self.side(1, at).wait_recv()
            self.add(1, at, self.from_beside.at[1, at])
            self.over(at).start()
        self.load(0).wait()
        for at in (3, 0, 2, 1):
            self.side(0, at).wait_recv()
            self.add(0, at, self.from_beside.at[0, at])

    def fold_over(self, at):
        self.over(at).wait_recv()
        self.add(0, at, self.from_across.at[at])

    def fold_line(self, at):
        self.fold_over(at)

        @pl.when(at > self.col)
        def _():
            @pl.when(self.col > 0)
            def _():
                self.line(at, 1).wait_recv()
                self.add(0, at, self.from_line.at[at])

            self.line(at, 1).start()

        @pl.when(at < self.col)
        def _():
            @pl.when(self.col < SIDE - 1)
            def _():
                self.line(at, -1).wait_recv()
                self.add(0, at, self.from_line.at[SIDE + at])

            self.line(at, -1).start()

    def result(self):
        total = self.own[0, self.col].astype(f32)
        return total

    def land(self):
        @pl.when(self.col > 0)
        def _():
            self.line(self.col, 1).wait_recv()
            self.add(0, self.col, self.from_line.at[self.col])

        @pl.when(self.col < SIDE - 1)
        def _():
            self.line(self.col, -1).wait_recv()
            self.add(0, self.col, self.from_line.at[SIDE + self.col])

    def finish(self):
        for far in range(2):
            for at in range(SIDE):
                self.side(far, at).wait_send()
        for at in range(SIDE):
            self.over(at).wait_send()

            @pl.when(at > self.col)
            def _(at=at):
                self.line(at, 1).wait_send()

            @pl.when(at < self.col)
            def _(at=at):
                self.line(at, -1).wait_send()


ORDER = (3, 0, 2, 1)


def settle_kernel(
    paired,
    back_ref,
    branch_ref,
    gates_ref,
    up_grad,
    down_grad,
    x_ref,
    dy_ref,
    normed_one,
    triple,
    mixed,
    hidden,
    normed_two,
    w_in,
    w_out,
    w_route,
    vecs,
    routes_ref,
    block_out,
    input_grad,
    small_out,
    up_out,
    down_out,
    own,
    beside,
    across,
    line,
    gate_in,
    small_part,
    small_own,
    small_beside,
    small_across,
    small_line,
    small_pair,
    small_sum,
    weight_in,
    weight_out,
    route_sum,
    vec_sum,
    grad_hidden,
    grad_triple,
    mine,
    theirs,
    fold_sems,
    small_sems,
    gate_send,
    gate_recv,
    swap_send,
    swap_recv,
    give_send,
    give_recv,
    keep_sems,
    pair_sems,
):
    row, col, _, _ = position()
    rank = row * SIDE + col
    half = lax.axis_index("dp") if paired else None
    partner = 1 - half if paired else None
    greet(partner)

    folds = [
        Fold(
            (back_ref if n < 2 else branch_ref).at[n % 2],
            own.at[n],
            beside.at[n],
            across.at[n],
            line.at[n],
            fold_sems.at[n],
        )
        for n in range(4)
    ]
    folds[0].start()
    folds[1].start()

    def gate_copy(step):
        to = lax.rem(rank + step, SHARES)
        return remote(
            gates_ref.at[to],
            gate_in.at[rank],
            gate_send.at[step],
            gate_recv.at[step],
            row=to // SIDE,
            col=lax.rem(to, SIDE),
        )

    def gate_wait(step):
        source = lax.rem(rank + SHARES - step, SHARES)
        return remote(
            gates_ref.at[rank],
            gate_in.at[source],
            gate_send.at[step],
            gate_recv.at[step],
            row=source // SIDE,
            col=lax.rem(source, SIDE),
        )

    gate_in[rank] = gates_ref[rank]

    @pl.loop(1, SHARES)
    def _(step):
        gate_copy(step).start()

    mats = ((up_grad, up_out), (down_grad, down_out))
    shares = (half,) if paired else (0, 1)

    def block(whole, q, owner):
        return whole.at[q, owner // SIDE, pl.ds(lax.rem(owner, SIDE) * PART, PART), :]

    def swap(mat, step):
        to = lax.rem(rank + step, SHARES)
        return remote(
            block(mats[mat][0], partner, to),
            theirs.at[step, mat],
            swap_send.at[step, mat],
            swap_recv.at[step, mat],
            dp=partner,
        )

    def fetch(mat, step):
        to = lax.rem(rank + step, SHARES)
        return pltpu.make_async_copy(
            block(mats[mat][0], half, to), mine.at[step, mat], keep_sems.at[step, mat]
        )

    def give(number, mat, q, step):
        to = lax.rem(rank + step, SHARES)
        source = mine.at[step, mat] if paired else block(mats[mat][0], q, to)
        slot = rank if paired else q * SHARES + rank
        return remote(
            source,
            mats[mat][1].at[slot],
            give_send.at[number, mat, step],
            give_recv.at[number, mat, step],
            row=to // SIDE,
            col=lax.rem(to, SIDE),
        )

    def given(number, mat, q, step):
        source = lax.rem(rank + SHARES - step, SHARES)
        slot = source if paired else q * SHARES + source
        return remote(
            mats[mat][1].at[slot],
            mats[mat][1].at[slot],
            give_send.at[number, mat, step],
            give_recv.at[number, mat, step],
            row=source // SIDE,
            col=lax.rem(source, SIDE),
        )

    def retain(number, mat, q):
        source = mine.at[0, mat] if paired else block(mats[mat][0], q, rank)
        slot = rank if paired else q * SHARES + rank
        return pltpu.make_async_copy(source, mats[mat][1].at[slot], pair_sems.at[number, mat])

    if paired:

        @pl.loop(0, SHARES)
        def _(step):
            for mat in range(2):
                swap(mat, step).start()
                fetch(mat, step).start()
    else:
        for number, q in enumerate(shares):
            for mat in range(2):
                retain(number, mat, q).start()

    folds[0].fold_side()
    folds[1].fold_side()
    folds[2].start()
    folds[3].start()
    for n in range(2):
        for at in ORDER:
            folds[n].fold_line(at)

    def pass_on(low, high):
        @pl.loop(low, high)
        def _(step):
            for mat in range(2):
                if paired:
                    fetch(mat, step).wait()
                    swap(mat, step).wait_recv()
                    mine[step, mat] = (
                        mine[step, mat].astype(f32) + theirs[step, mat].astype(f32)
                    ).astype(bf16)

                    @pl.when(step > 0)
                    def _():
                        give(0, mat, half, step).start()

                    @pl.when(step == 0)
                    def _():
                        retain(0, mat, half).start()
                else:

                    @pl.when(step > 0)
                    def _():
                        for number, q in enumerate(shares):
                            give(number, mat, q, step).start()

    @pl.loop(1, SHARES)
    def _(step):
        gate_wait(step).wait_recv()

    gate_grad = jnp.sum(gate_in[...], axis=0)
    folds[2].fold_side()
    folds[3].fold_side()

    low = half_lanes(2 * HEAD)
    names = lax.broadcasted_iota(jnp.int32, (ROWS, 32), 1)
    router = w_route[...]
    weight_in[...] = jnp.zeros_like(weight_in)
    weight_out[...] = jnp.zeros_like(weight_out)
    route_sum[...] = jnp.zeros_like(route_sum)
    vec_sum[...] = jnp.zeros_like(vec_sum)
    exact = lax.Precision.HIGHEST

    def norm_back(grad_out, normal, inverse, which):
        scaled = grad_out * vecs[which : which + 1]
        vec_sum[which : which + 1] += jnp.sum(grad_out * normal, axis=0, keepdims=True)
        vec_sum[which + 1 : which + 2] += jnp.sum(grad_out, axis=0, keepdims=True)
        return inverse * (
            scaled
            - jnp.mean(scaled, axis=-1, keepdims=True)
            - normal * jnp.mean(scaled * normal, axis=-1, keepdims=True)
        )

    def image(m):
        folds[m].land()
        grad_norm = folds[m].result()
        tokens = normed_two[m].astype(f32)
        logits = dot(normed_two[m], router.astype(bf16), ((1,), (1,)))
        hits = [routes_ref[m][:, k : k + 1] == names for k in range(TOP)]
        picked = [jnp.sum(jnp.where(hit, logits, 0.0), axis=1, keepdims=True) for hit in hits]
        top = jnp.maximum(picked[0], picked[1])
        grown = [jnp.exp(v - top) for v in picked]
        total = grown[0] + grown[1]
        gates = [v / total for v in grown]
        columns = jnp.transpose(gate_grad)[:ROWS]
        grads = [columns[:, 2 * m + k : 2 * m + k + 1] for k in range(TOP)]
        mean_grad = gates[0] * grads[0] + gates[1] * grads[1]
        dense = jnp.zeros((ROWS, 32), f32)
        for k in range(TOP):
            dense = dense + jnp.where(hits[k], gates[k] * (grads[k] - mean_grad), 0.0)
        route_sum[...] += lax.dot_general(
            dense, tokens, (((0,), (0,)), ((), ())), preferred_element_type=f32, precision=exact
        )
        grad_norm = grad_norm + lax.dot_general(
            dense, router, (((1,), (0,)), ((), ())), preferred_element_type=f32, precision=exact
        )
        normal, inverse = normalize(hidden[m])
        into_hidden = dy_ref[m].astype(f32) + norm_back(grad_norm, normal, inverse, 2)
        grad_hidden[m] = into_hidden
        grad_attn = into_hidden.astype(bf16)
        weight_out[...] += dot(mixed[m], grad_attn, ((0,), (0,)))
        grad_mixed = dot(grad_attn, w_out[...], ((1,), (1,))).astype(bf16)
        for pair in range(HEADS // 2):
            lanes = 2 * HEAD * pair
            queries = triple[m, :, lanes : lanes + 128]
            keys = triple[m, :, D + lanes : D + lanes + 128]
            values = triple[m, :, 2 * D + lanes : 2 * D + lanes + 128]
            cots = grad_mixed[:, lanes : lanes + 128]
            parts = []
            for which in range(2):
                prob = softmax_rows(queries, one_half(keys, low, which))
                weights = prob.astype(bf16)
                grad_prob = dot(cots, one_half(values, low, which), ((1,), (1,)))
                grad_scores = prob * (
                    grad_prob - jnp.sum(prob * grad_prob, axis=-1, keepdims=True)
                )
                grad_scores = grad_scores.astype(bf16)
                parts.append(
                    (
                        dot(grad_scores, keys, ((1,), (0,))) * HEAD ** (-0.5),
                        dot(grad_scores, queries, ((0,), (0,))) * HEAD ** (-0.5),
                        dot(weights, cots, ((0,), (0,))),
                    )
                )
            for n in range(3):
                grad_triple[m, :, n * D + lanes : n * D + lanes + 128] = jnp.where(
                    low, parts[0][n], parts[1][n]
                ).astype(bf16)
        weight_in[...] += dot(normed_one[m], grad_triple[m], ((0,), (0,)))
        grad_norm = dot(grad_triple[m], w_in[...], ((1,), (1,)))
        normal, inverse = normalize(x_ref[m].astype(f32))
        input_grad[m] = (grad_hidden[m] + norm_back(grad_norm, normal, inverse, 0))[:SEQ]

    pass_on(0, 4)
    image(0)
    pass_on(4, 8)
    image(1)

    for r in range(SIDE):
        for c in range(SIDE):
            at = r * SIDE + c
            small_part[at, :PART, :288] = weight_in[
                c * PART : (c + 1) * PART, r * 288 : (r + 1) * 288
            ].astype(bf16)
            small_part[at, :PART, 288:] = weight_out[
                r * PART : (r + 1) * PART, c * PART : (c + 1) * PART
            ].astype(bf16)
            tail = jnp.concatenate(
                [route_sum[r * 8 : (r + 1) * 8, :], vec_sum[...]], axis=0
            )[:, c * PART : (c + 1) * PART]
            small_part[at, PART:, :PART] = tail.astype(bf16)
            small_part[at, PART:, PART:] = jnp.zeros((16, D - PART), bf16)
    small = Fold(
        small_part, small_own, small_beside, small_across, small_line, small_sems
    )
    small.start()
    small.fold_side()
    for at in ORDER:
        small.fold_line(at)
    for n in (2, 3):
        for at in ORDER:
            folds[n].fold_line(at)
    small.land()
    if paired:
        small_pair[0] = small_own[0, col]
        pair = remote(
            small_pair.at[0], small_pair.at[1], pair_sems.at[2, 0], pair_sems.at[2, 1], dp=partner
        )
        pair.start()
    pass_on(8, SHARES)
    for m in range(2):
        folds[2 + m].land()
        block_out[m] = (hidden[m] + folds[2 + m].result()).astype(bf16)[:SEQ]
    if paired:
        pair.wait_recv()
        small_out[...] = small_own[0, col].astype(f32) + small_pair[1].astype(f32)
        pair.wait_send()
    else:
        small_out[...] = small_own[0, col].astype(f32)

    for fold in folds:
        fold.finish()
    small.finish()

    @pl.loop(1, SHARES)
    def _(step):
        gate_copy(step).wait_send()

    for number, q in enumerate(shares):
        for mat in range(2):
            retain(number, mat, q).wait()

            @pl.loop(1, SHARES)
            def _(step):
                given(number, mat, q, step).wait_recv()
                give(number, mat, q, step).wait_send()

    if paired:

        @pl.loop(0, SHARES)
        def _(step):
            for mat in range(2):
                swap(mat, step).wait_send()


def settle_call(paired, *operands):
    block = (ROWS, D)
    small = (PACK, D)
    experts = SHARES if paired else OWN * SHARES
    numbers = 1 if paired else 2
    sizes = [
        ((2, SEQ, D), bf16, VMEM),
        ((2, SEQ, D), f32, VMEM),
        (small, f32, VMEM),
        ((experts, PART, FPART), bf16, ANY),
        ((experts, PART, FPART), bf16, ANY),
    ]
    swapped = (SHARES, 2, PART, FPART) if paired else (1, 2, 16, 128)
    return pl.pallas_call(
        functools.partial(settle_kernel, paired),
        out_shape=[jax.ShapeDtypeStruct(shape, kind) for shape, kind, _ in sizes],
        in_specs=[ANY, ANY, VMEM, ANY, ANY] + [VMEM] * 12,
        out_specs=[space for _, _, space in sizes],
        scratch_shapes=[
            pltpu.VMEM((4, 2, SIDE) + block, bf16),
            pltpu.VMEM((4, 2, SIDE) + block, bf16),
            pltpu.VMEM((4, SIDE) + block, bf16),
            pltpu.VMEM((4, 2 * SIDE) + block, bf16),
            pltpu.VMEM((SHARES, 8, 256), f32),
            pltpu.VMEM((SHARES,) + small, bf16),
            pltpu.VMEM((2, SIDE) + small, bf16),
            pltpu.VMEM((2, SIDE) + small, bf16),
            pltpu.VMEM((SIDE,) + small, bf16),
            pltpu.VMEM((2 * SIDE,) + small, bf16),
            pltpu.VMEM((2,) + small, bf16),
            pltpu.VMEM(small, f32),
            pltpu.VMEM((D, WIDE), f32),
            pltpu.VMEM((D, D), f32),
            pltpu.VMEM((32, D), f32),
            pltpu.VMEM((8, D), f32),
            pltpu.VMEM((2, ROWS, D), f32),
            pltpu.VMEM((2, ROWS, WIDE), bf16),
            pltpu.VMEM(swapped, bf16),
            pltpu.VMEM(swapped, bf16),
            DMA((4, Fold.COUNT)),
            DMA((Fold.COUNT,)),
            DMA((SHARES,)),
            DMA((SHARES,)),
            DMA((SHARES, 2)),
            DMA((SHARES, 2)),
            DMA((numbers, 2, SHARES)),
            DMA((numbers, 2, SHARES)),
            DMA((SHARES, 2)),
            DMA((3, 2)),
        ],
        compiler_params=pltpu.CompilerParams(
            collective_id=1, has_side_effects=True, vmem_limit_bytes=56 << 20
        ),
        name="settle",
    )(*operands)


def on_device(
    block_input,
    first_gain,
    first_bias,
    project_in,
    project_out,
    second_gain,
    second_bias,
    router_weight,
    expert_up,
    expert_down,
    routes,
    out_grad,
):
    micro = block_input.shape[0]
    paired = lax.axis_size("dp") == 2
    rank = lax.axis_index("row") * SIDE + lax.axis_index("col")
    pad = ((0, 0), (0, ROWS - SEQ), (0, 0))
    x_rows, dy_rows = jnp.pad(block_input, pad), jnp.pad(out_grad, pad)
    vec_rows = jnp.stack([first_gain, first_bias, second_gain, second_bias])
    tail = jnp.concatenate([router_weight.T, vec_rows], axis=0)
    tail = jnp.pad(tail, ((0, 16 - tail.shape[0]), (0, D - PART)))
    pack = jnp.concatenate([jnp.concatenate([project_in, project_out], axis=1), tail], axis=0)
    places = jnp.pad(
        routes.reshape(micro, SHARES, SEQ, TOP),
        ((0, 0), (0, 0), (0, ROWS - SEQ), (0, 0)),
        constant_values=-1,
    )
    own_routes = lax.dynamic_index_in_dim(places, rank, axis=1, keepdims=False)
    place_rows = jnp.pad(
        places.reshape(micro, -1, TOP).transpose(0, 2, 1).reshape(micro, TOP, CHUNKS, LANES),
        ((0, 0), (0, 0), (0, 32 - CHUNKS), (0, 0)),
        constant_values=-1,
    )

    (
        x_all,
        dy_all,
        up,
        down,
        w_in,
        w_out,
        w_route,
        vecs,
        normed_one,
        triple,
        mixed,
        hidden,
        normed_two,
    ) = attend_call(paired, x_rows, dy_rows, pack, expert_up, expert_down)
    branch, back, up_grad, down_grad, gates = expert_call(
        x_all.reshape(micro, -1, D), dy_all.reshape(micro, -1, D), up, down, w_route, place_rows
    )
    gates = gates[:, :, :CHUNKS].reshape(micro * TOP, SHARES, ROWS).transpose(1, 0, 2)
    gates = jnp.pad(gates, ((0, 0), (0, 8 - micro * TOP), (0, 256 - ROWS)))
    blocks = (micro, SHARES, ROWS, D)
    block_output, input_grad, small, up_sum, down_sum = settle_call(
        paired,
        back.reshape(blocks),
        branch.reshape(blocks),
        gates,
        up_grad,
        down_grad,
        x_rows,
        dy_rows,
        normed_one,
        triple,
        mixed,
        hidden,
        normed_two,
        w_in,
        w_out,
        w_route,
        vecs,
        own_routes,
    )
    if not paired:
        small = lax.psum(small, "dp")
        up_sum = lax.psum_scatter(up_sum, "dp", scatter_dimension=0, tiled=True)
        down_sum = lax.psum_scatter(down_sum, "dp", scatter_dimension=0, tiled=True)
    return (
        block_output,
        input_grad,
        small[PART + 8, :PART],
        small[PART + 9, :PART],
        small[:PART, :288],
        small[:PART, 288:],
        small[PART + 10, :PART],
        small[PART + 11, :PART],
        small[PART : PART + 8, :PART].T,
        up_sum.astype(f32),
        down_sum.astype(f32),
    )


def solution(mesh):
    in_specs = (
        P(None, ("dp", "row", "col"), None),
        P("col"),
        P("col"),
        P("col", "row"),
        P("row", "col"),
        P("col"),
        P("col"),
        P("col", "row"),
        P(None, "col", "row"),
        P(None, "col", "row"),
        P(None, "dp", None),
        P(None, ("dp", "row", "col"), None),
    )
    out_specs = (
        P(None, ("dp", "row", "col"), None),
        P(None, ("dp", "row", "col"), None),
        P("col"),
        P("col"),
        P("col", "row"),
        P("row", "col"),
        P("col"),
        P("col"),
        P("col", "row"),
        P("dp", "col", "row"),
        P("dp", "col", "row"),
    )
    return jax.shard_map(
        on_device, mesh=mesh, in_specs=in_specs, out_specs=out_specs, check_vma=False
    )
```

```python
import functools

import jax
import jax.numpy as jnp
from jax import lax
from jax.experimental import pallas as pl
from jax.experimental.pallas import tpu as pltpu
from jax.sharding import PartitionSpec as P

D = 384
HEADS = 6
HEAD = 64
TOP = 2
SEQ = 197
ROWS = 208
SLOTS = 256
SIDE = 4
SHARES = SIDE * SIDE
OWN = 2
PART = D // SIDE
WIDE = 3 * D
FPART = 384
PACK = PART + 16

sqrt_half = 0.7071067811865476
inv_root_tau = 0.3989422804014327
bf16 = jnp.bfloat16
f32 = jnp.float32
MESH = pl.DeviceIdType.MESH
ANY = pl.BlockSpec(memory_space=pl.ANY)
TOKENS = SHARES * ROWS
LANES = 128
CHUNKS = TOKENS // LANES
ORDER = (3, 0, 2, 1)
VMEM = pl.BlockSpec(memory_space=pltpu.VMEM)
DMA = pltpu.SemaphoreType.DMA


def dot(left, right, dims):
    return lax.dot_general(left, right, (dims, ((), ())), preferred_element_type=f32)


def position():
    row = lax.axis_index("row")
    col = lax.axis_index("col")
    across = lax.rem(row + 2, SIDE)
    beside = row + 1 - 2 * lax.rem(row, 2)
    return (row, col, across, beside)


def peer(step):
    row, col, across, beside = position()
    group, shift = step // SIDE, lax.rem(step, SIDE)
    other = jnp.where(
        group == 0,
        row,
        jnp.where(group == 1, beside, jnp.where(group == 2, across, lax.rem(beside + 2, SIDE))),
    )
    return (
        other * SIDE + lax.rem(col + shift, SIDE),
        other * SIDE + lax.rem(col + SIDE - shift, SIDE),
    )


def remote(src, dst, send, recv, **target):
    return pltpu.make_async_remote_copy(
        src_ref=src,
        dst_ref=dst,
        send_sem=send,
        recv_sem=recv,
        device_id=target,
        device_id_type=MESH,
    )


def greet(partner):
    row, col, _, _ = position()
    rank = row * SIDE + col
    barrier = pltpu.get_barrier_semaphore()

    @pl.loop(1, SHARES)
    def _(step):
        other = lax.rem(rank + step, SHARES)
        pl.semaphore_signal(
            barrier,
            inc=1,
            device_id={"row": other // SIDE, "col": lax.rem(other, SIDE)},
            device_id_type=MESH,
        )

    if partner is not None:
        pl.semaphore_signal(barrier, inc=1, device_id={"dp": partner}, device_id_type=MESH)
    pl.semaphore_wait(barrier, SHARES if partner is not None else SHARES - 1)


class Spread:
    UP, DOWN, LINE, ACROSS, CROSSED, BESIDE, PASSED, KEEP = 0, 4, 8, 12, 16, 20, 28, 36
    COUNT = 37

    def __init__(self, source, slot, sems):
        self.source, self.slot, self.sems = source, slot, sems
        self.row, self.col, self.across, self.beside = position()
        self.corner = lax.rem(self.beside + 2, SIDE)

    def hop(self, block, send, recv, src=None, **target):
        src = block if src is None else src
        return remote(src, block, self.sems.at[send], self.sems.at[recv], **target)

    def line(self, row, at, toward, src=None):
        base = self.UP if toward > 0 else self.DOWN
        return self.hop(
            self.slot(row, at), base + at, self.LINE + at, src, row=self.row, col=self.col + toward
        )

    def over(self, at, src=None):
        return self.hop(
            self.slot(self.row, at),
            self.ACROSS + at,
            self.CROSSED + at,
            src,
            row=self.across,
            col=self.col,
        )

    def side(self, row, at, shift, src=None):
        return self.hop(
            self.slot(row, at),
            self.BESIDE + shift + at,
            self.PASSED + shift + at,
            src,
            row=self.beside,
            col=self.col,
        )

    def keep(self):
        return pltpu.make_async_copy(
            self.source, self.slot(self.row, self.col), self.sems.at[self.KEEP]
        )

    def start(self):
        @pl.when(self.col < SIDE - 1)
        def _():
            self.line(self.row, self.col, 1, self.source).start()

        @pl.when(self.col > 0)
        def _():
            self.line(self.row, self.col, -1, self.source).start()

        self.over(self.col, self.source).start()
        self.side(self.row, self.col, 0, self.source).start()
        self.keep().start()

    def each(self, distance, body):
        for sign in (-1, 1):
            at = self.col + sign * distance

            @pl.when((at >= 0) & (at < SIDE))
            def _(at=at, sign=sign):
                body(at, sign)

    def relay(self, distance):
        def body(at, sign):
            self.line(self.row, at, sign).wait_recv()
            onward = self.col - sign

            @pl.when((onward >= 0) & (onward < SIDE))
            def _():
                self.line(self.row, at, -sign).start()

            self.over(at).start()
            self.side(self.row, at, 0).start()

        self.each(distance, body)

    def cross(self, distance):
        def body(at, sign):
            block = self.slot(self.across, at)
            self.hop(
                block, self.ACROSS + at, self.CROSSED + at, row=self.across, col=self.col
            ).wait_recv()
            self.side(self.across, at, SIDE).start()

        if distance == 0:
            body(self.col, 0)
        else:
            self.each(distance, body)

    def landed(self):
        for at in range(SIDE):
            self.side(self.beside, at, 0).wait_recv()
            self.side(self.corner, at, SIDE).wait_recv()
        self.keep().wait()

    def finish(self):
        for at in range(SIDE):

            @pl.when((at <= self.col) & (self.col < SIDE - 1))
            def _(at=at):
                self.line(self.row, at, 1).wait_send()

            @pl.when((at >= self.col) & (self.col > 0))
            def _(at=at):
                self.line(self.row, at, -1).wait_send()

            self.over(at).wait_send()
            self.side(self.row, at, 0).wait_send()
            self.side(self.across, at, SIDE).wait_send()


def normalize(stream):
    mean_val = jnp.mean(stream, axis=-1, keepdims=True)
    spread = jnp.mean(stream * stream, axis=-1, keepdims=True) - mean_val * mean_val
    inverse = lax.rsqrt(spread + 1e-06)
    return ((stream - mean_val) * inverse, inverse)


def half_lanes(width):
    return lax.broadcasted_iota(jnp.int32, (ROWS, width), 1) < HEAD


def one_half(pair, low, which):
    keep = low if which == 0 else jnp.logical_not(low)
    return jnp.where(keep, pair.astype(f32), 0.0).astype(bf16)


def softmax_rows(queries, keys):
    scores = dot(queries, keys, ((1,), (1,))) * HEAD ** (-0.5)
    place = lax.broadcasted_iota(jnp.int32, scores.shape, 1)
    scores = jnp.where(place < SEQ, scores, -1e30)
    top = jnp.max(scores, axis=-1, keepdims=True)
    grown = jnp.exp(scores - top)
    return grown / jnp.sum(grown, axis=-1, keepdims=True)


class Fold:
    SIDE_SEND, SIDE_RECV, OVER_SEND, OVER_RECV, LINE_SEND, LINE_RECV = 0, 8, 16, 20, 24, 28
    COUNT = 36

    def __init__(self, part, beside, across, line, sems):
        self.part, self.from_beside = part, beside
        self.from_across, self.from_line, self.sems = across, line, sems
        self.row, self.col, self.across, self.beside = position()
        self.corner = lax.rem(self.beside + 2, SIDE)

    def block(self, far, at):
        return self.part((self.across if far else self.row) * SIDE + at)

    def side(self, far, at):
        row = self.corner if far else self.beside
        return remote(
            self.part(row * SIDE + at),
            self.from_beside.at[far, at],
            self.sems.at[self.SIDE_SEND + 4 * far + at],
            self.sems.at[self.SIDE_RECV + 4 * far + at],
            row=self.beside,
            col=self.col,
        )

    def over(self, at):
        return remote(
            self.block(1, at),
            self.from_across.at[at],
            self.sems.at[self.OVER_SEND + at],
            self.sems.at[self.OVER_RECV + at],
            row=self.across,
            col=self.col,
        )

    def line(self, at, toward):
        place = at if toward > 0 else SIDE + at
        return remote(
            self.block(0, at),
            self.from_line.at[place],
            self.sems.at[self.LINE_SEND + at],
            self.sems.at[self.LINE_RECV + place],
            row=self.row,
            col=self.col + toward,
        )

    def add(self, far, at, other):
        block = self.block(far, at)
        block[...] = (block[...].astype(f32) + other[...].astype(f32)).astype(bf16)

    def start(self):
        for far in (1, 0):
            for at in ORDER:
                self.side(far, at).start()

    def fold_side(self, far):
        for at in ORDER:
            self.side(far, at).wait_recv()
            self.add(far, at, self.from_beside.at[far, at])
            if far:
                self.over(at).start()

    def fold_line(self, at):
        self.over(at).wait_recv()
        self.add(0, at, self.from_across.at[at])

        @pl.when(at > self.col)
        def _():
            @pl.when(self.col > 0)
            def _():
                self.line(at, 1).wait_recv()
                self.add(0, at, self.from_line.at[at])

            self.line(at, 1).start()

        @pl.when(at < self.col)
        def _():
            @pl.when(self.col < SIDE - 1)
            def _():
                self.line(at, -1).wait_recv()
                self.add(0, at, self.from_line.at[SIDE + at])

            self.line(at, -1).start()

    def land(self):
        @pl.when(self.col > 0)
        def _():
            self.line(self.col, 1).wait_recv()
            self.add(0, self.col, self.from_line.at[self.col])

        @pl.when(self.col < SIDE - 1)
        def _():
            self.line(self.col, -1).wait_recv()
            self.add(0, self.col, self.from_line.at[SIDE + self.col])

    def result(self):
        return self.block(0, self.col)[...]

    def finish(self):
        for far in range(2):
            for at in range(SIDE):
                self.side(far, at).wait_send()
        for at in range(SIDE):
            self.over(at).wait_send()

            @pl.when(at > self.col)
            def _(at=at):
                self.line(at, 1).wait_send()

            @pl.when(at < self.col)
            def _(at=at):
                self.line(at, -1).wait_send()


def rows_of(index):
    return pl.ds(pl.multiple_of(index * ROWS, 16), ROWS)


BLOCK_ORDER = ('p0', 'own0', 'spot0', 'pr1', 'pr2', 'pr3', 'c0', 'px0', 'px1', 'px2', 'px3', 'pick0', 'pick1', 'pf0', 'asm0', 'image0', 'a0', 'image1', 'b0', 'cr1', 'f1', 'cr2', 'f1', 'cr3', 'f1', 'cx0', 'f1', 'h1', 'ar1', 'f1', 'br1', 'h1', 'cx1', 'f1', 'h1', 'ar2', 'f1', 'h1', 'br2', 'cx2', 'y1', 'h1', 'ar3', 'y1', 'br3', 'cx3', 'y1', 'h1', 'ax0', 'y1', 'bx0', 'y1', 'j1', 'ax1', 'y1', 'j1', 'bx1', 'y1', 'j1', 'ax2', 'y1', 'j1', 'bx2', 'j1', 'ax3', 'j1', 'bx3', 'h8', 'j8', 'cf0', 'takeg0', 'takeg1', 'af0', 'gate0', 'takex0', 'bf0', 'gate1', 'takex1', 'mine0', 'sent0', 'other0', 'ex1', 'swap0', 'ex0', 'cs0', 'putg0', '0b0', 'putg1', '1b0', 'gates0', '0f0', '1f0', '0n0', '1n0', 'as0', 'bs0', 'putx0', '2b0', 'putx1', '3b0', 'clear0', '2f0', '3f0', '0l3', '0l0', '0l2', '0l1', 'g1', '1l3', '1l0', 'g1', '1l2', '1l1', 'g1', 'wait0', 'unimage0', 'unimage1', 'small0', 'sf0', 'sn0', '2n0', '3n0', 'g1', '2l3', 'g1', '2l0', 'g1', '2l2', 'g1', '2l1', 'k1', 'sl3', 'sl0', 'sl2', 'sl1', 'k1', '3l3', 'k1', '3l0', 'k1', '3l2', 'k1', '3l1', 'sums0', 'g8', 'k8', 'done0', 'done1', 'ps0')


def block_kernel(
    paired,
    x_ref,
    dy_ref,
    pack_ref,
    eup_ref,
    edown_ref,
    places,
    routes_ref,
    block_out,
    input_grad,
    small_out,
    up_out,
    down_out,
    packs,
    w_in,
    w_out,
    w_route,
    vecs,
    normed_one,
    triple,
    mixed,
    hidden,
    normed_two,
    x_all,
    dy_all,
    up_ref,
    down_ref,
    pick,
    logit,
    gate_rows,
    own_gate,
    spots,
    slot_gate,
    slot_x,
    slot_g,
    out_sum,
    back_sum,
    gate_sum,
    gate_out,
    gate_part,
    gate_in,
    beside,
    across,
    line,
    small_part,
    small_beside,
    small_across,
    small_line,
    small_pair,
    weight_in,
    weight_out,
    route_sum,
    vec_sum,
    grad_hidden,
    grad_triple,
    theirs,
    spread_sems,
    fetch_send,
    fetch_recv,
    pass_send,
    pass_recv,
    keep_sems,
    fold_sems,
    gate_send,
    gate_recv,
    swap_send,
    swap_recv,
    give_send,
    give_recv,
    retain_sems,
    pair_sems,
):
    row, col, _, _ = position()
    rank = row * SIDE + col
    half = lax.axis_index("dp") if paired else None
    partner = 1 - half if paired else None
    greet(partner)

    low = half_lanes(2 * HEAD)
    tokens = [
        Spread(
            normed_two.at[m],
            lambda r, c, m=m: x_all.at[m, rows_of(r * SIDE + c)],
            spread_sems.at[2 + m],
        )
        for m in range(2)
    ]
    spreads = {
        "p": Spread(pack_ref, lambda r, c: packs.at[r * SIDE + c], spread_sems.at[0]),
        "c": Spread(dy_ref, lambda r, c: dy_all.at[:, rows_of(r * SIDE + c)], spread_sems.at[1]),
        "a": tokens[0],
        "b": tokens[1],
    }

    def assemble():
        for r in range(SIDE):
            for c in range(SIDE):
                at = r * SIDE + c
                w_in[c * PART : (c + 1) * PART, r * 288 : (r + 1) * 288] = packs[at, :PART, :288]
                w_out[r * PART : (r + 1) * PART, c * PART : (c + 1) * PART] = packs[at, :PART, 288:]
                tail = packs[at, PART:, :PART].astype(f32)
                w_route[r * 8 : (r + 1) * 8, c * PART : (c + 1) * PART] = tail[:8]
                if r == 0:
                    vecs[:, c * PART : (c + 1) * PART] = tail[8:]

    def attend(m):
        stream = x_ref[m].astype(f32)
        normal, _ = normalize(stream)
        first = (normal * vecs[0:1] + vecs[1:2]).astype(bf16)
        normed_one[m] = first
        triple[m] = dot(first, w_in[...], ((1,), (0,))).astype(bf16)
        for pair in range(HEADS // 2):
            lanes = 2 * HEAD * pair
            queries = triple[m, :, lanes : lanes + 128]
            keys = triple[m, :, D + lanes : D + lanes + 128]
            values = triple[m, :, 2 * D + lanes : 2 * D + lanes + 128]
            parts = []
            for which in range(2):
                prob = softmax_rows(queries, one_half(keys, low, which)).astype(bf16)
                parts.append(dot(prob, values, ((1,), (0,))))
            mixed[m, :, lanes : lanes + 128] = jnp.where(low, parts[0], parts[1]).astype(bf16)
        after = stream + dot(mixed[m], w_out[...], ((1,), (0,)))
        hidden[m] = after
        normal, _ = normalize(after)
        normed_two[m] = (normal * vecs[2:3] + vecs[3:4]).astype(bf16)

    mats = ((eup_ref, up_ref), (edown_ref, down_ref))
    shares = (half,) if paired else (0, 1)

    def into(whole, own, owner):
        return whole.at[own, owner // SIDE, pl.ds(lax.rem(owner, SIDE) * PART, PART), :]

    def fetch(number, mat, own, step):
        blocks, whole = mats[mat]
        to, _ = peer(step)
        return remote(
            blocks.at[own * SHARES + to],
            into(whole, own, rank),
            fetch_send.at[number, mat, step],
            fetch_recv.at[number, mat, step],
            row=to // SIDE,
            col=lax.rem(to, SIDE),
        )

    def arrival(number, mat, own, step):
        _, source = peer(step)
        block = into(mats[mat][1], own, source)
        return remote(
            block,
            block,
            fetch_send.at[number, mat, step],
            fetch_recv.at[number, mat, step],
            row=source // SIDE,
            col=lax.rem(source, SIDE),
        )

    def hand(mat, step):
        blocks, whole = mats[mat]
        _, source = peer(step)
        block = into(whole, half, source)
        src = blocks.at[half * SHARES + rank] if isinstance(step, int) else block
        return remote(src, block, pass_send.at[mat, step], pass_recv.at[mat, step], dp=partner)

    def keep(number, mat, own):
        blocks, whole = mats[mat]
        return pltpu.make_async_copy(
            blocks.at[own * SHARES + rank], into(whole, own, rank), keep_sems.at[number, mat]
        )

    def begin_fetch():
        for number, own in enumerate(shares):
            for mat in range(2):
                keep(number, mat, own).start()
                if paired:
                    hand(mat, 0).start()

    def fetch_some(first, last):
        for number, own in enumerate(shares):

            @pl.loop(first, last)
            def _(step):
                for mat in range(2):
                    fetch(number, mat, own, step).start()

    def pass_some(first, last):
        for number, own in enumerate(shares):

            @pl.loop(first, last)
            def _(step):
                for mat in range(2):
                    arrival(number, mat, own, step).wait_recv()
                    if paired:
                        hand(mat, step).start()

    def have_own():
        for number, own in enumerate(shares):
            for mat in range(2):
                keep(number, mat, own).wait()

    def have_other():
        if paired:

            @pl.loop(0, SHARES)
            def _(step):
                for mat in range(2):
                    hand(mat, step).wait_recv()

    def fetch_sent():
        for number, own in enumerate(shares):

            @pl.loop(1, SHARES)
            def _(step):
                for mat in range(2):
                    fetch(number, mat, own, step).wait_send()

        if paired:

            @pl.loop(0, SHARES)
            def _(step):
                for mat in range(2):
                    hand(mat, step).wait_send()

    slot_place = lax.broadcasted_iota(jnp.int32, (SLOTS, LANES), 0).astype(f32)
    names = lax.broadcasted_iota(jnp.int32, (32, LANES), 0)

    def own_routes(m, q):
        mine = rank + SHARES * q
        return (places[m, 0] == mine, places[m, 1] == mine)

    def find_spots():
        down_lane = lax.broadcasted_iota(jnp.int32, (LANES, LANES), 0)
        lane = lax.broadcasted_iota(jnp.int32, (LANES, LANES), 1)
        upper = jnp.where(down_lane <= lane, 1.0, 0.0).astype(bf16)
        below = lax.broadcasted_iota(jnp.int32, (32, 32), 0)
        above = lax.broadcasted_iota(jnp.int32, (32, 32), 1)
        earlier = jnp.where(below > above, 1.0, 0.0).astype(bf16)
        ones = jnp.ones((LANES, LANES), bf16)
        for m in range(2):
            for q in range(OWN):
                one, two = own_routes(m, q)
                routed = jnp.where(one | two, 1.0, 0.0).astype(bf16)
                within = dot(routed, upper, ((1,), (0,)))
                per_row = dot(routed, ones, ((1,), (0,))).astype(bf16)
                before = dot(earlier, per_row, ((1,), (0,)))
                spots[m, q] = jnp.where(one | two, within + before - 1.0, -1.0)

    def make_pick(m):
        @pl.loop(0, CHUNKS)
        def _(i):
            lanes = pl.ds(pl.multiple_of(i * LANES, LANES), LANES)
            for q in range(OWN):
                hit = spots[m, q, pl.ds(i, 1), :] == slot_place
                pick[m, q * SLOTS : (q + 1) * SLOTS, lanes] = jnp.where(hit, 1.0, 0.0).astype(bf16)

    def take(source, target, m):
        found = dot(pick[m], source[m], ((1,), (0,))).astype(bf16)
        for q in range(OWN):
            target[q, m * SLOTS : (m + 1) * SLOTS, :] = found[q * SLOTS : (q + 1) * SLOTS]

    def make_gates(m):
        logit[...] = dot(w_route[...].astype(bf16), x_all[m], ((1,), (1,)))
        for k in range(TOP):
            gate_rows[k] = jnp.zeros((32, LANES), f32)

        @pl.loop(0, CHUNKS)
        def _(i):
            piece = logit[:, pl.ds(pl.multiple_of(i * LANES, LANES), LANES)]
            for k in range(TOP):
                chosen = places[m, k, pl.ds(i, 1), :] == names
                gate_rows[k, pl.ds(i, 1), :] = jnp.sum(
                    jnp.where(chosen, piece, 0.0), axis=0, keepdims=True
                )

        first, second = gate_rows[0], gate_rows[1]
        top = jnp.maximum(first, second)
        first, second = jnp.exp(first - top), jnp.exp(second - top)
        total = first + second
        first, second = first / total, second / total
        rows = slice(m * SLOTS, (m + 1) * SLOTS)
        for q in range(OWN):
            one, two = own_routes(m, q)
            own_gate[q] = jnp.where(one, first, jnp.where(two, second, 0.0))
            slot_gate[q, rows, :] = jnp.zeros((SLOTS, LANES), f32)

        @pl.loop(0, CHUNKS)
        def _(i):
            for q in range(OWN):
                hit = spots[m, q, pl.ds(i, 1), :] == slot_place
                slot_gate[q, rows, :] += jnp.where(hit, own_gate[q, pl.ds(i, 1), :], 0.0)

        for q in range(OWN):
            slot_gate[q, rows, :] = jnp.broadcast_to(
                jnp.sum(slot_gate[q, rows, :], axis=1, keepdims=True), (SLOTS, LANES)
            )

    def expert(q):
        out_sum[...] = jnp.zeros_like(out_sum)
        back_sum[...] = jnp.zeros_like(back_sum)
        gate_sum[q] = jnp.zeros((2 * SLOTS, LANES), f32)

        @pl.loop(0, SIDE)
        def _(f):
            inputs, cots = slot_x[q], slot_g[q]
            up, down = up_ref[q, f], down_ref[q, f]
            pre = dot(inputs, up, ((1,), (0,)))
            grad = dot(cots, down, ((1,), (0,)))
            cdf = 0.5 * (1.0 + lax.erf(pre * sqrt_half))
            act = pre * cdf
            gate = slot_gate[q][:, :1]
            scaled = (gate * act).astype(bf16)
            gate_sum[q] += jnp.broadcast_to(
                jnp.sum(grad * act, axis=1, keepdims=True), (2 * SLOTS, LANES)
            )
            slope = cdf + pre * jnp.exp(-0.5 * pre * pre) * inv_root_tau
            grad_pre = (gate * grad * slope).astype(bf16)
            out_sum[...] += dot(scaled, down, ((1,), (1,)))
            back_sum[...] += dot(grad_pre, up, ((1,), (1,)))
            up_ref[q, f] = dot(inputs, grad_pre, ((0,), (0,))).astype(bf16)
            down_ref[q, f] = dot(cots, scaled, ((0,), (0,))).astype(bf16)

        slot_x[q] = out_sum[...].astype(bf16)
        slot_g[q] = back_sum[...].astype(bf16)

    def put(source, target, m):
        rows = slice(m * SLOTS, (m + 1) * SLOTS)
        stacked = jnp.concatenate([source[0, rows, :], source[1, rows, :]], axis=0)

        @pl.loop(0, CHUNKS // 2)
        def _(i):
            there = pl.ds(pl.multiple_of(i * 2 * LANES, 2 * LANES), 2 * LANES)
            target[m, there, :] = dot(pick[m, :, there], stacked, ((0,), (0,))).astype(bf16)

    def gate_back():
        gate_part[...] = jnp.zeros_like(gate_part)
        for m in range(2):
            rows = slice(m * SLOTS, (m + 1) * SLOTS)
            for k in range(TOP):
                gate_out[m, k] = jnp.zeros((32, LANES), f32)

            @pl.loop(0, CHUNKS)
            def _(i):
                for q in range(OWN):
                    hit = spots[m, q, pl.ds(i, 1), :] == slot_place
                    found = jnp.sum(
                        jnp.where(hit, gate_sum[q, rows, :], 0.0), axis=0, keepdims=True
                    )
                    for k in range(TOP):
                        here = places[m, k, pl.ds(i, 1), :] == rank + SHARES * q
                        gate_out[m, k, pl.ds(i, 1), :] += jnp.where(here, found, 0.0)

            for to in range(SHARES):
                first = to * ROWS // LANES
                shift = to * ROWS - first * LANES
                span = -(-(shift + ROWS) // LANES)
                for k in range(TOP):
                    wide = jnp.concatenate(
                        [gate_out[m, k, first + n : first + n + 1, :] for n in range(span)], axis=1
                    )
                    gate_part[to, 2 * m + k : 2 * m + k + 1, :ROWS] = wide[:, shift : shift + ROWS]

    def gate_copy(step):
        to, _ = peer(step)
        return remote(
            gate_part.at[to],
            gate_in.at[rank],
            gate_send.at[step],
            gate_recv.at[step],
            row=to // SIDE,
            col=lax.rem(to, SIDE),
        )

    def gate_wait(step):
        _, source = peer(step)
        return remote(
            gate_part.at[rank],
            gate_in.at[source],
            gate_send.at[step],
            gate_recv.at[step],
            row=source // SIDE,
            col=lax.rem(source, SIDE),
        )

    def start_gates():
        gate_back()
        gate_in[rank] = gate_part[rank]

        @pl.loop(1, SHARES)
        def _(step):
            gate_copy(step).start()

    def wait_gates():
        @pl.loop(1, SHARES)
        def _(step):
            gate_wait(step).wait_recv()

    folds = [
        Fold(
            lambda index, n=n: (dy_all if n < 2 else x_all).at[n % 2, rows_of(index)],
            beside.at[n],
            across.at[n],
            line.at[n],
            fold_sems.at[n],
        )
        for n in range(4)
    ]
    small = Fold(
        lambda index: small_part.at[index], small_beside, small_across, small_line, fold_sems.at[4]
    )

    givers = ((up_ref, up_out), (down_ref, down_out))

    def swap(mat, step):
        to, _ = peer(step)
        return remote(
            into(givers[mat][0], partner, to),
            theirs.at[step, mat],
            swap_send.at[step, mat],
            swap_recv.at[step, mat],
            dp=partner,
        )

    def give(number, mat, q, step):
        to, _ = peer(step)
        return remote(
            into(givers[mat][0], q, to),
            givers[mat][1].at[rank if paired else q * SHARES + rank],
            give_send.at[number, mat, step],
            give_recv.at[number, mat, step],
            row=to // SIDE,
            col=lax.rem(to, SIDE),
        )

    def given(number, mat, q, step):
        _, source = peer(step)
        block = givers[mat][1].at[source if paired else q * SHARES + source]
        return remote(
            block,
            block,
            give_send.at[number, mat, step],
            give_recv.at[number, mat, step],
            row=source // SIDE,
            col=lax.rem(source, SIDE),
        )

    def retain(number, mat, q):
        return pltpu.make_async_copy(
            into(givers[mat][0], q, rank),
            givers[mat][1].at[rank if paired else q * SHARES + rank],
            retain_sems.at[number, mat],
        )

    def start_swap():
        if paired:

            @pl.loop(0, SHARES)
            def _(step):
                for mat in range(2):
                    swap(mat, step).start()

    def give_some(first, last):
        for number, q in enumerate(shares):

            @pl.loop(first, last)
            def _(step):
                for mat in range(2):
                    if paired:
                        swap(mat, step).wait_recv()
                        to, _ = peer(step)
                        block = into(givers[mat][0], half, to)
                        block[...] = (
                            block[...].astype(f32) + theirs[step, mat].astype(f32)
                        ).astype(bf16)

                    @pl.when(step > 0)
                    def _():
                        give(number, mat, q, step).start()

                    @pl.when(step == 0)
                    def _():
                        retain(number, mat, q).start()

    token_names = lax.broadcasted_iota(jnp.int32, (ROWS, 32), 1)
    exact = lax.Precision.HIGHEST

    def clear_sums():
        weight_in[...] = jnp.zeros_like(weight_in)
        weight_out[...] = jnp.zeros_like(weight_out)
        route_sum[...] = jnp.zeros_like(route_sum)
        vec_sum[...] = jnp.zeros_like(vec_sum)

    def norm_back(grad_out, normal, inverse, which):
        scaled = grad_out * vecs[which : which + 1]
        vec_sum[which : which + 1] += jnp.sum(grad_out * normal, axis=0, keepdims=True)
        vec_sum[which + 1 : which + 2] += jnp.sum(grad_out, axis=0, keepdims=True)
        return inverse * (
            scaled
            - jnp.mean(scaled, axis=-1, keepdims=True)
            - normal * jnp.mean(scaled * normal, axis=-1, keepdims=True)
        )

    def attend_back(m):
        folds[m].land()
        grad_norm = folds[m].result().astype(f32)
        router = w_route[...]
        logits = dot(normed_two[m], router.astype(bf16), ((1,), (1,)))
        hits = [routes_ref[m][:, k : k + 1] == token_names for k in range(TOP)]
        picked = [jnp.sum(jnp.where(hit, logits, 0.0), axis=1, keepdims=True) for hit in hits]
        top = jnp.maximum(picked[0], picked[1])
        grown = [jnp.exp(v - top) for v in picked]
        total = grown[0] + grown[1]
        gates = [v / total for v in grown]
        columns = jnp.transpose(jnp.sum(gate_in[...], axis=0))[:ROWS]
        grads = [columns[:, 2 * m + k : 2 * m + k + 1] for k in range(TOP)]
        mean_grad = gates[0] * grads[0] + gates[1] * grads[1]
        dense = jnp.zeros((ROWS, 32), f32)
        for k in range(TOP):
            dense = dense + jnp.where(hits[k], gates[k] * (grads[k] - mean_grad), 0.0)
        route_sum[...] += lax.dot_general(
            dense,
            normed_two[m].astype(f32),
            (((0,), (0,)), ((), ())),
            preferred_element_type=f32,
            precision=exact,
        )
        grad_norm = grad_norm + lax.dot_general(
            dense, router, (((1,), (0,)), ((), ())), preferred_element_type=f32, precision=exact
        )
        normal, inverse = normalize(hidden[m])
        into_hidden = dy_ref[m].astype(f32) + norm_back(grad_norm, normal, inverse, 2)
        grad_hidden[m] = into_hidden
        grad_attn = into_hidden.astype(bf16)
        weight_out[...] += dot(mixed[m], grad_attn, ((0,), (0,)))
        grad_mixed = dot(grad_attn, w_out[...], ((1,), (1,))).astype(bf16)
        for pair in range(HEADS // 2):
            lanes = 2 * HEAD * pair
            queries = triple[m, :, lanes : lanes + 128]
            keys = triple[m, :, D + lanes : D + lanes + 128]
            values = triple[m, :, 2 * D + lanes : 2 * D + lanes + 128]
            cots = grad_mixed[:, lanes : lanes + 128]
            parts = []
            for which in range(2):
                prob = softmax_rows(queries, one_half(keys, low, which))
                weights = prob.astype(bf16)
                grad_prob = dot(cots, one_half(values, low, which), ((1,), (1,)))
                grad_scores = prob * (
                    grad_prob - jnp.sum(prob * grad_prob, axis=-1, keepdims=True)
                )
                grad_scores = grad_scores.astype(bf16)
                parts.append(
                    (
                        dot(grad_scores, keys, ((1,), (0,))) * HEAD ** (-0.5),
                        dot(grad_scores, queries, ((0,), (0,))) * HEAD ** (-0.5),
                        dot(weights, cots, ((0,), (0,))),
                    )
                )
            for n in range(3):
                grad_triple[m, :, n * D + lanes : n * D + lanes + 128] = jnp.where(
                    low, parts[0][n], parts[1][n]
                ).astype(bf16)
        weight_in[...] += dot(normed_one[m], grad_triple[m], ((0,), (0,)))
        grad_norm = dot(grad_triple[m], w_in[...], ((1,), (1,)))
        normal, inverse = normalize(x_ref[m].astype(f32))
        input_grad[m] = (grad_hidden[m] + norm_back(grad_norm, normal, inverse, 0))[:SEQ]

    def gather_small():
        for r in range(SIDE):
            for c in range(SIDE):
                at = r * SIDE + c
                small_part[at, :PART, :288] = weight_in[
                    c * PART : (c + 1) * PART, r * 288 : (r + 1) * 288
                ].astype(bf16)
                small_part[at, :PART, 288:] = weight_out[
                    r * PART : (r + 1) * PART, c * PART : (c + 1) * PART
                ].astype(bf16)
                tail = jnp.concatenate([route_sum[r * 8 : (r + 1) * 8, :], vec_sum[...]], axis=0)
                small_part[at, PART:, :PART] = tail[:, c * PART : (c + 1) * PART].astype(bf16)
                small_part[at, PART:, PART:] = jnp.zeros((16, D - PART), bf16)

    pair = None
    if paired:
        pair = remote(
            small_pair.at[0], small_pair.at[1], pair_sems.at[0], pair_sems.at[1], dp=partner
        )

    def end_small():
        small.land()
        if paired:
            small_pair[0] = small.result()
            pair.start()

    def finish_small():
        if paired:
            pair.wait_recv()
            small_out[...] = small.result().astype(f32) + small_pair[1].astype(f32)
            pair.wait_send()
        else:
            small_out[...] = small.result().astype(f32)

    def finish_branch(m):
        folds[2 + m].land()
        block_out[m] = (hidden[m] + folds[2 + m].result().astype(f32)).astype(bf16)[:SEQ]

    limits = {"f": SHARES // 2, "y": SHARES, "h": SHARES // 2, "j": SHARES, "g": SHARES // 2, "k": SHARES}
    at = {"f": 1, "y": SHARES // 2, "h": 1, "j": SHARES // 2, "g": 0, "k": SHARES // 2}
    ranged = {
        "f": fetch_some,
        "y": fetch_some,
        "h": pass_some,
        "j": pass_some,
        "g": give_some,
        "k": give_some,
    }
    plain = {
        "own": begin_fetch,
        "asm": assemble,
        "spot": find_spots,
        "mine": have_own,
        "other": have_other,
        "sent": fetch_sent,
        "gates": start_gates,
        "wait": wait_gates,
        "clear": clear_sums,
        "swap": start_swap,
        "sums": end_small,
    }
    numbered = {
        "image": attend,
        "pick": make_pick,
        "gate": make_gates,
        "takex": lambda m: take(x_all, slot_x, m),
        "takeg": lambda m: take(dy_all, slot_g, m),
        "putx": lambda m: put(slot_x, x_all, m),
        "putg": lambda m: put(slot_g, dy_all, m),
        "unimage": attend_back,
        "done": finish_branch,
    }
    for step in BLOCK_ORDER:
        name, number = step[:-1], int(step[-1], 16)
        if name in ranged:
            last = min(at[name] + number, limits[name])
            ranged[name](at[name], last)
            at[name] = last
        elif name in plain:
            plain[name]()
        elif name in numbered:
            numbered[name](number)
        elif name == "ex":
            expert(number if half is None else (half if number == 0 else partner))
        elif name == "small":
            gather_small()
            small.start()
        elif name[0] in spreads:
            act = spreads[name[0]]
            if name[1:] == "":
                act.start()
            elif name[1:] == "r":
                act.relay(number)
            elif name[1:] == "x":
                act.cross(number)
            elif name[1:] == "f":
                act.landed()
            elif name[1:] == "s":
                act.finish()
        else:
            fold = small if name[0] == "s" else folds[int(name[0])]
            if name[1:] == "b":
                fold.start()
            elif name[1:] == "f":
                fold.fold_side(1)
            elif name[1:] == "n":
                fold.fold_side(0)
            else:
                fold.fold_line(number)
    finish_small()

    for fold in folds:
        fold.finish()
    small.finish()

    @pl.loop(1, SHARES)
    def _(step):
        gate_copy(step).wait_send()

    for number, q in enumerate(shares):
        for mat in range(2):
            retain(number, mat, q).wait()

            @pl.loop(1, SHARES)
            def _(step):
                given(number, mat, q, step).wait_recv()
                give(number, mat, q, step).wait_send()

    if paired:

        @pl.loop(0, SHARES)
        def _(step):
            for mat in range(2):
                swap(mat, step).wait_send()


def block_call(paired, x_rows, dy_rows, pack, expert_up, expert_down, places, own_routes):
    block, small = (ROWS, D), (PACK, D)
    experts = SHARES if paired else OWN * SHARES
    numbers = 1 if paired else 2
    outputs = [
        ((2, SEQ, D), bf16, VMEM),
        ((2, SEQ, D), f32, VMEM),
        (small, f32, VMEM),
        ((experts, PART, FPART), bf16, ANY),
        ((experts, PART, FPART), bf16, ANY),
    ]
    scratch = [
        ((SHARES,) + small, bf16),
        ((D, WIDE), bf16),
        ((D, D), bf16),
        ((32, D), f32),
        ((8, D), f32),
        ((2,) + block, bf16),
        ((2, ROWS, WIDE), bf16),
        ((2,) + block, bf16),
        ((2,) + block, f32),
        ((2,) + block, bf16),
        ((2, TOKENS, D), bf16),
        ((2, TOKENS, D), bf16),
        ((OWN, SIDE, D, FPART), bf16),
        ((OWN, SIDE, D, FPART), bf16),
        ((2, OWN * SLOTS, TOKENS), bf16),
        ((32, TOKENS), f32),
        ((TOP, 32, LANES), f32),
        ((OWN, 32, LANES), f32),
        ((2, OWN, 32, LANES), f32),
        ((OWN, 2 * SLOTS, LANES), f32),
        ((OWN, 2 * SLOTS, D), bf16),
        ((OWN, 2 * SLOTS, D), bf16),
        ((2 * SLOTS, D), f32),
        ((2 * SLOTS, D), f32),
        ((OWN, 2 * SLOTS, LANES), f32),
        ((2, TOP, 32, LANES), f32),
        ((SHARES, 8, 256), f32),
        ((SHARES, 8, 256), f32),
        ((4, 2, SIDE) + block, bf16),
        ((4, SIDE) + block, bf16),
        ((4, 2 * SIDE) + block, bf16),
        ((SHARES,) + small, bf16),
        ((2, SIDE) + small, bf16),
        ((SIDE,) + small, bf16),
        ((2 * SIDE,) + small, bf16),
        ((2,) + small, bf16),
        ((D, WIDE), f32),
        ((D, D), f32),
        ((32, D), f32),
        ((8, D), f32),
        ((2,) + block, f32),
        ((2, ROWS, WIDE), bf16),
        ((SHARES, 2, PART, FPART) if paired else (1, 2, 16, LANES), bf16),
    ]
    semaphores = [
        (4, Spread.COUNT),
        (numbers, 2, SHARES),
        (numbers, 2, SHARES),
        (2, SHARES),
        (2, SHARES),
        (numbers, 2),
        (5, Fold.COUNT),
        (SHARES,),
        (SHARES,),
        (SHARES, 2),
        (SHARES, 2),
        (numbers, 2, SHARES),
        (numbers, 2, SHARES),
        (numbers, 2),
        (2,),
    ]
    return pl.pallas_call(
        functools.partial(block_kernel, paired),
        out_shape=[jax.ShapeDtypeStruct(shape, kind) for shape, kind, _ in outputs],
        in_specs=[VMEM, VMEM, VMEM, ANY, ANY, VMEM, VMEM],
        out_specs=[space for _, _, space in outputs],
        scratch_shapes=[pltpu.VMEM(shape, kind) for shape, kind in scratch]
        + [DMA(shape) for shape in semaphores],
        compiler_params=pltpu.CompilerParams(
            collective_id=0, has_side_effects=True, vmem_limit_bytes=63 << 20
        ),
        name="block",
    )(x_rows, dy_rows, pack, expert_up, expert_down, places, own_routes)


def on_device(
    block_input,
    first_gain,
    first_bias,
    project_in,
    project_out,
    second_gain,
    second_bias,
    router_weight,
    expert_up,
    expert_down,
    routes,
    out_grad,
):
    micro = block_input.shape[0]
    paired = lax.axis_size("dp") == 2
    rank = lax.axis_index("row") * SIDE + lax.axis_index("col")
    pad = ((0, 0), (0, ROWS - SEQ), (0, 0))
    x_rows, dy_rows = jnp.pad(block_input, pad), jnp.pad(out_grad, pad)
    vec_rows = jnp.stack([first_gain, first_bias, second_gain, second_bias])
    tail = jnp.concatenate([router_weight.T, vec_rows], axis=0)
    tail = jnp.pad(tail, ((0, 16 - tail.shape[0]), (0, D - PART)))
    pack = jnp.concatenate([jnp.concatenate([project_in, project_out], axis=1), tail], axis=0)
    places = jnp.pad(
        routes.reshape(micro, SHARES, SEQ, TOP),
        ((0, 0), (0, 0), (0, ROWS - SEQ), (0, 0)),
        constant_values=-1,
    )
    own_routes = lax.dynamic_index_in_dim(places, rank, axis=1, keepdims=False)
    place_rows = jnp.pad(
        places.reshape(micro, -1, TOP).transpose(0, 2, 1).reshape(micro, TOP, CHUNKS, LANES),
        ((0, 0), (0, 0), (0, 32 - CHUNKS), (0, 0)),
        constant_values=-1,
    )

    block_output, input_grad, small, up_sum, down_sum = block_call(
        paired, x_rows, dy_rows, pack, expert_up, expert_down, place_rows, own_routes
    )
    if not paired:
        small = lax.psum(small, "dp")
        up_sum = lax.psum_scatter(up_sum, "dp", scatter_dimension=0, tiled=True)
        down_sum = lax.psum_scatter(down_sum, "dp", scatter_dimension=0, tiled=True)
    return (
        block_output,
        input_grad,
        small[PART + 8, :PART],
        small[PART + 9, :PART],
        small[:PART, :288],
        small[:PART, 288:],
        small[PART + 10, :PART],
        small[PART + 11, :PART],
        small[PART : PART + 8, :PART].T,
        up_sum.astype(f32),
        down_sum.astype(f32),
    )


def solution(mesh):
    in_specs = (
        P(None, ("dp", "row", "col"), None),
        P("col"),
        P("col"),
        P("col", "row"),
        P("row", "col"),
        P("col"),
        P("col"),
        P("col", "row"),
        P(None, "col", "row"),
        P(None, "col", "row"),
        P(None, "dp", None),
        P(None, ("dp", "row", "col"), None),
    )
    out_specs = (
        P(None, ("dp", "row", "col"), None),
        P(None, ("dp", "row", "col"), None),
        P("col"),
        P("col"),
        P("col", "row"),
        P("row", "col"),
        P("col"),
        P("col"),
        P("col", "row"),
        P("dp", "col", "row"),
        P("dp", "col", "row"),
    )
    return jax.shard_map(
        on_device, mesh=mesh, in_specs=in_specs, out_specs=out_specs, check_vma=False
    )
```

```python
import functools

import jax
import jax.numpy as jnp
from jax import lax
from jax.experimental import pallas as pl
from jax.experimental.pallas import tpu as pltpu
from jax.sharding import PartitionSpec as P

D = 384
HEADS = 6
HEAD = 64
TOP = 2
SEQ = 197
ROWS = 208
SLOTS = 256
SIDE = 4
SHARES = SIDE * SIDE
OWN = 2
PART = D // SIDE
WIDE = 3 * D
FPART = 384
PACK = PART + 16

sqrt_half = 0.7071067811865476
inv_root_tau = 0.3989422804014327
bf16 = jnp.bfloat16
f32 = jnp.float32
MESH = pl.DeviceIdType.MESH
ANY = pl.BlockSpec(memory_space=pl.ANY)
TOKENS = SHARES * ROWS
LANES = 128
CHUNKS = TOKENS // LANES
ORDER = (3, 0, 2, 1)
VMEM = pl.BlockSpec(memory_space=pltpu.VMEM)
DMA = pltpu.SemaphoreType.DMA


def dot(left, right, dims):
    return lax.dot_general(left, right, (dims, ((), ())), preferred_element_type=f32)


def position():
    row = lax.axis_index("row")
    col = lax.axis_index("col")
    across = lax.rem(row + 2, SIDE)
    beside = row + 1 - 2 * lax.rem(row, 2)
    return (row, col, across, beside)


def peer(step):
    row, col, across, beside = position()
    group, shift = step // SIDE, lax.rem(step, SIDE)
    other = jnp.where(
        group == 0,
        row,
        jnp.where(group == 1, beside, jnp.where(group == 2, across, lax.rem(beside + 2, SIDE))),
    )
    return (
        other * SIDE + lax.rem(col + shift, SIDE),
        other * SIDE + lax.rem(col + SIDE - shift, SIDE),
    )


def remote(src, dst, send, recv, **target):
    return pltpu.make_async_remote_copy(
        src_ref=src,
        dst_ref=dst,
        send_sem=send,
        recv_sem=recv,
        device_id=target,
        device_id_type=MESH,
    )


def greet(partner):
    row, col, _, _ = position()
    rank = row * SIDE + col
    barrier = pltpu.get_barrier_semaphore()

    @pl.loop(1, SHARES)
    def _(step):
        other = lax.rem(rank + step, SHARES)
        pl.semaphore_signal(
            barrier,
            inc=1,
            device_id={"row": other // SIDE, "col": lax.rem(other, SIDE)},
            device_id_type=MESH,
        )

    if partner is not None:
        pl.semaphore_signal(barrier, inc=1, device_id={"dp": partner}, device_id_type=MESH)
    pl.semaphore_wait(barrier, SHARES if partner is not None else SHARES - 1)


class Spread:
    UP, DOWN, LINE, ACROSS, CROSSED, BESIDE, PASSED, KEEP = 0, 4, 8, 12, 16, 20, 28, 36
    COUNT = 37

    def __init__(self, source, slot, sems):
        self.source, self.slot, self.sems = source, slot, sems
        self.row, self.col, self.across, self.beside = position()
        self.corner = lax.rem(self.beside + 2, SIDE)

    def hop(self, block, send, recv, src=None, **target):
        src = block if src is None else src
        return remote(src, block, self.sems.at[send], self.sems.at[recv], **target)

    def line(self, row, at, toward, src=None):
        base = self.UP if toward > 0 else self.DOWN
        return self.hop(
            self.slot(row, at), base + at, self.LINE + at, src, row=self.row, col=self.col + toward
        )

    def over(self, at, src=None):
        return self.hop(
            self.slot(self.row, at),
            self.ACROSS + at,
            self.CROSSED + at,
            src,
            row=self.across,
            col=self.col,
        )

    def side(self, row, at, shift, src=None):
        return self.hop(
            self.slot(row, at),
            self.BESIDE + shift + at,
            self.PASSED + shift + at,
            src,
            row=self.beside,
            col=self.col,
        )

    def keep(self):
        return pltpu.make_async_copy(
            self.source, self.slot(self.row, self.col), self.sems.at[self.KEEP]
        )

    def start(self):
        @pl.when(self.col < SIDE - 1)
        def _():
            self.line(self.row, self.col, 1, self.source).start()

        @pl.when(self.col > 0)
        def _():
            self.line(self.row, self.col, -1, self.source).start()

        self.over(self.col, self.source).start()
        self.side(self.row, self.col, 0, self.source).start()
        self.keep().start()

    def each(self, distance, body):
        for sign in (-1, 1):
            at = self.col + sign * distance

            @pl.when((at >= 0) & (at < SIDE))
            def _(at=at, sign=sign):
                body(at, sign)

    def relay(self, distance):
        def body(at, sign):
            self.line(self.row, at, sign).wait_recv()
            onward = self.col - sign

            @pl.when((onward >= 0) & (onward < SIDE))
            def _():
                self.line(self.row, at, -sign).start()

            self.over(at).start()
            self.side(self.row, at, 0).start()

        self.each(distance, body)

    def cross(self, distance):
        def body(at, sign):
            block = self.slot(self.across, at)
            self.hop(
                block, self.ACROSS + at, self.CROSSED + at, row=self.across, col=self.col
            ).wait_recv()
            self.side(self.across, at, SIDE).start()

        if distance == 0:
            body(self.col, 0)
        else:
            self.each(distance, body)

    def landed(self):
        for at in range(SIDE):
            self.side(self.beside, at, 0).wait_recv()
            self.side(self.corner, at, SIDE).wait_recv()
        self.keep().wait()

    def finish(self):
        for at in range(SIDE):

            @pl.when((at <= self.col) & (self.col < SIDE - 1))
            def _(at=at):
                self.line(self.row, at, 1).wait_send()

            @pl.when((at >= self.col) & (self.col > 0))
            def _(at=at):
                self.line(self.row, at, -1).wait_send()

            self.over(at).wait_send()
            self.side(self.row, at, 0).wait_send()
            self.side(self.across, at, SIDE).wait_send()


def normalize(stream):
    mean_val = jnp.mean(stream, axis=-1, keepdims=True)
    spread = jnp.mean(stream * stream, axis=-1, keepdims=True) - mean_val * mean_val
    inverse = lax.rsqrt(spread + 1e-06)
    return ((stream - mean_val) * inverse, inverse)


def half_lanes(width):
    return lax.broadcasted_iota(jnp.int32, (ROWS, width), 1) < HEAD


def one_half(pair, low, which):
    keep = low if which == 0 else jnp.logical_not(low)
    return jnp.where(keep, pair.astype(f32), 0.0).astype(bf16)


def softmax_rows(queries, keys):
    scores = dot(queries, keys, ((1,), (1,))) * HEAD ** (-0.5)
    place = lax.broadcasted_iota(jnp.int32, scores.shape, 1)
    scores = jnp.where(place < SEQ, scores, -1e30)
    top = jnp.max(scores, axis=-1, keepdims=True)
    grown = jnp.exp(scores - top)
    return grown / jnp.sum(grown, axis=-1, keepdims=True)


class Fold:
    SIDE_SEND, SIDE_RECV, OVER_SEND, OVER_RECV, LINE_SEND, LINE_RECV = 0, 8, 16, 20, 24, 28
    COUNT = 36

    def __init__(self, part, beside, across, line, sems):
        self.part, self.from_beside = part, beside
        self.from_across, self.from_line, self.sems = across, line, sems
        self.row, self.col, self.across, self.beside = position()
        self.corner = lax.rem(self.beside + 2, SIDE)

    def block(self, far, at):
        return self.part((self.across if far else self.row) * SIDE + at)

    def side(self, far, at):
        row = self.corner if far else self.beside
        return remote(
            self.part(row * SIDE + at),
            self.from_beside.at[far, at],
            self.sems.at[self.SIDE_SEND + 4 * far + at],
            self.sems.at[self.SIDE_RECV + 4 * far + at],
            row=self.beside,
            col=self.col,
        )

    def over(self, at):
        return remote(
            self.block(1, at),
            self.from_across.at[at],
            self.sems.at[self.OVER_SEND + at],
            self.sems.at[self.OVER_RECV + at],
            row=self.across,
            col=self.col,
        )

    def line(self, at, toward):
        place = at if toward > 0 else SIDE + at
        return remote(
            self.block(0, at),
            self.from_line.at[place],
            self.sems.at[self.LINE_SEND + at],
            self.sems.at[self.LINE_RECV + place],
            row=self.row,
            col=self.col + toward,
        )

    def add(self, far, at, other):
        block = self.block(far, at)
        block[...] = (block[...].astype(f32) + other[...].astype(f32)).astype(bf16)

    def start(self):
        for far in (1, 0):
            for at in ORDER:
                self.side(far, at).start()

    def fold_side(self, far):
        for at in ORDER:
            self.side(far, at).wait_recv()
            self.add(far, at, self.from_beside.at[far, at])
            if far:
                self.over(at).start()

    def fold_line(self, at):
        self.over(at).wait_recv()
        self.add(0, at, self.from_across.at[at])

        @pl.when(at > self.col)
        def _():
            @pl.when(self.col > 0)
            def _():
                self.line(at, 1).wait_recv()
                self.add(0, at, self.from_line.at[at])

            self.line(at, 1).start()

        @pl.when(at < self.col)
        def _():
            @pl.when(self.col < SIDE - 1)
            def _():
                self.line(at, -1).wait_recv()
                self.add(0, at, self.from_line.at[SIDE + at])

            self.line(at, -1).start()

    def land(self):
        @pl.when(self.col > 0)
        def _():
            self.line(self.col, 1).wait_recv()
            self.add(0, self.col, self.from_line.at[self.col])

        @pl.when(self.col < SIDE - 1)
        def _():
            self.line(self.col, -1).wait_recv()
            self.add(0, self.col, self.from_line.at[SIDE + self.col])

    def result(self):
        return self.block(0, self.col)[...]

    def finish(self):
        for far in range(2):
            for at in range(SIDE):
                self.side(far, at).wait_send()
        for at in range(SIDE):
            self.over(at).wait_send()

            @pl.when(at > self.col)
            def _(at=at):
                self.line(at, 1).wait_send()

            @pl.when(at < self.col)
            def _(at=at):
                self.line(at, -1).wait_send()


def rows_of(index):
    return pl.ds(pl.multiple_of(index * ROWS, 16), ROWS)


BLOCK_ORDER = ('y1', 'c0', 'p0', 'pr1', 'pr2', 'px0', 'cr1', 'y1', 'spot0', 'pr3', 'j1', 'px1', 'px2', 'px3', 'cr2', 'y1', 'j1', 'pf0', 'asm0', 'image0', 'a0', 'image1', 'b0', 'y1', 'ar1', 'br1', 'pick0', 'f1', 'cr3', 'j1', 'f1', 'ar2', 'cx0', 'cx1', 'f1', 'h1', 'j1', 'own0', 'ax0', 'f1', 'cx2', 'f2', 'pick1', 'mine0', 'bx0', 'br2', 'cx3', 'bx1', 'h1', 'y1', 'clear0', 'ar3', 'j1', 'br3', 'ax1', 'ax2', 'cf0', 'ax3', 'h1', 'af0', 'y1', 'h1', 'takeg1', 'bx2', 'f1', 'h2', 'y1', 'bx3', 'cs0', 'gate0', 'takex0', 'bf0', 'gate1', 'h1', 'takeg0', 'j2', 'y1', 'takex1', 'other0', 'ex2', 'bs0', 'sent0', 'j1', 'ex0', 'swap0', 'sent1', 'ex1', 'other1', 'g1', 'ex3', 'g1', 'putg0', '0b0', 'g1', '0f0', '0n0', 'putg1', '1b0', '1f0', 'g1', '1n0', 'as0', 'swap1', 'putx0', '0l3', 'gates0', 'putx1', '0l2', 'k1', '3b0', '1l3', '3f0', 'g2', '2b0', '1l2', 'g1', 'wait0', '2f0', '1l0', '0l0', '2n0', '1l1', 'k1', 'g1', '0l1', 'unimage1', 'unimage0', '2l0', 'k1', '3n0', 'ps0', 'small0', 'k1', '2l3', 'sf0', '2l2', '3l2', '3l0', '2l1', 'sn0', 'sl1', 'sl2', 'sl0', 'k2', '3l1', 'k1', 'done0', 'k1', 'sl3', 'sums0', '3l3', 'done1')


def block_kernel(
    paired,
    x_in,
    dy_in,
    project_in,
    project_out,
    router_weight,
    gain_one,
    bias_one,
    gain_two,
    bias_two,
    eup_ref,
    edown_ref,
    routes_in,
    block_out,
    input_grad,
    small_out,
    up_out,
    down_out,
    x_ref,
    dy_ref,
    pack_ref,
    flat_routes,
    places,
    routes_ref,
    packs,
    w_in,
    w_out,
    w_route,
    vecs,
    normed_one,
    triple,
    mixed,
    hidden,
    normed_two,
    x_all,
    dy_all,
    up_ref,
    down_ref,
    pick,
    logit,
    gate_rows,
    own_gate,
    spots,
    slot_gate,
    slot_x,
    slot_g,
    out_sum,
    back_sum,
    gate_sum,
    gate_out,
    gate_part,
    gate_in,
    beside,
    across,
    line,
    small_part,
    small_beside,
    small_across,
    small_line,
    small_pair,
    weight_in,
    weight_out,
    route_sum,
    vec_sum,
    grad_hidden,
    grad_triple,
    theirs,
    spread_sems,
    fetch_send,
    fetch_recv,
    pass_send,
    pass_recv,
    keep_sems,
    fold_sems,
    gate_send,
    gate_recv,
    swap_send,
    swap_recv,
    give_send,
    give_recv,
    retain_sems,
    pair_sems,
):
    row, col, across_row, beside_row = position()
    corner_row = lax.rem(beside_row + 2, SIDE)
    rank = row * SIDE + col
    half = lax.axis_index("dp") if paired else None
    partner = 1 - half if paired else None

    for source, target in ((x_in, x_ref), (dy_in, dy_ref)):
        target[...] = jnp.zeros_like(target)
        for m in range(2):
            target[m, :SEQ, :] = source[:, m, :]
    pack_ref[:PART, :288] = project_in[...]
    pack_ref[:PART, 288:] = project_out[...]
    pack_ref[PART:, :] = jnp.zeros((PACK - PART, D), bf16)
    vectors = [v[...].astype(f32) for v in (gain_one, bias_one, gain_two, bias_two)]
    tail = jnp.concatenate(
        [router_weight[...].astype(f32)] + vectors + [jnp.zeros((4, PART), f32)], axis=0
    )
    pack_ref[PART:, :PART] = tail.astype(bf16)
    greet(partner)

    def load_routes():
        flat_routes[...] = jnp.full_like(flat_routes, -1)
        for index in range(SHARES):
            for m in range(2):
                flat_routes[TOP * m : TOP * (m + 1), index * ROWS : index * ROWS + SEQ] = routes_in[
                    m, :, index * SEQ : (index + 1) * SEQ
                ]
        places[...] = jnp.full_like(places, -1)

        @pl.loop(0, CHUNKS)
        def _(i):
            lanes = pl.ds(pl.multiple_of(i * LANES, LANES), LANES)
            for pair in range(2 * TOP):
                places[pair // TOP, pair % TOP, pl.ds(i, 1), :] = flat_routes[
                    pair : pair + 1, lanes
                ]

        own = flat_routes[:, :ROWS]
        for index in range(1, SHARES):
            own = jnp.where(rank == index, flat_routes[:, index * ROWS : (index + 1) * ROWS], own)
        routes_ref[...] = jnp.transpose(own.astype(f32))

    low = half_lanes(2 * HEAD)
    tokens = [
        Spread(
            normed_two.at[m],
            lambda r, c, m=m: x_all.at[m, rows_of(r * SIDE + c)],
            spread_sems.at[2 + m],
        )
        for m in range(2)
    ]
    spreads = {
        "p": Spread(pack_ref, lambda r, c: packs.at[r * SIDE + c], spread_sems.at[0]),
        "c": Spread(dy_ref, lambda r, c: dy_all.at[:, rows_of(r * SIDE + c)], spread_sems.at[1]),
        "a": tokens[0],
        "b": tokens[1],
    }

    def assemble():
        for r in range(SIDE):
            for c in range(SIDE):
                at = r * SIDE + c
                w_in[c * PART : (c + 1) * PART, r * 288 : (r + 1) * 288] = packs[at, :PART, :288]
                w_out[r * PART : (r + 1) * PART, c * PART : (c + 1) * PART] = packs[at, :PART, 288:]
                tail = packs[at, PART:, :PART].astype(f32)
                w_route[r * 8 : (r + 1) * 8, c * PART : (c + 1) * PART] = tail[:8]
                if r == 0:
                    vecs[:, c * PART : (c + 1) * PART] = tail[8:]

    def attend(m):
        stream = x_ref[m].astype(f32)
        normal, _ = normalize(stream)
        first = (normal * vecs[0:1] + vecs[1:2]).astype(bf16)
        normed_one[m] = first
        triple[m] = dot(first, w_in[...], ((1,), (0,))).astype(bf16)
        for pair in range(HEADS // 2):
            lanes = 2 * HEAD * pair
            queries = triple[m, :, lanes : lanes + 128]
            keys = triple[m, :, D + lanes : D + lanes + 128]
            values = triple[m, :, 2 * D + lanes : 2 * D + lanes + 128]
            parts = []
            for which in range(2):
                prob = softmax_rows(queries, one_half(keys, low, which)).astype(bf16)
                parts.append(dot(prob, values, ((1,), (0,))))
            mixed[m, :, lanes : lanes + 128] = jnp.where(low, parts[0], parts[1]).astype(bf16)
        after = stream + dot(mixed[m], w_out[...], ((1,), (0,)))
        hidden[m] = after
        normal, _ = normalize(after)
        normed_two[m] = (normal * vecs[2:3] + vecs[3:4]).astype(bf16)

    mats = ((eup_ref, up_ref), (edown_ref, down_ref))
    shares = (half,) if paired else (0, 1)

    def into(whole, own, owner):
        return whole.at[own, owner // SIDE, pl.ds(lax.rem(owner, SIDE) * PART, PART), :]

    def fetch(number, mat, own, step):
        blocks, whole = mats[mat]
        to, _ = peer(step)
        return remote(
            blocks.at[own * SHARES + to],
            into(whole, own, rank),
            fetch_send.at[number, mat, step],
            fetch_recv.at[number, mat, step],
            row=to // SIDE,
            col=lax.rem(to, SIDE),
        )

    def arrival(number, mat, own, step):
        _, source = peer(step)
        block = into(mats[mat][1], own, source)
        return remote(
            block,
            block,
            fetch_send.at[number, mat, step],
            fetch_recv.at[number, mat, step],
            row=source // SIDE,
            col=lax.rem(source, SIDE),
        )

    def hand(mat, step):
        blocks, whole = mats[mat]
        _, source = peer(step)
        block = into(whole, half, source)
        src = blocks.at[half * SHARES + rank] if isinstance(step, int) else block
        return remote(src, block, pass_send.at[mat, step], pass_recv.at[mat, step], dp=partner)

    def keep(number, mat, own):
        blocks, whole = mats[mat]
        return pltpu.make_async_copy(
            blocks.at[own * SHARES + rank], into(whole, own, rank), keep_sems.at[number, mat]
        )

    def begin_fetch():
        for number, own in enumerate(shares):
            for mat in range(2):
                keep(number, mat, own).start()
                if paired:
                    hand(mat, 0).start()

    def fetch_some(first, last):
        for number, own in enumerate(shares):

            @pl.loop(first, last)
            def _(step):
                for mat in range(2):
                    fetch(number, mat, own, step).start()

    def pass_some(first, last):
        for number, own in enumerate(shares):

            @pl.loop(first, last)
            def _(step):
                for mat in range(2):
                    arrival(number, mat, own, step).wait_recv()
                    if paired:
                        hand(mat, step).start()

    def have_own():
        for number, own in enumerate(shares):
            for mat in range(2):
                keep(number, mat, own).wait()

    def side_steps(number):
        return (number * SHARES // 2, (number + 1) * SHARES // 2)

    def have_other(number):
        if paired:

            @pl.loop(*side_steps(number))
            def _(step):
                for mat in range(2):
                    hand(mat, step).wait_recv()

    def handed(number):
        if paired:

            @pl.loop(*side_steps(number))
            def _(step):
                for mat in range(2):
                    hand(mat, step).wait_send()

    slot_place = lax.broadcasted_iota(jnp.int32, (SLOTS, LANES), 0).astype(f32)
    names = lax.broadcasted_iota(jnp.int32, (32, LANES), 0)

    def own_routes(m, q):
        mine = rank + SHARES * q
        return (places[m, 0] == mine, places[m, 1] == mine)

    def find_spots():
        load_routes()
        down_lane = lax.broadcasted_iota(jnp.int32, (LANES, LANES), 0)
        lane = lax.broadcasted_iota(jnp.int32, (LANES, LANES), 1)
        upper = jnp.where(down_lane <= lane, 1.0, 0.0).astype(bf16)
        below = lax.broadcasted_iota(jnp.int32, (32, 32), 0)
        above = lax.broadcasted_iota(jnp.int32, (32, 32), 1)
        earlier = jnp.where(below > above, 1.0, 0.0).astype(bf16)
        ones = jnp.ones((LANES, LANES), bf16)
        for m in range(2):
            for q in range(OWN):
                one, two = own_routes(m, q)
                routed = jnp.where(one | two, 1.0, 0.0).astype(bf16)
                within = dot(routed, upper, ((1,), (0,)))
                per_row = dot(routed, ones, ((1,), (0,))).astype(bf16)
                before = dot(earlier, per_row, ((1,), (0,)))
                spots[m, q] = jnp.where(one | two, within + before - 1.0, -1.0)

    def make_pick(m):
        @pl.loop(0, CHUNKS)
        def _(i):
            lanes = pl.ds(pl.multiple_of(i * LANES, LANES), LANES)
            for q in range(OWN):
                hit = spots[m, q, pl.ds(i, 1), :] == slot_place
                pick[m, q * SLOTS : (q + 1) * SLOTS, lanes] = jnp.where(hit, 1.0, 0.0).astype(bf16)

    def take(source, target, m):
        found = dot(pick[m], source[m], ((1,), (0,))).astype(bf16)
        for q in range(OWN):
            target[q, m * SLOTS : (m + 1) * SLOTS, :] = found[q * SLOTS : (q + 1) * SLOTS]

    def make_gates(m):
        logit[...] = dot(w_route[...].astype(bf16), x_all[m], ((1,), (1,)))
        for k in range(TOP):
            gate_rows[k] = jnp.zeros((32, LANES), f32)

        @pl.loop(0, CHUNKS)
        def _(i):
            piece = logit[:, pl.ds(pl.multiple_of(i * LANES, LANES), LANES)]
            for k in range(TOP):
                chosen = places[m, k, pl.ds(i, 1), :] == names
                gate_rows[k, pl.ds(i, 1), :] = jnp.sum(
                    jnp.where(chosen, piece, 0.0), axis=0, keepdims=True
                )

        first, second = gate_rows[0], gate_rows[1]
        top = jnp.maximum(first, second)
        first, second = jnp.exp(first - top), jnp.exp(second - top)
        total = first + second
        first, second = first / total, second / total
        rows = slice(m * SLOTS, (m + 1) * SLOTS)
        for q in range(OWN):
            one, two = own_routes(m, q)
            own_gate[q] = jnp.where(one, first, jnp.where(two, second, 0.0))
            slot_gate[q, rows, :] = jnp.zeros((SLOTS, LANES), f32)

        @pl.loop(0, CHUNKS)
        def _(i):
            for q in range(OWN):
                hit = spots[m, q, pl.ds(i, 1), :] == slot_place
                slot_gate[q, rows, :] += jnp.where(hit, own_gate[q, pl.ds(i, 1), :], 0.0)

        for q in range(OWN):
            slot_gate[q, rows, :] = jnp.broadcast_to(
                jnp.sum(slot_gate[q, rows, :], axis=1, keepdims=True), (SLOTS, LANES)
            )

    def expert(q, number):
        if number == 0:
            out_sum[q] = jnp.zeros((2 * SLOTS, D), f32)
            back_sum[q] = jnp.zeros((2 * SLOTS, D), f32)
            gate_sum[q] = jnp.zeros((2 * SLOTS, LANES), f32)
        near, far = ((row, beside_row), (across_row, corner_row))[number]

        @pl.loop(0, 2)
        def _(turn):
            f = jnp.where(turn == 0, near, far)
            inputs, cots = slot_x[q], slot_g[q]
            up, down = up_ref[q, f], down_ref[q, f]
            pre = dot(inputs, up, ((1,), (0,)))
            grad = dot(cots, down, ((1,), (0,)))
            cdf = 0.5 * (1.0 + lax.erf(pre * sqrt_half))
            act = pre * cdf
            gate = slot_gate[q][:, :1]
            scaled = (gate * act).astype(bf16)
            gate_sum[q] += jnp.broadcast_to(
                jnp.sum(grad * act, axis=1, keepdims=True), (2 * SLOTS, LANES)
            )
            slope = cdf + pre * jnp.exp(-0.5 * pre * pre) * inv_root_tau
            grad_pre = (gate * grad * slope).astype(bf16)
            out_sum[q] += dot(scaled, down, ((1,), (1,)))
            back_sum[q] += dot(grad_pre, up, ((1,), (1,)))
            up_ref[q, f] = dot(inputs, grad_pre, ((0,), (0,))).astype(bf16)
            down_ref[q, f] = dot(cots, scaled, ((0,), (0,))).astype(bf16)

        if number == 1:
            slot_x[q] = out_sum[q].astype(bf16)
            slot_g[q] = back_sum[q].astype(bf16)

    def put(source, target, m):
        rows = slice(m * SLOTS, (m + 1) * SLOTS)
        stacked = jnp.concatenate([source[0, rows, :], source[1, rows, :]], axis=0)

        @pl.loop(0, CHUNKS // 2)
        def _(i):
            there = pl.ds(pl.multiple_of(i * 2 * LANES, 2 * LANES), 2 * LANES)
            target[m, there, :] = dot(pick[m, :, there], stacked, ((0,), (0,))).astype(bf16)

    def gate_back():
        gate_part[...] = jnp.zeros_like(gate_part)
        for m in range(2):
            rows = slice(m * SLOTS, (m + 1) * SLOTS)
            for k in range(TOP):
                gate_out[m, k] = jnp.zeros((32, LANES), f32)

            @pl.loop(0, CHUNKS)
            def _(i):
                for q in range(OWN):
                    hit = spots[m, q, pl.ds(i, 1), :] == slot_place
                    found = jnp.sum(
                        jnp.where(hit, gate_sum[q, rows, :], 0.0), axis=0, keepdims=True
                    )
                    for k in range(TOP):
                        here = places[m, k, pl.ds(i, 1), :] == rank + SHARES * q
                        gate_out[m, k, pl.ds(i, 1), :] += jnp.where(here, found, 0.0)

            for to in range(SHARES):
                first = to * ROWS // LANES
                shift = to * ROWS - first * LANES
                span = -(-(shift + ROWS) // LANES)
                for k in range(TOP):
                    wide = jnp.concatenate(
                        [gate_out[m, k, first + n : first + n + 1, :] for n in range(span)], axis=1
                    )
                    gate_part[to, 2 * m + k : 2 * m + k + 1, :ROWS] = wide[:, shift : shift + ROWS]

    def gate_copy(step):
        to, _ = peer(step)
        return remote(
            gate_part.at[to],
            gate_in.at[rank],
            gate_send.at[step],
            gate_recv.at[step],
            row=to // SIDE,
            col=lax.rem(to, SIDE),
        )

    def gate_wait(step):
        _, source = peer(step)
        return remote(
            gate_part.at[rank],
            gate_in.at[source],
            gate_send.at[step],
            gate_recv.at[step],
            row=source // SIDE,
            col=lax.rem(source, SIDE),
        )

    def start_gates():
        gate_back()
        gate_in[rank] = gate_part[rank]

        @pl.loop(1, SHARES)
        def _(step):
            gate_copy(step).start()

    def wait_gates():
        @pl.loop(1, SHARES)
        def _(step):
            gate_wait(step).wait_recv()

    folds = [
        Fold(
            lambda index, n=n: (dy_all if n < 2 else x_all).at[n % 2, rows_of(index)],
            beside.at[n],
            across.at[n],
            line.at[n],
            fold_sems.at[n],
        )
        for n in range(4)
    ]
    small = Fold(
        lambda index: small_part.at[index], small_beside, small_across, small_line, fold_sems.at[4]
    )

    givers = ((up_ref, up_out), (down_ref, down_out))

    def swap(mat, step):
        to, _ = peer(step)
        return remote(
            into(givers[mat][0], partner, to),
            theirs.at[step, mat],
            swap_send.at[step, mat],
            swap_recv.at[step, mat],
            dp=partner,
        )

    def give(number, mat, q, step):
        to, _ = peer(step)
        return remote(
            into(givers[mat][0], q, to),
            givers[mat][1].at[rank if paired else q * SHARES + rank],
            give_send.at[number, mat, step],
            give_recv.at[number, mat, step],
            row=to // SIDE,
            col=lax.rem(to, SIDE),
        )

    def given(number, mat, q, step):
        _, source = peer(step)
        block = givers[mat][1].at[source if paired else q * SHARES + source]
        return remote(
            block,
            block,
            give_send.at[number, mat, step],
            give_recv.at[number, mat, step],
            row=source // SIDE,
            col=lax.rem(source, SIDE),
        )

    def retain(number, mat, q):
        return pltpu.make_async_copy(
            into(givers[mat][0], q, rank),
            givers[mat][1].at[rank if paired else q * SHARES + rank],
            retain_sems.at[number, mat],
        )

    def start_swap(number):
        if paired:

            @pl.loop(*side_steps(number))
            def _(step):
                for mat in range(2):
                    swap(mat, step).start()

    def give_some(first, last):
        for number, q in enumerate(shares):

            @pl.loop(first, last)
            def _(step):
                for mat in range(2):
                    if paired:
                        swap(mat, step).wait_recv()
                        to, _ = peer(step)
                        block = into(givers[mat][0], half, to)
                        block[...] = (
                            block[...].astype(f32) + theirs[step, mat].astype(f32)
                        ).astype(bf16)

                    @pl.when(step > 0)
                    def _():
                        give(number, mat, q, step).start()

                    @pl.when(step == 0)
                    def _():
                        retain(number, mat, q).start()

    token_names = lax.broadcasted_iota(jnp.int32, (ROWS, 32), 1).astype(f32)
    exact = lax.Precision.HIGHEST

    def clear_sums():
        weight_in[...] = jnp.zeros_like(weight_in)
        weight_out[...] = jnp.zeros_like(weight_out)
        route_sum[...] = jnp.zeros_like(route_sum)
        vec_sum[...] = jnp.zeros_like(vec_sum)

    def norm_back(grad_out, normal, inverse, which):
        scaled = grad_out * vecs[which : which + 1]
        vec_sum[which : which + 1] += jnp.sum(grad_out * normal, axis=0, keepdims=True)
        vec_sum[which + 1 : which + 2] += jnp.sum(grad_out, axis=0, keepdims=True)
        return inverse * (
            scaled
            - jnp.mean(scaled, axis=-1, keepdims=True)
            - normal * jnp.mean(scaled * normal, axis=-1, keepdims=True)
        )

    def attend_back(m):
        folds[m].land()
        grad_norm = folds[m].result().astype(f32)
        router = w_route[...]
        logits = dot(normed_two[m], router.astype(bf16), ((1,), (1,)))
        hits = [
            routes_ref[:, TOP * m + k : TOP * m + k + 1] == token_names for k in range(TOP)
        ]
        picked = [jnp.sum(jnp.where(hit, logits, 0.0), axis=1, keepdims=True) for hit in hits]
        top = jnp.maximum(picked[0], picked[1])
        grown = [jnp.exp(v - top) for v in picked]
        total = grown[0] + grown[1]
        gates = [v / total for v in grown]
        columns = jnp.transpose(jnp.sum(gate_in[...], axis=0))[:ROWS]
        grads = [columns[:, 2 * m + k : 2 * m + k + 1] for k in range(TOP)]
        mean_grad = gates[0] * grads[0] + gates[1] * grads[1]
        dense = jnp.zeros((ROWS, 32), f32)
        for k in range(TOP):
            dense = dense + jnp.where(hits[k], gates[k] * (grads[k] - mean_grad), 0.0)
        route_sum[...] += lax.dot_general(
            dense,
            normed_two[m].astype(f32),
            (((0,), (0,)), ((), ())),
            preferred_element_type=f32,
            precision=exact,
        )
        grad_norm = grad_norm + lax.dot_general(
            dense, router, (((1,), (0,)), ((), ())), preferred_element_type=f32, precision=exact
        )
        normal, inverse = normalize(hidden[m])
        into_hidden = dy_ref[m].astype(f32) + norm_back(grad_norm, normal, inverse, 2)
        grad_hidden[m] = into_hidden
        grad_attn = into_hidden.astype(bf16)
        weight_out[...] += dot(mixed[m], grad_attn, ((0,), (0,)))
        grad_mixed = dot(grad_attn, w_out[...], ((1,), (1,))).astype(bf16)
        grad_triple[m, :, :D] = grad_mixed

        @pl.loop(0, HEADS // 2)
        def _(pair):
            def lanes(n):
                return pl.ds(pl.multiple_of(n * D + pair * 128, 128), 128)

            queries, keys, values = (triple[m, :, lanes(n)] for n in range(3))
            cots = grad_triple[m, :, lanes(0)]
            parts = []
            for which in range(2):
                prob = softmax_rows(queries, one_half(keys, low, which))
                weights = prob.astype(bf16)
                grad_prob = dot(cots, one_half(values, low, which), ((1,), (1,)))
                grad_scores = prob * (
                    grad_prob - jnp.sum(prob * grad_prob, axis=-1, keepdims=True)
                )
                grad_scores = grad_scores.astype(bf16)
                parts.append(
                    (
                        dot(grad_scores, keys, ((1,), (0,))) * HEAD ** (-0.5),
                        dot(grad_scores, queries, ((0,), (0,))) * HEAD ** (-0.5),
                        dot(weights, cots, ((0,), (0,))),
                    )
                )
            for n in range(3):
                grad_triple[m, :, lanes(n)] = jnp.where(
                    low, parts[0][n], parts[1][n]
                ).astype(bf16)

        weight_in[...] += dot(normed_one[m], grad_triple[m], ((0,), (0,)))
        grad_norm = dot(grad_triple[m], w_in[...], ((1,), (1,)))
        normal, inverse = normalize(x_ref[m].astype(f32))
        input_grad[m] = (grad_hidden[m] + norm_back(grad_norm, normal, inverse, 0))[:SEQ]

    def gather_small():
        for r in range(SIDE):
            for c in range(SIDE):
                at = r * SIDE + c
                small_part[at, :PART, :288] = weight_in[
                    c * PART : (c + 1) * PART, r * 288 : (r + 1) * 288
                ].astype(bf16)
                small_part[at, :PART, 288:] = weight_out[
                    r * PART : (r + 1) * PART, c * PART : (c + 1) * PART
                ].astype(bf16)
                tail = jnp.concatenate([route_sum[r * 8 : (r + 1) * 8, :], vec_sum[...]], axis=0)
                small_part[at, PART:, :PART] = tail[:, c * PART : (c + 1) * PART].astype(bf16)
                small_part[at, PART:, PART:] = jnp.zeros((16, D - PART), bf16)

    pair = None
    if paired:
        pair = remote(
            small_pair.at[0], small_pair.at[1], pair_sems.at[0], pair_sems.at[1], dp=partner
        )

    def end_small():
        small.land()
        if paired:
            small_pair[0] = small.result()
            pair.start()

    def finish_small():
        if paired:
            pair.wait_recv()
            small_out[...] = small.result().astype(f32) + small_pair[1].astype(f32)
            pair.wait_send()
        else:
            small_out[...] = small.result().astype(f32)

    def finish_branch(m):
        folds[2 + m].land()
        block_out[m] = (hidden[m] + folds[2 + m].result().astype(f32)).astype(bf16)[:SEQ]

    limits = {"f": SHARES // 2, "y": SHARES, "h": SHARES // 2, "j": SHARES, "g": SHARES // 2, "k": SHARES}
    at = {"f": 1, "y": SHARES // 2, "h": 1, "j": SHARES // 2, "g": 0, "k": SHARES // 2}
    ranged = {
        "f": fetch_some,
        "y": fetch_some,
        "h": pass_some,
        "j": pass_some,
        "g": give_some,
        "k": give_some,
    }
    plain = {
        "own": begin_fetch,
        "asm": assemble,
        "spot": find_spots,
        "mine": have_own,
        "gates": start_gates,
        "wait": wait_gates,
        "clear": clear_sums,
        "sums": end_small,
    }
    numbered = {
        "other": have_other,
        "sent": handed,
        "swap": start_swap,
        "image": attend,
        "pick": make_pick,
        "gate": make_gates,
        "takex": lambda m: take(x_all, slot_x, m),
        "takeg": lambda m: take(dy_all, slot_g, m),
        "putx": lambda m: put(slot_x, x_all, m),
        "putg": lambda m: put(slot_g, dy_all, m),
        "unimage": attend_back,
        "done": finish_branch,
    }
    for step in BLOCK_ORDER:
        name, number = step[:-1], int(step[-1], 16)
        if name in ranged:
            last = min(at[name] + number, limits[name])
            ranged[name](at[name], last)
            at[name] = last
        elif name in plain:
            plain[name]()
        elif name in numbered:
            numbered[name](number)
        elif name == "ex":
            expert(number // 2 if half is None else (half, partner)[number // 2], number % 2)
        elif name == "small":
            gather_small()
            small.start()
        elif name[0] in spreads:
            act = spreads[name[0]]
            if name[1:] == "":
                act.start()
            elif name[1:] == "r":
                act.relay(number)
            elif name[1:] == "x":
                act.cross(number)
            elif name[1:] == "f":
                act.landed()
            elif name[1:] == "s":
                act.finish()
        else:
            fold = small if name[0] == "s" else folds[int(name[0])]
            if name[1:] == "b":
                fold.start()
            elif name[1:] == "f":
                fold.fold_side(1)
            elif name[1:] == "n":
                fold.fold_side(0)
            else:
                fold.fold_line(number)
    finish_small()

    for fold in folds:
        fold.finish()
    small.finish()

    @pl.loop(1, SHARES)
    def _(step):
        gate_copy(step).wait_send()

    for number, q in enumerate(shares):
        for mat in range(2):
            retain(number, mat, q).wait()

        @pl.loop(1, SHARES)
        def _(step):
            for mat in range(2):
                fetch(number, mat, q, step).wait_send()

        for mat in range(2):

            @pl.loop(1, SHARES)
            def _(step):
                given(number, mat, q, step).wait_recv()
                give(number, mat, q, step).wait_send()

    if paired:

        @pl.loop(0, SHARES)
        def _(step):
            for mat in range(2):
                swap(mat, step).wait_send()


def block_call(paired, *operands):
    block, small = (ROWS, D), (PACK, D)
    experts = SHARES if paired else OWN * SHARES
    numbers = 1 if paired else 2
    outputs = [
        ((2, SEQ, D), bf16, VMEM),
        ((2, SEQ, D), f32, VMEM),
        (small, f32, VMEM),
        ((experts, PART, FPART), bf16, ANY),
        ((experts, PART, FPART), bf16, ANY),
    ]
    scratch = [
        ((2,) + block, bf16),
        ((2,) + block, bf16),
        (small, bf16),
        ((8, TOKENS), jnp.int32),
        ((2, TOP, 32, LANES), jnp.int32),
        ((ROWS, 8), f32),
        ((SHARES,) + small, bf16),
        ((D, WIDE), bf16),
        ((D, D), bf16),
        ((32, D), f32),
        ((8, D), f32),
        ((2,) + block, bf16),
        ((2, ROWS, WIDE), bf16),
        ((2,) + block, bf16),
        ((2,) + block, f32),
        ((2,) + block, bf16),
        ((2, TOKENS, D), bf16),
        ((2, TOKENS, D), bf16),
        ((OWN, SIDE, D, FPART), bf16),
        ((OWN, SIDE, D, FPART), bf16),
        ((2, OWN * SLOTS, TOKENS), bf16),
        ((32, TOKENS), f32),
        ((TOP, 32, LANES), f32),
        ((OWN, 32, LANES), f32),
        ((2, OWN, 32, LANES), f32),
        ((OWN, 2 * SLOTS, LANES), f32),
        ((OWN, 2 * SLOTS, D), bf16),
        ((OWN, 2 * SLOTS, D), bf16),
        ((OWN, 2 * SLOTS, D), f32),
        ((OWN, 2 * SLOTS, D), f32),
        ((OWN, 2 * SLOTS, LANES), f32),
        ((2, TOP, 32, LANES), f32),
        ((SHARES, 8, 256), f32),
        ((SHARES, 8, 256), f32),
        ((4, 2, SIDE) + block, bf16),
        ((4, SIDE) + block, bf16),
        ((4, 2 * SIDE) + block, bf16),
        ((SHARES,) + small, bf16),
        ((2, SIDE) + small, bf16),
        ((SIDE,) + small, bf16),
        ((2 * SIDE,) + small, bf16),
        ((2,) + small, bf16),
        ((D, WIDE), f32),
        ((D, D), f32),
        ((32, D), f32),
        ((8, D), f32),
        ((2,) + block, f32),
        ((2, ROWS, WIDE), bf16),
        ((SHARES, 2, PART, FPART) if paired else (1, 2, 16, LANES), bf16),
    ]
    semaphores = [
        (4, Spread.COUNT),
        (numbers, 2, SHARES),
        (numbers, 2, SHARES),
        (2, SHARES),
        (2, SHARES),
        (numbers, 2),
        (5, Fold.COUNT),
        (SHARES,),
        (SHARES,),
        (SHARES, 2),
        (SHARES, 2),
        (numbers, 2, SHARES),
        (numbers, 2, SHARES),
        (numbers, 2),
        (2,),
    ]
    return pl.pallas_call(
        functools.partial(block_kernel, paired),
        out_shape=[jax.ShapeDtypeStruct(shape, kind) for shape, kind, _ in outputs],
        in_specs=[VMEM] * 9 + [ANY, ANY, VMEM],
        out_specs=[space for _, _, space in outputs],
        scratch_shapes=[pltpu.VMEM(shape, kind) for shape, kind in scratch]
        + [DMA(shape) for shape in semaphores],
        compiler_params=pltpu.CompilerParams(
            collective_id=0, has_side_effects=True, vmem_limit_bytes=63 << 20
        ),
        name="block",
    )(*operands)


def final_kernel(
    output, grad, small, up, down, output_rows, grad_rows, g_in, g_out, *rest
):
    *g_vecs, g_router, g_up, g_down = rest
    g_up[...] = up[...].astype(f32)
    g_down[...] = down[...].astype(f32)

    @pl.when(pl.program_id(0) == 0)
    def _():
        for m in range(2):
            output_rows[:, m, :] = output[m]
            grad_rows[:, m, :] = grad[m]
        g_in[...] = small[:PART, :288]
        g_out[...] = small[:PART, 288:]
        g_router[...] = small[PART : PART + 8, :PART]
        for n in range(4):
            g_vecs[n][...] = small[PART + 8 + n : PART + 9 + n, :PART]


def final_call(output, grad, small, up, down):
    steps = 4
    share = up.shape[0] // steps if up.shape[0] % steps == 0 else up.shape[0]
    blocks = pl.BlockSpec((share, PART, FPART), lambda i: (i, 0, 0))

    def whole(*shape):
        return pl.BlockSpec(shape, lambda i: (0,) * len(shape))

    sizes = [
        ((SEQ, 2, D), bf16),
        ((SEQ, 2, D), f32),
        ((PART, 288), f32),
        ((PART, PART), f32),
        ((1, PART), f32),
        ((1, PART), f32),
        ((1, PART), f32),
        ((1, PART), f32),
        ((8, PART), f32),
        (up.shape, f32),
        (up.shape, f32),
    ]
    return pl.pallas_call(
        final_kernel,
        grid=(up.shape[0] // share,),
        out_shape=[jax.ShapeDtypeStruct(shape, kind) for shape, kind in sizes],
        in_specs=[whole(2, SEQ, D), whole(2, SEQ, D), whole(PACK, D), blocks, blocks],
        out_specs=[whole(*shape) for shape, _ in sizes[:9]] + [blocks, blocks],
        name="final",
    )(output, grad, small, up, down)


def on_device(
    block_input,
    first_gain,
    first_bias,
    project_in,
    project_out,
    second_gain,
    second_bias,
    router_weight,
    expert_up,
    expert_down,
    routes,
    out_grad,
):
    paired = lax.axis_size("dp") == 2
    block_output, input_grad, small, up_sum, down_sum = block_call(
        paired,
        block_input.transpose(1, 0, 2),
        out_grad.transpose(1, 0, 2),
        project_in,
        project_out,
        router_weight.T,
        first_gain[None],
        first_bias[None],
        second_gain[None],
        second_bias[None],
        expert_up,
        expert_down,
        routes.transpose(0, 2, 1),
    )
    if not paired:
        small = lax.psum(small, "dp")
        up_sum = lax.psum_scatter(up_sum, "dp", scatter_dimension=0, tiled=True)
        down_sum = lax.psum_scatter(down_sum, "dp", scatter_dimension=0, tiled=True)
    output, grad, g_in, g_out, *g_vecs, g_router, g_up, g_down = final_call(
        block_output, input_grad, small, up_sum, down_sum
    )
    return (
        output.transpose(1, 0, 2),
        grad.transpose(1, 0, 2),
        g_vecs[0][0],
        g_vecs[1][0],
        g_in,
        g_out,
        g_vecs[2][0],
        g_vecs[3][0],
        g_router.T,
        g_up,
        g_down,
    )


def solution(mesh):
    in_specs = (
        P(None, ("dp", "row", "col"), None),
        P("col"),
        P("col"),
        P("col", "row"),
        P("row", "col"),
        P("col"),
        P("col"),
        P("col", "row"),
        P(None, "col", "row"),
        P(None, "col", "row"),
        P(None, "dp", None),
        P(None, ("dp", "row", "col"), None),
    )
    out_specs = (
        P(None, ("dp", "row", "col"), None),
        P(None, ("dp", "row", "col"), None),
        P("col"),
        P("col"),
        P("col", "row"),
        P("row", "col"),
        P("col"),
        P("col"),
        P("col", "row"),
        P("dp", "col", "row"),
        P("dp", "col", "row"),
    )
    return jax.shard_map(
        on_device, mesh=mesh, in_specs=in_specs, out_specs=out_specs, check_vma=False
    )
```

```python
import functools

import jax
import jax.numpy as jnp
from jax import lax
from jax.experimental import pallas as pl
from jax.experimental.pallas import tpu as pltpu
from jax.sharding import PartitionSpec as P

D = 384
HEADS = 6
HEAD = 64
TOP = 2
SEQ = 197
ROWS = 200
SLOTS = 256
SIDE = 4
SHARES = SIDE * SIDE
OWN = 2
PART = D // SIDE
WIDE = 3 * D
FPART = 384
PACK = PART + 16

sqrt_half = 0.7071067811865476
inv_root_tau = 0.3989422804014327
bf16 = jnp.bfloat16
f32 = jnp.float32
MESH = pl.DeviceIdType.MESH
ANY = pl.BlockSpec(memory_space=pl.ANY)
TOKENS = SHARES * ROWS
LANES = 128
CHUNKS = TOKENS // LANES
ORDER = (3, 0, 2, 1)
VMEM = pl.BlockSpec(memory_space=pltpu.VMEM)
DMA = pltpu.SemaphoreType.DMA


def dot(left, right, dims):
    return lax.dot_general(left, right, (dims, ((), ())), preferred_element_type=f32)


def position():
    row = lax.axis_index("row")
    col = lax.axis_index("col")
    across = lax.rem(row + 2, SIDE)
    beside = row + 1 - 2 * lax.rem(row, 2)
    return (row, col, across, beside)


def peer(step):
    row, col, across, beside = position()
    group, shift = step // SIDE, lax.rem(step, SIDE)
    other = jnp.where(
        group == 0,
        row,
        jnp.where(group == 1, beside, jnp.where(group == 2, across, lax.rem(beside + 2, SIDE))),
    )
    return (
        other * SIDE + lax.rem(col + shift, SIDE),
        other * SIDE + lax.rem(col + SIDE - shift, SIDE),
    )


def remote(src, dst, send, recv, **target):
    return pltpu.make_async_remote_copy(
        src_ref=src,
        dst_ref=dst,
        send_sem=send,
        recv_sem=recv,
        device_id=target,
        device_id_type=MESH,
    )


def greet(partner):
    row, col, _, _ = position()
    rank = row * SIDE + col
    barrier = pltpu.get_barrier_semaphore()

    @pl.loop(1, SHARES)
    def _(step):
        other = lax.rem(rank + step, SHARES)
        pl.semaphore_signal(
            barrier,
            inc=1,
            device_id={"row": other // SIDE, "col": lax.rem(other, SIDE)},
            device_id_type=MESH,
        )

    if partner is not None:
        pl.semaphore_signal(barrier, inc=1, device_id={"dp": partner}, device_id_type=MESH)


def meet(partner):
    pl.semaphore_wait(
        pltpu.get_barrier_semaphore(), SHARES if partner is not None else SHARES - 1
    )


class Spread:
    UP, DOWN, LINE, ACROSS, CROSSED, BESIDE, PASSED, KEEP = 0, 4, 8, 12, 16, 20, 28, 36
    COUNT = 37

    def __init__(self, source, slot, sems):
        self.source, self.slot, self.sems = source, slot, sems
        self.row, self.col, self.across, self.beside = position()
        self.corner = lax.rem(self.beside + 2, SIDE)

    def hop(self, block, send, recv, src=None, **target):
        src = block if src is None else src
        return remote(src, block, self.sems.at[send], self.sems.at[recv], **target)

    def line(self, row, at, toward, src=None):
        base = self.UP if toward > 0 else self.DOWN
        return self.hop(
            self.slot(row, at), base + at, self.LINE + at, src, row=self.row, col=self.col + toward
        )

    def over(self, at, src=None):
        return self.hop(
            self.slot(self.row, at),
            self.ACROSS + at,
            self.CROSSED + at,
            src,
            row=self.across,
            col=self.col,
        )

    def side(self, row, at, shift, src=None):
        return self.hop(
            self.slot(row, at),
            self.BESIDE + shift + at,
            self.PASSED + shift + at,
            src,
            row=self.beside,
            col=self.col,
        )

    def keep(self):
        return pltpu.make_async_copy(
            self.source, self.slot(self.row, self.col), self.sems.at[self.KEEP]
        )

    def start(self):
        @pl.when(self.col < SIDE - 1)
        def _():
            self.line(self.row, self.col, 1, self.source).start()

        @pl.when(self.col > 0)
        def _():
            self.line(self.row, self.col, -1, self.source).start()

        self.over(self.col, self.source).start()
        self.side(self.row, self.col, 0, self.source).start()
        self.keep().start()

    def each(self, distance, body):
        for sign in (-1, 1):
            at = self.col + sign * distance

            @pl.when((at >= 0) & (at < SIDE))
            def _(at=at, sign=sign):
                body(at, sign)

    def relay(self, distance):
        def body(at, sign):
            self.line(self.row, at, sign).wait_recv()
            onward = self.col - sign

            @pl.when((onward >= 0) & (onward < SIDE))
            def _():
                self.line(self.row, at, -sign).start()

            self.over(at).start()
            self.side(self.row, at, 0).start()

        self.each(distance, body)

    def cross(self, distance):
        def body(at, sign):
            block = self.slot(self.across, at)
            self.hop(
                block, self.ACROSS + at, self.CROSSED + at, row=self.across, col=self.col
            ).wait_recv()
            self.side(self.across, at, SIDE).start()

        if distance == 0:
            body(self.col, 0)
        else:
            self.each(distance, body)

    def landed(self):
        for at in range(SIDE):
            self.side(self.beside, at, 0).wait_recv()
            self.side(self.corner, at, SIDE).wait_recv()
        self.keep().wait()

    def finish(self):
        for at in range(SIDE):

            @pl.when((at <= self.col) & (self.col < SIDE - 1))
            def _(at=at):
                self.line(self.row, at, 1).wait_send()

            @pl.when((at >= self.col) & (self.col > 0))
            def _(at=at):
                self.line(self.row, at, -1).wait_send()

            self.over(at).wait_send()
            self.side(self.row, at, 0).wait_send()
            self.side(self.across, at, SIDE).wait_send()


def normalize(stream):
    mean_val = jnp.mean(stream, axis=-1, keepdims=True)
    spread = jnp.mean(stream * stream, axis=-1, keepdims=True) - mean_val * mean_val
    inverse = lax.rsqrt(spread + 1e-06)
    return ((stream - mean_val) * inverse, inverse)


def half_lanes(width):
    return lax.broadcasted_iota(jnp.int32, (ROWS, width), 1) < HEAD


def one_half(pair, low, which):
    keep = low if which == 0 else jnp.logical_not(low)
    return jnp.where(keep, pair.astype(f32), 0.0).astype(bf16)


def softmax_rows(queries, keys):
    scores = dot(queries, keys, ((1,), (1,))) * HEAD ** (-0.5)
    place = lax.broadcasted_iota(jnp.int32, scores.shape, 1)
    scores = jnp.where(place < SEQ, scores, -1e30)
    top = jnp.max(scores, axis=-1, keepdims=True)
    grown = jnp.exp(scores - top)
    return grown / jnp.sum(grown, axis=-1, keepdims=True)


class Fold:
    SIDE_SEND, SIDE_RECV, OVER_SEND, OVER_RECV, LINE_SEND, LINE_RECV = 0, 8, 16, 20, 24, 28
    COUNT = 36

    def __init__(self, part, beside, across, line, sems):
        self.part, self.from_beside = part, beside
        self.from_across, self.from_line, self.sems = across, line, sems
        self.row, self.col, self.across, self.beside = position()
        self.corner = lax.rem(self.beside + 2, SIDE)

    def block(self, far, at):
        return self.part((self.across if far else self.row) * SIDE + at)

    def side(self, far, at):
        row = self.corner if far else self.beside
        return remote(
            self.part(row * SIDE + at),
            self.from_beside.at[far, at],
            self.sems.at[self.SIDE_SEND + 4 * far + at],
            self.sems.at[self.SIDE_RECV + 4 * far + at],
            row=self.beside,
            col=self.col,
        )

    def over(self, at):
        return remote(
            self.block(1, at),
            self.from_across.at[at],
            self.sems.at[self.OVER_SEND + at],
            self.sems.at[self.OVER_RECV + at],
            row=self.across,
            col=self.col,
        )

    def line(self, at, toward):
        place = at if toward > 0 else SIDE + at
        return remote(
            self.block(0, at),
            self.from_line.at[place],
            self.sems.at[self.LINE_SEND + at],
            self.sems.at[self.LINE_RECV + place],
            row=self.row,
            col=self.col + toward,
        )

    def add(self, far, at, other):
        block = self.block(far, at)
        block[...] = (block[...].astype(f32) + other[...].astype(f32)).astype(bf16)

    def start(self):
        for far in (1, 0):
            for at in ORDER:
                self.side(far, at).start()

    def fold_side(self, far):
        for at in ORDER:
            self.side(far, at).wait_recv()
            self.add(far, at, self.from_beside.at[far, at])
            if far:
                self.over(at).start()

    def fold_line(self, at):
        self.over(at).wait_recv()
        self.add(0, at, self.from_across.at[at])

        @pl.when(at > self.col)
        def _():
            @pl.when(self.col > 0)
            def _():
                self.line(at, 1).wait_recv()
                self.add(0, at, self.from_line.at[at])

            self.line(at, 1).start()

        @pl.when(at < self.col)
        def _():
            @pl.when(self.col < SIDE - 1)
            def _():
                self.line(at, -1).wait_recv()
                self.add(0, at, self.from_line.at[SIDE + at])

            self.line(at, -1).start()

    def land(self):
        @pl.when(self.col > 0)
        def _():
            self.line(self.col, 1).wait_recv()
            self.add(0, self.col, self.from_line.at[self.col])

        @pl.when(self.col < SIDE - 1)
        def _():
            self.line(self.col, -1).wait_recv()
            self.add(0, self.col, self.from_line.at[SIDE + self.col])

    def result(self):
        return self.block(0, self.col)[...]

    def finish(self):
        for far in range(2):
            for at in range(SIDE):
                self.side(far, at).wait_send()
        for at in range(SIDE):
            self.over(at).wait_send()

            @pl.when(at > self.col)
            def _(at=at):
                self.line(at, 1).wait_send()

            @pl.when(at < self.col)
            def _(at=at):
                self.line(at, -1).wait_send()


def rows_of(index):
    return pl.ds(pl.multiple_of(index * ROWS, 8), ROWS)


BLOCK_ORDER = ('y1', 'p0', 'f1', 'pr1', 'c0', 'h1', 'px0', 'spot0', 'pr2', 'j1', 'f1', 'cx0', 'cr1', 'pr3', 'px1', 'px2', 'y1', 'px3', 'pf0', 'asm0', 'image1', 'f1', 'b0', 'cr2', 'clear0', 'image0', 'h1', 'f1', 'cx1', 'a0', 'cx2', 'br1', 'cr3', 'own0', 'f1', 'pick0', 'h1', 'bx0', 'ar1', 'cx3', 'bx1', 'h1', 'br2', 'h1', 'y1', 'ar2', 'br3', 'f1', 'pick1', 'bx2', 'ax0', 'ar3', 'j1', 'cf0', 'j1', 'ax1', 'f1', 'y1', 'takeg1', 'cs0', 'ax2', 'y1', 'bx3', 'h1', 'bf0', 'takex1', 'takeg0', 'ax3', 'af0', 'y1', 'gate0', 'h1', 'gate1', 'j2', 'y1', 'takex0', 'bs0', 'mine0', 'sent0', 'ex0', 'y1', 'j2', 'other0', 'ex2', 'j1', 'swap0', 'ps0', 'sent1', 'ex1', 'g1', 'as0', 'other1', 'ex3', 'g2', 'putg1', '1b0', '1f0', 'g1', 'gates0', 'putg0', 'g2', 'swap1', 'g1', '0b0', '0f0', 'k1', '1n0', 'putx1', '3b0', '1l3', '0n0', '0l3', '1l2', '1l0', 'k1', '3n0', '0l2', 'putx0', '2b0', '2n0', '3f0', 'k1', '0l0', '1l1', '0l1', 'wait0', '3l2', 'unimage1', 'k1', 'g1', '2f0', 'unimage0', 'small0', '3l0', 'sf0', '2l0', '3l3', 'sn0', 'out0', 'out1', '2l3', '3l1', 'sl3', 'k1', 'sl2', '2l2', 'k1', 'sl0', 'sl1', '2l1', 'k2', 'done0', 'sums0', 'done1')


def block_kernel(
    paired,
    x_in,
    dy_in,
    project_in,
    project_out,
    router_weight,
    gain_one,
    bias_one,
    gain_two,
    bias_two,
    eup_ref,
    edown_ref,
    routes_in,
    block_out,
    input_grad,
    small_out,
    up_out,
    down_out,
    x_ref,
    dy_ref,
    pack_ref,
    flat_routes,
    places,
    routes_ref,
    packs,
    w_in,
    w_out,
    w_route,
    vecs,
    normed_one,
    triple,
    mixed,
    hidden,
    normed_two,
    x_all,
    dy_all,
    up_ref,
    down_ref,
    pick,
    logit,
    gate_rows,
    own_gate,
    spots,
    slot_gate,
    slot_x,
    slot_g,
    out_sum,
    back_sum,
    gate_sum,
    gate_out,
    gate_part,
    gate_in,
    beside,
    across,
    line,
    small_part,
    small_beside,
    small_across,
    small_line,
    small_pair,
    weight_in,
    weight_out,
    route_sum,
    vec_sum,
    grad_hidden,
    grad_triple,
    theirs,
    spread_sems,
    fetch_send,
    fetch_recv,
    pass_send,
    pass_recv,
    keep_sems,
    fold_sems,
    gate_send,
    gate_recv,
    swap_send,
    swap_recv,
    give_send,
    give_recv,
    retain_sems,
    pair_sems,
):
    row, col, across_row, beside_row = position()
    corner_row = lax.rem(beside_row + 2, SIDE)
    rank = row * SIDE + col
    half = lax.axis_index("dp") if paired else None
    partner = 1 - half if paired else None

    greet(partner)
    for source, target in ((x_in, x_ref), (dy_in, dy_ref)):
        target[...] = jnp.zeros_like(target)
        for m in range(2):
            target[m, :SEQ, :] = source[:, m, :]
    pack_ref[:PART, :288] = project_in[...]
    pack_ref[:PART, 288:] = project_out[...]
    pack_ref[PART:, :] = jnp.zeros((PACK - PART, D), bf16)
    vectors = [v[...].astype(f32) for v in (gain_one, bias_one, gain_two, bias_two)]
    tail = jnp.concatenate(
        [router_weight[...].astype(f32)] + vectors + [jnp.zeros((4, PART), f32)], axis=0
    )
    pack_ref[PART:, :PART] = tail.astype(bf16)
    meet(partner)

    def load_routes():
        flat_routes[...] = jnp.full_like(flat_routes, -1)
        for index in range(SHARES):
            for m in range(2):
                flat_routes[TOP * m : TOP * (m + 1), index * ROWS : index * ROWS + SEQ] = routes_in[
                    m, :, index * SEQ : (index + 1) * SEQ
                ]
        places[...] = jnp.full_like(places, -1)

        @pl.loop(0, CHUNKS)
        def _(i):
            lanes = pl.ds(pl.multiple_of(i * LANES, LANES), LANES)
            for pair in range(2 * TOP):
                places[pair // TOP, pair % TOP, pl.ds(i, 1), :] = flat_routes[
                    pair : pair + 1, lanes
                ]

        own = flat_routes[:, :ROWS]
        for index in range(1, SHARES):
            own = jnp.where(rank == index, flat_routes[:, index * ROWS : (index + 1) * ROWS], own)
        routes_ref[...] = jnp.transpose(own.astype(f32))

    low = half_lanes(2 * HEAD)
    tokens = [
        Spread(
            normed_two.at[m],
            lambda r, c, m=m: x_all.at[m, rows_of(r * SIDE + c)],
            spread_sems.at[2 + m],
        )
        for m in range(2)
    ]
    spreads = {
        "p": Spread(pack_ref, lambda r, c: packs.at[r * SIDE + c], spread_sems.at[0]),
        "c": Spread(dy_ref, lambda r, c: dy_all.at[:, rows_of(r * SIDE + c)], spread_sems.at[1]),
        "a": tokens[0],
        "b": tokens[1],
    }

    def assemble():
        for r in range(SIDE):
            for c in range(SIDE):
                at = r * SIDE + c
                w_in[c * PART : (c + 1) * PART, r * 288 : (r + 1) * 288] = packs[at, :PART, :288]
                w_out[r * PART : (r + 1) * PART, c * PART : (c + 1) * PART] = packs[at, :PART, 288:]
                tail = packs[at, PART:, :PART].astype(f32)
                w_route[r * 8 : (r + 1) * 8, c * PART : (c + 1) * PART] = tail[:8]
                if r == 0:
                    vecs[:, c * PART : (c + 1) * PART] = tail[8:]

    def attend(m):
        stream = x_ref[m].astype(f32)
        normal, _ = normalize(stream)
        first = (normal * vecs[0:1] + vecs[1:2]).astype(bf16)
        normed_one[m] = first
        triple[m] = dot(first, w_in[...], ((1,), (0,))).astype(bf16)
        for pair in range(HEADS // 2):
            lanes = 2 * HEAD * pair
            queries = triple[m, :, lanes : lanes + 128]
            keys = triple[m, :, D + lanes : D + lanes + 128]
            values = triple[m, :, 2 * D + lanes : 2 * D + lanes + 128]
            parts = []
            for which in range(2):
                prob = softmax_rows(queries, one_half(keys, low, which)).astype(bf16)
                parts.append(dot(prob, values, ((1,), (0,))))
            mixed[m, :, lanes : lanes + 128] = jnp.where(low, parts[0], parts[1]).astype(bf16)
        after = stream + dot(mixed[m], w_out[...], ((1,), (0,)))
        hidden[m] = after
        normal, _ = normalize(after)
        normed_two[m] = (normal * vecs[2:3] + vecs[3:4]).astype(bf16)

    mats = ((eup_ref, up_ref), (edown_ref, down_ref))
    shares = (half,) if paired else (0, 1)

    def into(whole, own, owner):
        return whole.at[own, owner // SIDE, pl.ds(lax.rem(owner, SIDE) * PART, PART), :]

    def fetch(number, mat, own, step):
        blocks, whole = mats[mat]
        to, _ = peer(step)
        return remote(
            blocks.at[own * SHARES + to],
            into(whole, own, rank),
            fetch_send.at[number, mat, step],
            fetch_recv.at[number, mat, step],
            row=to // SIDE,
            col=lax.rem(to, SIDE),
        )

    def arrival(number, mat, own, step):
        _, source = peer(step)
        block = into(mats[mat][1], own, source)
        return remote(
            block,
            block,
            fetch_send.at[number, mat, step],
            fetch_recv.at[number, mat, step],
            row=source // SIDE,
            col=lax.rem(source, SIDE),
        )

    def hand(mat, step):
        blocks, whole = mats[mat]
        _, source = peer(step)
        block = into(whole, half, source)
        src = blocks.at[half * SHARES + rank] if isinstance(step, int) else block
        return remote(src, block, pass_send.at[mat, step], pass_recv.at[mat, step], dp=partner)

    def keep(number, mat, own):
        blocks, whole = mats[mat]
        return pltpu.make_async_copy(
            blocks.at[own * SHARES + rank], into(whole, own, rank), keep_sems.at[number, mat]
        )

    def begin_fetch():
        for number, own in enumerate(shares):
            for mat in range(2):
                keep(number, mat, own).start()
                if paired:
                    hand(mat, 0).start()

    def fetch_some(first, last):
        for number, own in enumerate(shares):

            @pl.loop(first, last)
            def _(step):
                for mat in range(2):
                    fetch(number, mat, own, step).start()

    def pass_some(first, last):
        for number, own in enumerate(shares):

            @pl.loop(first, last)
            def _(step):
                for mat in range(2):
                    arrival(number, mat, own, step).wait_recv()
                    if paired:
                        hand(mat, step).start()

    def have_own():
        for number, own in enumerate(shares):
            for mat in range(2):
                keep(number, mat, own).wait()

    def side_steps(number):
        return (number * SHARES // 2, (number + 1) * SHARES // 2)

    def have_other(number):
        if paired:

            @pl.loop(*side_steps(number))
            def _(step):
                for mat in range(2):
                    hand(mat, step).wait_recv()

    def handed(number):
        if paired:

            @pl.loop(*side_steps(number))
            def _(step):
                for mat in range(2):
                    hand(mat, step).wait_send()

    slot_place = lax.broadcasted_iota(jnp.int32, (SLOTS, LANES), 0).astype(f32)
    names = lax.broadcasted_iota(jnp.int32, (32, LANES), 0)

    def own_routes(m, q):
        mine = rank + SHARES * q
        return (places[m, 0] == mine, places[m, 1] == mine)

    def find_spots():
        load_routes()
        down_lane = lax.broadcasted_iota(jnp.int32, (LANES, LANES), 0)
        lane = lax.broadcasted_iota(jnp.int32, (LANES, LANES), 1)
        upper = jnp.where(down_lane <= lane, 1.0, 0.0).astype(bf16)
        below = lax.broadcasted_iota(jnp.int32, (32, 32), 0)
        above = lax.broadcasted_iota(jnp.int32, (32, 32), 1)
        earlier = jnp.where(below > above, 1.0, 0.0).astype(bf16)
        ones = jnp.ones((LANES, LANES), bf16)
        for m in range(2):
            for q in range(OWN):
                one, two = own_routes(m, q)
                routed = jnp.where(one | two, 1.0, 0.0).astype(bf16)
                within = dot(routed, upper, ((1,), (0,)))
                per_row = dot(routed, ones, ((1,), (0,))).astype(bf16)
                before = dot(earlier, per_row, ((1,), (0,)))
                spots[m, q] = jnp.where(one | two, within + before - 1.0, -1.0)

    def make_pick(m):
        @pl.loop(0, CHUNKS)
        def _(i):
            lanes = pl.ds(pl.multiple_of(i * LANES, LANES), LANES)
            for q in range(OWN):
                hit = spots[m, q, pl.ds(i, 1), :] == slot_place
                pick[m, q * SLOTS : (q + 1) * SLOTS, lanes] = jnp.where(hit, 1.0, 0.0).astype(bf16)

    def take(source, target, m):
        found = dot(pick[m], source[m], ((1,), (0,))).astype(bf16)
        for q in range(OWN):
            target[q, m * SLOTS : (m + 1) * SLOTS, :] = found[q * SLOTS : (q + 1) * SLOTS]

    def make_gates(m):
        logit[...] = dot(w_route[...].astype(bf16), x_all[m], ((1,), (1,)))
        for k in range(TOP):
            gate_rows[k] = jnp.zeros((32, LANES), f32)

        @pl.loop(0, CHUNKS)
        def _(i):
            piece = logit[:, pl.ds(pl.multiple_of(i * LANES, LANES), LANES)]
            for k in range(TOP):
                chosen = places[m, k, pl.ds(i, 1), :] == names
                gate_rows[k, pl.ds(i, 1), :] = jnp.sum(
                    jnp.where(chosen, piece, 0.0), axis=0, keepdims=True
                )

        first, second = gate_rows[0], gate_rows[1]
        top = jnp.maximum(first, second)
        first, second = jnp.exp(first - top), jnp.exp(second - top)
        total = first + second
        first, second = first / total, second / total
        rows = slice(m * SLOTS, (m + 1) * SLOTS)
        for q in range(OWN):
            one, two = own_routes(m, q)
            own_gate[q] = jnp.where(one, first, jnp.where(two, second, 0.0))
            slot_gate[q, rows, :] = jnp.zeros((SLOTS, LANES), f32)

        @pl.loop(0, CHUNKS)
        def _(i):
            for q in range(OWN):
                hit = spots[m, q, pl.ds(i, 1), :] == slot_place
                slot_gate[q, rows, :] += jnp.where(hit, own_gate[q, pl.ds(i, 1), :], 0.0)

        for q in range(OWN):
            slot_gate[q, rows, :] = jnp.broadcast_to(
                jnp.sum(slot_gate[q, rows, :], axis=1, keepdims=True), (SLOTS, LANES)
            )

    def expert(q, number):
        if number == 0:
            out_sum[q] = jnp.zeros((2 * SLOTS, D), f32)
            back_sum[q] = jnp.zeros((2 * SLOTS, D), f32)
            gate_sum[q] = jnp.zeros((2 * SLOTS, LANES), f32)
        near, far = ((row, beside_row), (across_row, corner_row))[number]

        @pl.loop(0, 2)
        def _(turn):
            f = jnp.where(turn == 0, near, far)
            inputs, cots = slot_x[q], slot_g[q]
            up, down = up_ref[q, f], down_ref[q, f]
            pre = dot(inputs, up, ((1,), (0,)))
            grad = dot(cots, down, ((1,), (0,)))
            cdf = 0.5 * (1.0 + lax.erf(pre * sqrt_half))
            act = pre * cdf
            gate = slot_gate[q][:, :1]
            scaled = (gate * act).astype(bf16)
            gate_sum[q] += jnp.broadcast_to(
                jnp.sum(grad * act, axis=1, keepdims=True), (2 * SLOTS, LANES)
            )
            slope = cdf + pre * jnp.exp(-0.5 * pre * pre) * inv_root_tau
            grad_pre = (gate * grad * slope).astype(bf16)
            out_sum[q] += dot(scaled, down, ((1,), (1,)))
            back_sum[q] += dot(grad_pre, up, ((1,), (1,)))
            up_ref[q, f] = dot(inputs, grad_pre, ((0,), (0,))).astype(bf16)
            down_ref[q, f] = dot(cots, scaled, ((0,), (0,))).astype(bf16)

        if number == 1:
            slot_x[q] = out_sum[q].astype(bf16)
            slot_g[q] = back_sum[q].astype(bf16)

    def put(source, target, m):
        rows = slice(m * SLOTS, (m + 1) * SLOTS)
        stacked = jnp.concatenate([source[0, rows, :], source[1, rows, :]], axis=0)

        @pl.loop(0, CHUNKS // 5)
        def _(i):
            there = pl.ds(pl.multiple_of(i * 5 * LANES, 5 * LANES), 5 * LANES)
            target[m, there, :] = dot(pick[m, :, there], stacked, ((0,), (0,))).astype(bf16)

    def gate_back():
        gate_part[...] = jnp.zeros_like(gate_part)
        for m in range(2):
            rows = slice(m * SLOTS, (m + 1) * SLOTS)
            for k in range(TOP):
                gate_out[m, k] = jnp.zeros((32, LANES), f32)

            @pl.loop(0, CHUNKS)
            def _(i):
                for q in range(OWN):
                    hit = spots[m, q, pl.ds(i, 1), :] == slot_place
                    found = jnp.sum(
                        jnp.where(hit, gate_sum[q, rows, :], 0.0), axis=0, keepdims=True
                    )
                    for k in range(TOP):
                        here = places[m, k, pl.ds(i, 1), :] == rank + SHARES * q
                        gate_out[m, k, pl.ds(i, 1), :] += jnp.where(here, found, 0.0)

            for to in range(SHARES):
                first = to * ROWS // LANES
                shift = to * ROWS - first * LANES
                span = -(-(shift + ROWS) // LANES)
                for k in range(TOP):
                    wide = jnp.concatenate(
                        [gate_out[m, k, first + n : first + n + 1, :] for n in range(span)], axis=1
                    )
                    gate_part[to, 2 * m + k : 2 * m + k + 1, :ROWS] = wide[:, shift : shift + ROWS]

    def gate_copy(step):
        to, _ = peer(step)
        return remote(
            gate_part.at[to],
            gate_in.at[rank],
            gate_send.at[step],
            gate_recv.at[step],
            row=to // SIDE,
            col=lax.rem(to, SIDE),
        )

    def gate_wait(step):
        _, source = peer(step)
        return remote(
            gate_part.at[rank],
            gate_in.at[source],
            gate_send.at[step],
            gate_recv.at[step],
            row=source // SIDE,
            col=lax.rem(source, SIDE),
        )

    def start_gates():
        gate_back()
        gate_in[rank] = gate_part[rank]

        @pl.loop(1, SHARES)
        def _(step):
            gate_copy(step).start()

    def wait_gates():
        @pl.loop(1, SHARES)
        def _(step):
            gate_wait(step).wait_recv()

    folds = [
        Fold(
            lambda index, n=n: (dy_all if n < 2 else x_all).at[n % 2, rows_of(index)],
            beside.at[n],
            across.at[n],
            line.at[n],
            fold_sems.at[n],
        )
        for n in range(4)
    ]
    small = Fold(
        lambda index: small_part.at[index], small_beside, small_across, small_line, fold_sems.at[4]
    )

    givers = ((up_ref, up_out), (down_ref, down_out))

    def swap(mat, step):
        to, _ = peer(step)
        return remote(
            into(givers[mat][0], partner, to),
            theirs.at[step, mat],
            swap_send.at[step, mat],
            swap_recv.at[step, mat],
            dp=partner,
        )

    def give(number, mat, q, step):
        to, _ = peer(step)
        return remote(
            into(givers[mat][0], q, to),
            givers[mat][1].at[rank if paired else q * SHARES + rank],
            give_send.at[number, mat, step],
            give_recv.at[number, mat, step],
            row=to // SIDE,
            col=lax.rem(to, SIDE),
        )

    def given(number, mat, q, step):
        _, source = peer(step)
        block = givers[mat][1].at[source if paired else q * SHARES + source]
        return remote(
            block,
            block,
            give_send.at[number, mat, step],
            give_recv.at[number, mat, step],
            row=source // SIDE,
            col=lax.rem(source, SIDE),
        )

    def retain(number, mat, q):
        return pltpu.make_async_copy(
            into(givers[mat][0], q, rank),
            givers[mat][1].at[rank if paired else q * SHARES + rank],
            retain_sems.at[number, mat],
        )

    def start_swap(number):
        if paired:

            @pl.loop(*side_steps(number))
            def _(step):
                for mat in range(2):
                    swap(mat, step).start()

    def give_some(first, last):
        for number, q in enumerate(shares):

            @pl.loop(first, last)
            def _(step):
                for mat in range(2):
                    if paired:
                        swap(mat, step).wait_recv()
                        to, _ = peer(step)
                        block = into(givers[mat][0], half, to)
                        block[...] = (
                            block[...].astype(f32) + theirs[step, mat].astype(f32)
                        ).astype(bf16)

                    @pl.when(step > 0)
                    def _():
                        give(number, mat, q, step).start()

                    @pl.when(step == 0)
                    def _():
                        retain(number, mat, q).start()

    token_names = lax.broadcasted_iota(jnp.int32, (ROWS, 32), 1).astype(f32)
    exact = lax.Precision.HIGHEST

    def clear_sums():
        weight_in[...] = jnp.zeros_like(weight_in)
        weight_out[...] = jnp.zeros_like(weight_out)
        route_sum[...] = jnp.zeros_like(route_sum)
        vec_sum[...] = jnp.zeros_like(vec_sum)

    def norm_back(grad_out, normal, inverse, which):
        scaled = grad_out * vecs[which : which + 1]
        vec_sum[which : which + 1] += jnp.sum(grad_out * normal, axis=0, keepdims=True)
        vec_sum[which + 1 : which + 2] += jnp.sum(grad_out, axis=0, keepdims=True)
        return inverse * (
            scaled
            - jnp.mean(scaled, axis=-1, keepdims=True)
            - normal * jnp.mean(scaled * normal, axis=-1, keepdims=True)
        )

    def attend_back(m):
        folds[m].land()
        grad_norm = folds[m].result().astype(f32)
        router = w_route[...]
        logits = dot(normed_two[m], router.astype(bf16), ((1,), (1,)))
        hits = [
            routes_ref[:, TOP * m + k : TOP * m + k + 1] == token_names for k in range(TOP)
        ]
        picked = [jnp.sum(jnp.where(hit, logits, 0.0), axis=1, keepdims=True) for hit in hits]
        top = jnp.maximum(picked[0], picked[1])
        grown = [jnp.exp(v - top) for v in picked]
        total = grown[0] + grown[1]
        gates = [v / total for v in grown]
        columns = jnp.transpose(jnp.sum(gate_in[...], axis=0))[:ROWS]
        grads = [columns[:, 2 * m + k : 2 * m + k + 1] for k in range(TOP)]
        mean_grad = gates[0] * grads[0] + gates[1] * grads[1]
        dense = jnp.zeros((ROWS, 32), f32)
        for k in range(TOP):
            dense = dense + jnp.where(hits[k], gates[k] * (grads[k] - mean_grad), 0.0)
        route_sum[...] += lax.dot_general(
            dense,
            normed_two[m].astype(f32),
            (((0,), (0,)), ((), ())),
            preferred_element_type=f32,
            precision=exact,
        )
        grad_norm = grad_norm + lax.dot_general(
            dense, router, (((1,), (0,)), ((), ())), preferred_element_type=f32, precision=exact
        )
        normal, inverse = normalize(hidden[m])
        into_hidden = dy_ref[m].astype(f32) + norm_back(grad_norm, normal, inverse, 2)
        grad_hidden[m] = into_hidden
        grad_attn = into_hidden.astype(bf16)
        weight_out[...] += dot(mixed[m], grad_attn, ((0,), (0,)))
        grad_mixed = dot(grad_attn, w_out[...], ((1,), (1,))).astype(bf16)
        grad_triple[m, :, :D] = grad_mixed

        @pl.loop(0, HEADS // 2)
        def _(pair):
            def lanes(n):
                return pl.ds(pl.multiple_of(n * D + pair * 128, 128), 128)

            queries, keys, values = (triple[m, :, lanes(n)] for n in range(3))
            cots = grad_triple[m, :, lanes(0)]
            parts = []
            for which in range(2):
                prob = softmax_rows(queries, one_half(keys, low, which))
                weights = prob.astype(bf16)
                grad_prob = dot(cots, one_half(values, low, which), ((1,), (1,)))
                grad_scores = prob * (
                    grad_prob - jnp.sum(prob * grad_prob, axis=-1, keepdims=True)
                )
                grad_scores = grad_scores.astype(bf16)
                parts.append(
                    (
                        dot(grad_scores, keys, ((1,), (0,))) * HEAD ** (-0.5),
                        dot(grad_scores, queries, ((0,), (0,))) * HEAD ** (-0.5),
                        dot(weights, cots, ((0,), (0,))),
                    )
                )
            for n in range(3):
                grad_triple[m, :, lanes(n)] = jnp.where(
                    low, parts[0][n], parts[1][n]
                ).astype(bf16)

        weight_in[...] += dot(normed_one[m], grad_triple[m], ((0,), (0,)))
        grad_norm = dot(grad_triple[m], w_in[...], ((1,), (1,)))
        normal, inverse = normalize(x_ref[m].astype(f32))
        grad_hidden[m] += norm_back(grad_norm, normal, inverse, 0)

    def write_grad(m):
        input_grad[:, m, :] = grad_hidden[m][:SEQ]

    def gather_small():
        for r in range(SIDE):
            for c in range(SIDE):
                at = r * SIDE + c
                small_part[at, :PART, :288] = weight_in[
                    c * PART : (c + 1) * PART, r * 288 : (r + 1) * 288
                ].astype(bf16)
                small_part[at, :PART, 288:] = weight_out[
                    r * PART : (r + 1) * PART, c * PART : (c + 1) * PART
                ].astype(bf16)
                tail = jnp.concatenate([route_sum[r * 8 : (r + 1) * 8, :], vec_sum[...]], axis=0)
                small_part[at, PART:, :PART] = tail[:, c * PART : (c + 1) * PART].astype(bf16)
                small_part[at, PART:, PART:] = jnp.zeros((16, D - PART), bf16)

    pair = None
    if paired:
        pair = remote(
            small_pair.at[0], small_pair.at[1], pair_sems.at[0], pair_sems.at[1], dp=partner
        )

    def end_small():
        small.land()
        if paired:
            small_pair[0] = small.result()
            pair.start()

    def finish_small():
        if paired:
            pair.wait_recv()
            small_out[...] = small.result().astype(f32) + small_pair[1].astype(f32)
            pair.wait_send()
        else:
            small_out[...] = small.result().astype(f32)

    def finish_branch(m):
        folds[2 + m].land()
        block_out[m] = (hidden[m] + folds[2 + m].result().astype(f32)).astype(bf16)[:SEQ]

    limits = {"f": SHARES // 2, "y": SHARES, "h": SHARES // 2, "j": SHARES, "g": SHARES // 2, "k": SHARES}
    at = {"f": 1, "y": SHARES // 2, "h": 1, "j": SHARES // 2, "g": 0, "k": SHARES // 2}
    ranged = {
        "f": fetch_some,
        "y": fetch_some,
        "h": pass_some,
        "j": pass_some,
        "g": give_some,
        "k": give_some,
    }
    plain = {
        "own": begin_fetch,
        "asm": assemble,
        "spot": find_spots,
        "mine": have_own,
        "gates": start_gates,
        "wait": wait_gates,
        "clear": clear_sums,
        "sums": end_small,
    }
    numbered = {
        "other": have_other,
        "sent": handed,
        "swap": start_swap,
        "image": attend,
        "pick": make_pick,
        "gate": make_gates,
        "takex": lambda m: take(x_all, slot_x, m),
        "takeg": lambda m: take(dy_all, slot_g, m),
        "putx": lambda m: put(slot_x, x_all, m),
        "putg": lambda m: put(slot_g, dy_all, m),
        "unimage": attend_back,
        "out": write_grad,
        "done": finish_branch,
    }
    for step in BLOCK_ORDER:
        name, number = step[:-1], int(step[-1], 16)
        if name in ranged:
            last = min(at[name] + number, limits[name])
            ranged[name](at[name], last)
            at[name] = last
        elif name in plain:
            plain[name]()
        elif name in numbered:
            numbered[name](number)
        elif name == "ex":
            expert(number // 2 if half is None else (half, partner)[number // 2], number % 2)
        elif name == "small":
            gather_small()
            small.start()
        elif name[0] in spreads:
            act = spreads[name[0]]
            if name[1:] == "":
                act.start()
            elif name[1:] == "r":
                act.relay(number)
            elif name[1:] == "x":
                act.cross(number)
            elif name[1:] == "f":
                act.landed()
            elif name[1:] == "s":
                act.finish()
        else:
            fold = small if name[0] == "s" else folds[int(name[0])]
            if name[1:] == "b":
                fold.start()
            elif name[1:] == "f":
                fold.fold_side(1)
            elif name[1:] == "n":
                fold.fold_side(0)
            else:
                fold.fold_line(number)
    finish_small()

    for fold in folds:
        fold.finish()
    small.finish()

    @pl.loop(1, SHARES)
    def _(step):
        gate_copy(step).wait_send()

    for number, q in enumerate(shares):
        for mat in range(2):
            retain(number, mat, q).wait()

        @pl.loop(1, SHARES)
        def _(step):
            for mat in range(2):
                fetch(number, mat, q, step).wait_send()

        for mat in range(2):

            @pl.loop(1, SHARES)
            def _(step):
                given(number, mat, q, step).wait_recv()
                give(number, mat, q, step).wait_send()

    if paired:

        @pl.loop(0, SHARES)
        def _(step):
            for mat in range(2):
                swap(mat, step).wait_send()


def block_call(paired, *operands):
    block, small = (ROWS, D), (PACK, D)
    experts = SHARES if paired else OWN * SHARES
    numbers = 1 if paired else 2
    outputs = [
        ((2, SEQ, D), bf16, VMEM),
        ((SEQ, 2, D), f32, VMEM),
        (small, f32, VMEM),
        ((experts, PART, FPART), bf16, ANY),
        ((experts, PART, FPART), bf16, ANY),
    ]
    scratch = [
        ((2,) + block, bf16),
        ((2,) + block, bf16),
        (small, bf16),
        ((8, TOKENS), jnp.int32),
        ((2, TOP, 32, LANES), jnp.int32),
        ((ROWS, 8), f32),
        ((SHARES,) + small, bf16),
        ((D, WIDE), bf16),
        ((D, D), bf16),
        ((32, D), f32),
        ((8, D), f32),
        ((2,) + block, bf16),
        ((2, ROWS, WIDE), bf16),
        ((2,) + block, bf16),
        ((2,) + block, f32),
        ((2,) + block, bf16),
        ((2, TOKENS, D), bf16),
        ((2, TOKENS, D), bf16),
        ((OWN, SIDE, D, FPART), bf16),
        ((OWN, SIDE, D, FPART), bf16),
        ((2, OWN * SLOTS, TOKENS), bf16),
        ((32, TOKENS), f32),
        ((TOP, 32, LANES), f32),
        ((OWN, 32, LANES), f32),
        ((2, OWN, 32, LANES), f32),
        ((OWN, 2 * SLOTS, LANES), f32),
        ((OWN, 2 * SLOTS, D), bf16),
        ((OWN, 2 * SLOTS, D), bf16),
        ((OWN, 2 * SLOTS, D), f32),
        ((OWN, 2 * SLOTS, D), f32),
        ((OWN, 2 * SLOTS, LANES), f32),
        ((2, TOP, 32, LANES), f32),
        ((SHARES, 8, 256), f32),
        ((SHARES, 8, 256), f32),
        ((4, 2, SIDE) + block, bf16),
        ((4, SIDE) + block, bf16),
        ((4, 2 * SIDE) + block, bf16),
        ((SHARES,) + small, bf16),
        ((2, SIDE) + small, bf16),
        ((SIDE,) + small, bf16),
        ((2 * SIDE,) + small, bf16),
        ((2,) + small, bf16),
        ((D, WIDE), f32),
        ((D, D), f32),
        ((32, D), f32),
        ((8, D), f32),
        ((2,) + block, f32),
        ((2, ROWS, WIDE), bf16),
        ((SHARES, 2, PART, FPART) if paired else (1, 2, 16, LANES), bf16),
    ]
    semaphores = [
        (4, Spread.COUNT),
        (numbers, 2, SHARES),
        (numbers, 2, SHARES),
        (2, SHARES),
        (2, SHARES),
        (numbers, 2),
        (5, Fold.COUNT),
        (SHARES,),
        (SHARES,),
        (SHARES, 2),
        (SHARES, 2),
        (numbers, 2, SHARES),
        (numbers, 2, SHARES),
        (numbers, 2),
        (2,),
    ]
    return pl.pallas_call(
        functools.partial(block_kernel, paired),
        out_shape=[jax.ShapeDtypeStruct(shape, kind) for shape, kind, _ in outputs],
        in_specs=[VMEM] * 9 + [ANY, ANY, VMEM],
        out_specs=[space for _, _, space in outputs],
        scratch_shapes=[pltpu.VMEM(shape, kind) for shape, kind in scratch]
        + [DMA(shape) for shape in semaphores],
        compiler_params=pltpu.CompilerParams(
            collective_id=0, has_side_effects=True, vmem_limit_bytes=63 << 20
        ),
        name="block",
    )(*operands)


def final_kernel(
    output, grad, small, up, down, output_rows, grad_rows, g_in, g_out, *rest
):
    *g_vecs, g_router, g_up, g_down = rest
    g_up[...] = up[...].astype(f32)
    g_down[...] = down[...].astype(f32)

    step = pl.program_id(0)
    for m in range(2):

        @pl.when(step == m)
        def _(m=m):
            output_rows[:, m, :] = output[m]

    @pl.when(step == 2)
    def _():
        grad_rows[...] = grad[...]

    @pl.when(step == 0)
    def _():
        g_in[...] = small[:PART, :288]
        g_out[...] = small[:PART, 288:]
        g_router[...] = small[PART : PART + 8, :PART]
        for n in range(4):
            g_vecs[n][...] = small[PART + 8 + n : PART + 9 + n, :PART]


def final_call(output, grad, small, up, down):
    steps = 4
    rows = up.shape[0] * PART // steps
    shape = up.shape
    up, down = (v.reshape(-1, FPART) for v in (up, down))
    blocks = pl.BlockSpec((rows, FPART), lambda i: (i, 0))

    def whole(*shape):
        return pl.BlockSpec(shape, lambda i: (0,) * len(shape))

    sizes = [
        ((SEQ, 2, D), bf16),
        ((SEQ, 2, D), f32),
        ((PART, 288), f32),
        ((PART, PART), f32),
        ((1, PART), f32),
        ((1, PART), f32),
        ((1, PART), f32),
        ((1, PART), f32),
        ((8, PART), f32),
        (up.shape, f32),
        (up.shape, f32),
    ]
    *rest, g_up, g_down = pl.pallas_call(
        final_kernel,
        grid=(steps,),
        out_shape=[jax.ShapeDtypeStruct(shape, kind) for shape, kind in sizes],
        in_specs=[whole(2, SEQ, D), whole(SEQ, 2, D), whole(PACK, D), blocks, blocks],
        out_specs=[whole(*shape) for shape, _ in sizes[:9]] + [blocks, blocks],
        name="final",
    )(output, grad, small, up, down)
    return (*rest, g_up.reshape(shape), g_down.reshape(shape))


def on_device(
    block_input,
    first_gain,
    first_bias,
    project_in,
    project_out,
    second_gain,
    second_bias,
    router_weight,
    expert_up,
    expert_down,
    routes,
    out_grad,
):
    paired = lax.axis_size("dp") == 2
    block_output, input_grad, small, up_sum, down_sum = block_call(
        paired,
        block_input.transpose(1, 0, 2),
        out_grad.transpose(1, 0, 2),
        project_in,
        project_out,
        router_weight.T,
        first_gain[None],
        first_bias[None],
        second_gain[None],
        second_bias[None],
        expert_up,
        expert_down,
        routes.transpose(0, 2, 1),
    )
    if not paired:
        small = lax.psum(small, "dp")
        up_sum = lax.psum_scatter(up_sum, "dp", scatter_dimension=0, tiled=True)
        down_sum = lax.psum_scatter(down_sum, "dp", scatter_dimension=0, tiled=True)
    output, grad, g_in, g_out, *g_vecs, g_router, g_up, g_down = final_call(
        block_output, input_grad, small, up_sum, down_sum
    )
    return (
        output.transpose(1, 0, 2),
        grad.transpose(1, 0, 2),
        g_vecs[0][0],
        g_vecs[1][0],
        g_in,
        g_out,
        g_vecs[2][0],
        g_vecs[3][0],
        g_router.T,
        g_up,
        g_down,
    )


def solution(mesh):
    in_specs = (
        P(None, ("dp", "row", "col"), None),
        P("col"),
        P("col"),
        P("col", "row"),
        P("row", "col"),
        P("col"),
        P("col"),
        P("col", "row"),
        P(None, "col", "row"),
        P(None, "col", "row"),
        P(None, "dp", None),
        P(None, ("dp", "row", "col"), None),
    )
    out_specs = (
        P(None, ("dp", "row", "col"), None),
        P(None, ("dp", "row", "col"), None),
        P("col"),
        P("col"),
        P("col", "row"),
        P("row", "col"),
        P("col"),
        P("col"),
        P("col", "row"),
        P("dp", "col", "row"),
        P("dp", "col", "row"),
    )
    return jax.shard_map(
        on_device, mesh=mesh, in_specs=in_specs, out_specs=out_specs, check_vma=False
    )
```

```python
import functools

import jax
import jax.numpy as jnp
from jax import lax
from jax.experimental import pallas as pl
from jax.experimental.pallas import tpu as pltpu
from jax.sharding import PartitionSpec as P

D = 384
HEADS = 6
HEAD = 64
TOP = 2
SEQ = 197
ROWS = 200
SLOTS = 256
SIDE = 4
SHARES = SIDE * SIDE
OWN = 2
PART = D // SIDE
WIDE = 3 * D
FPART = 384
PACK = PART + 16

sqrt_half = 0.7071067811865476
inv_root_tau = 0.3989422804014327
bf16 = jnp.bfloat16
f32 = jnp.float32
MESH = pl.DeviceIdType.MESH
ANY = pl.BlockSpec(memory_space=pl.ANY)
TOKENS = SHARES * ROWS
LANES = 128
CHUNKS = TOKENS // LANES
ORDER = (3, 0, 2, 1)
VMEM = pl.BlockSpec(memory_space=pltpu.VMEM)
DMA = pltpu.SemaphoreType.DMA


def dot(left, right, dims):
    return lax.dot_general(left, right, (dims, ((), ())), preferred_element_type=f32)


def position():
    row = lax.axis_index("row")
    col = lax.axis_index("col")
    across = lax.rem(row + 2, SIDE)
    beside = row + 1 - 2 * lax.rem(row, 2)
    return (row, col, across, beside)


def peer(step):
    row, col, across, beside = position()
    group, shift = step // SIDE, lax.rem(step, SIDE)
    other = jnp.where(
        group == 0,
        row,
        jnp.where(group == 1, beside, jnp.where(group == 2, across, lax.rem(beside + 2, SIDE))),
    )
    return (
        other * SIDE + lax.rem(col + shift, SIDE),
        other * SIDE + lax.rem(col + SIDE - shift, SIDE),
    )


def remote(src, dst, send, recv, **target):
    return pltpu.make_async_remote_copy(
        src_ref=src,
        dst_ref=dst,
        send_sem=send,
        recv_sem=recv,
        device_id=target,
        device_id_type=MESH,
    )


def greet(partner):
    row, col, _, _ = position()
    rank = row * SIDE + col
    barrier = pltpu.get_barrier_semaphore()

    @pl.loop(1, SHARES)
    def _(step):
        other = lax.rem(rank + step, SHARES)
        pl.semaphore_signal(
            barrier,
            inc=1,
            device_id={"row": other // SIDE, "col": lax.rem(other, SIDE)},
            device_id_type=MESH,
        )

    if partner is not None:
        pl.semaphore_signal(barrier, inc=1, device_id={"dp": partner}, device_id_type=MESH)


def meet(partner):
    pl.semaphore_wait(
        pltpu.get_barrier_semaphore(), SHARES if partner is not None else SHARES - 1
    )


class Spread:
    UP, DOWN, LINE, ACROSS, CROSSED, BESIDE, PASSED, KEEP = 0, 4, 8, 12, 16, 20, 28, 36
    COUNT = 37

    def __init__(self, source, slot, sems):
        self.source, self.slot, self.sems = source, slot, sems
        self.row, self.col, self.across, self.beside = position()
        self.corner = lax.rem(self.beside + 2, SIDE)

    def hop(self, block, send, recv, src=None, **target):
        src = block if src is None else src
        return remote(src, block, self.sems.at[send], self.sems.at[recv], **target)

    def line(self, row, at, toward, src=None):
        base = self.UP if toward > 0 else self.DOWN
        return self.hop(
            self.slot(row, at), base + at, self.LINE + at, src, row=self.row, col=self.col + toward
        )

    def over(self, at, src=None):
        return self.hop(
            self.slot(self.row, at),
            self.ACROSS + at,
            self.CROSSED + at,
            src,
            row=self.across,
            col=self.col,
        )

    def side(self, row, at, shift, src=None):
        return self.hop(
            self.slot(row, at),
            self.BESIDE + shift + at,
            self.PASSED + shift + at,
            src,
            row=self.beside,
            col=self.col,
        )

    def keep(self):
        return pltpu.make_async_copy(
            self.source, self.slot(self.row, self.col), self.sems.at[self.KEEP]
        )

    def start(self):
        @pl.when(self.col < SIDE - 1)
        def _():
            self.line(self.row, self.col, 1, self.source).start()

        @pl.when(self.col > 0)
        def _():
            self.line(self.row, self.col, -1, self.source).start()

        self.over(self.col, self.source).start()
        self.side(self.row, self.col, 0, self.source).start()
        self.keep().start()

    def each(self, distance, body):
        for sign in (-1, 1):
            at = self.col + sign * distance

            @pl.when((at >= 0) & (at < SIDE))
            def _(at=at, sign=sign):
                body(at, sign)

    def relay(self, distance):
        def body(at, sign):
            self.line(self.row, at, sign).wait_recv()
            onward = self.col - sign

            @pl.when((onward >= 0) & (onward < SIDE))
            def _():
                self.line(self.row, at, -sign).start()

            self.over(at).start()
            self.side(self.row, at, 0).start()

        self.each(distance, body)

    def cross(self, distance):
        def body(at, sign):
            block = self.slot(self.across, at)
            self.hop(
                block, self.ACROSS + at, self.CROSSED + at, row=self.across, col=self.col
            ).wait_recv()
            self.side(self.across, at, SIDE).start()

        if distance == 0:
            body(self.col, 0)
        else:
            self.each(distance, body)

    def landed(self):
        for at in range(SIDE):
            self.side(self.beside, at, 0).wait_recv()
            self.side(self.corner, at, SIDE).wait_recv()
        self.keep().wait()

    def finish(self):
        for at in range(SIDE):

            @pl.when((at <= self.col) & (self.col < SIDE - 1))
            def _(at=at):
                self.line(self.row, at, 1).wait_send()

            @pl.when((at >= self.col) & (self.col > 0))
            def _(at=at):
                self.line(self.row, at, -1).wait_send()

            self.over(at).wait_send()
            self.side(self.row, at, 0).wait_send()
            self.side(self.across, at, SIDE).wait_send()


def normalize(stream):
    mean_val = jnp.mean(stream, axis=-1, keepdims=True)
    spread = jnp.mean(stream * stream, axis=-1, keepdims=True) - mean_val * mean_val
    inverse = lax.rsqrt(spread + 1e-06)
    return ((stream - mean_val) * inverse, inverse)


def half_lanes(width):
    return lax.broadcasted_iota(jnp.int32, (ROWS, width), 1) < HEAD


def one_half(pair, low, which):
    keep = low if which == 0 else jnp.logical_not(low)
    return jnp.where(keep, pair.astype(f32), 0.0).astype(bf16)


def softmax_rows(queries, keys):
    scores = dot(queries, keys, ((1,), (1,))) * HEAD ** (-0.5)
    place = lax.broadcasted_iota(jnp.int32, scores.shape, 1)
    scores = jnp.where(place < SEQ, scores, -1e30)
    top = jnp.max(scores, axis=-1, keepdims=True)
    grown = jnp.exp(scores - top)
    return grown / jnp.sum(grown, axis=-1, keepdims=True)


class Fold:
    SIDE_SEND, SIDE_RECV, OVER_SEND, OVER_RECV, LINE_SEND, LINE_RECV = 0, 8, 16, 20, 24, 28
    COUNT = 36

    def __init__(self, part, beside, across, line, sems):
        self.part, self.from_beside = part, beside
        self.from_across, self.from_line, self.sems = across, line, sems
        self.row, self.col, self.across, self.beside = position()
        self.corner = lax.rem(self.beside + 2, SIDE)

    def block(self, far, at):
        return self.part((self.across if far else self.row) * SIDE + at)

    def side(self, far, at):
        row = self.corner if far else self.beside
        return remote(
            self.part(row * SIDE + at),
            self.from_beside.at[far, at],
            self.sems.at[self.SIDE_SEND + 4 * far + at],
            self.sems.at[self.SIDE_RECV + 4 * far + at],
            row=self.beside,
            col=self.col,
        )

    def over(self, at):
        return remote(
            self.block(1, at),
            self.from_across.at[at],
            self.sems.at[self.OVER_SEND + at],
            self.sems.at[self.OVER_RECV + at],
            row=self.across,
            col=self.col,
        )

    def line(self, at, toward):
        place = at if toward > 0 else SIDE + at
        return remote(
            self.block(0, at),
            self.from_line.at[place],
            self.sems.at[self.LINE_SEND + at],
            self.sems.at[self.LINE_RECV + place],
            row=self.row,
            col=self.col + toward,
        )

    def come(self, at, toward):
        place = at if toward > 0 else SIDE + at
        return remote(
            self.block(0, at),
            self.from_line.at[place],
            self.sems.at[self.LINE_SEND + at],
            self.sems.at[self.LINE_RECV + place],
            row=self.row,
            col=self.col - toward,
        )

    def add(self, far, at, other):
        block = self.block(far, at)
        block[...] = (block[...].astype(f32) + other[...].astype(f32)).astype(bf16)

    def start(self):
        for far in (1, 0):
            for at in ORDER:
                self.side(far, at).start()

    def fold_side(self, far):
        for at in ORDER:
            self.side(far, at).wait_recv()
            self.add(far, at, self.from_beside.at[far, at])
            if far:
                self.over(at).start()

    def fold_line(self, at):
        self.over(at).wait_recv()
        self.add(0, at, self.from_across.at[at])

        @pl.when(at > self.col)
        def _():
            @pl.when(self.col > 0)
            def _():
                self.come(at, 1).wait_recv()
                self.add(0, at, self.from_line.at[at])

            self.line(at, 1).start()

        @pl.when(at < self.col)
        def _():
            @pl.when(self.col < SIDE - 1)
            def _():
                self.come(at, -1).wait_recv()
                self.add(0, at, self.from_line.at[SIDE + at])

            self.line(at, -1).start()

    def land(self):
        @pl.when(self.col > 0)
        def _():
            self.come(self.col, 1).wait_recv()
            self.add(0, self.col, self.from_line.at[self.col])

        @pl.when(self.col < SIDE - 1)
        def _():
            self.come(self.col, -1).wait_recv()
            self.add(0, self.col, self.from_line.at[SIDE + self.col])

    def result(self):
        return self.block(0, self.col)[...]

    def finish(self):
        for far in range(2):
            for at in range(SIDE):
                self.side(far, at).wait_send()
        for at in range(SIDE):
            self.over(at).wait_send()

            @pl.when(at > self.col)
            def _(at=at):
                self.line(at, 1).wait_send()

            @pl.when(at < self.col)
            def _(at=at):
                self.line(at, -1).wait_send()


def rows_of(index):
    return pl.ds(pl.multiple_of(index * ROWS, 8), ROWS)


BLOCK_ORDER = ('y1', 'p0', 'f1', 'pr1', 'c0', 'pr2', 'h1', 'px0', 'spot0', 'j1', 'f1', 'cx0', 'cr1', 'pr3', 'px1', 'px2', 'y1', 'px3', 'pf0', 'asm0', 'image1', 'f1', 'b0', 'cr2', 'clear0', 'image0', 'h1', 'cx1', 'a0', 'cx2', 'br1', 'f1', 'cr3', 'f1', 'pick0', 'h1', 'bx0', 'ar1', 'cx3', 'bx1', 'own0', 'h1', 'br2', 'h1', 'y1', 'ar2', 'br3', 'f1', 'ar3', 'pick1', 'bx2', 'ax0', 'j1', 'cf0', 'j1', 'ax1', 'f1', 'y1', 'takeg1', 'cs0', 'ax2', 'y1', 'bx3', 'h1', 'bf0', 'takex1', 'takeg0', 'ax3', 'af0', 'y1', 'gate0', 'h1', 'gate1', 'y1', 'j2', 'takex0', 'bs0', 'mine0', 'sent0', 'ex0', 'y1', 'j2', 'other0', 'ex2', 'j1', 'swap0', 'ps0', 'sent1', 'ex1', 'g1', 'as0', 'other1', 'ex3', 'g2', 'putg1', '1b0', '1f0', 'g2', 'gates0', 'putg0', 'g1', 'swap1', 'g1', '0b0', '0f0', 'k1', '1n0', 'putx1', '3b0', '1l3', '0n0', '0l3', '1l2', '1l0', 'k1', '0l2', '3n0', 'putx0', '2b0', '2n0', '3f0', 'k1', '0l0', '1l1', '0l1', 'wait0', '3l2', 'unimage1', 'k1', 'g1', '2f0', 'unimage0', 'small0', '3l0', 'sf0', '2l0', '3l3', 'out0', 'sn0', 'out1', '2l3', '3l1', 'sl3', 'k1', 'sl2', '2l2', 'k1', 'sl0', 'sl1', '2l1', 'k2', 'done0', 'sums0', 'done1')


def block_kernel(
    paired,
    x_in,
    dy_in,
    project_in,
    project_out,
    router_weight,
    gain_one,
    bias_one,
    gain_two,
    bias_two,
    eup_ref,
    edown_ref,
    routes_in,
    block_out,
    input_grad,
    small_out,
    up_out,
    down_out,
    x_ref,
    dy_ref,
    pack_ref,
    flat_routes,
    places,
    routes_ref,
    packs,
    w_in,
    w_out,
    w_route,
    vecs,
    normed_one,
    triple,
    mixed,
    hidden,
    normed_two,
    x_all,
    dy_all,
    up_ref,
    down_ref,
    pick,
    logit,
    gate_rows,
    own_gate,
    spots,
    slot_gate,
    slot_x,
    slot_g,
    out_sum,
    back_sum,
    gate_sum,
    gate_out,
    gate_part,
    gate_in,
    beside,
    across,
    line,
    small_part,
    small_beside,
    small_across,
    small_line,
    small_pair,
    weight_in,
    weight_out,
    route_sum,
    vec_sum,
    grad_hidden,
    grad_triple,
    theirs,
    spread_sems,
    fetch_send,
    fetch_recv,
    pass_send,
    pass_recv,
    keep_sems,
    fold_sems,
    gate_send,
    gate_recv,
    swap_send,
    swap_recv,
    give_send,
    give_recv,
    retain_sems,
    pair_sems,
):
    row, col, across_row, beside_row = position()
    corner_row = lax.rem(beside_row + 2, SIDE)
    rank = row * SIDE + col
    half = lax.axis_index("dp") if paired else None
    partner = 1 - half if paired else None

    greet(partner)
    for source, target in ((x_in, x_ref), (dy_in, dy_ref)):
        target[...] = jnp.zeros_like(target)
        for m in range(2):
            target[m, :SEQ, :] = source[:, m, :]
    pack_ref[:PART, :288] = project_in[...]
    pack_ref[:PART, 288:] = project_out[...]
    pack_ref[PART:, :] = jnp.zeros((PACK - PART, D), bf16)
    vectors = [v[...].astype(f32) for v in (gain_one, bias_one, gain_two, bias_two)]
    tail = jnp.concatenate(
        [router_weight[...].astype(f32)] + vectors + [jnp.zeros((4, PART), f32)], axis=0
    )
    pack_ref[PART:, :PART] = tail.astype(bf16)
    meet(partner)

    def load_routes():
        flat_routes[...] = jnp.full_like(flat_routes, -1)
        for index in range(SHARES):
            for m in range(2):
                flat_routes[TOP * m : TOP * (m + 1), index * ROWS : index * ROWS + SEQ] = routes_in[
                    m, :, index * SEQ : (index + 1) * SEQ
                ]
        places[...] = jnp.full_like(places, -1)

        @pl.loop(0, CHUNKS)
        def _(i):
            lanes = pl.ds(pl.multiple_of(i * LANES, LANES), LANES)
            for pair in range(2 * TOP):
                places[pair // TOP, pair % TOP, pl.ds(i, 1), :] = flat_routes[
                    pair : pair + 1, lanes
                ]

        own = flat_routes[:, :ROWS]
        for index in range(1, SHARES):
            own = jnp.where(rank == index, flat_routes[:, index * ROWS : (index + 1) * ROWS], own)
        routes_ref[...] = jnp.transpose(own.astype(f32))

    low = half_lanes(2 * HEAD)
    tokens = [
        Spread(
            normed_two.at[m],
            lambda r, c, m=m: x_all.at[m, rows_of(r * SIDE + c)],
            spread_sems.at[2 + m],
        )
        for m in range(2)
    ]
    spreads = {
        "p": Spread(pack_ref, lambda r, c: packs.at[r * SIDE + c], spread_sems.at[0]),
        "c": Spread(dy_ref, lambda r, c: dy_all.at[:, rows_of(r * SIDE + c)], spread_sems.at[1]),
        "a": tokens[0],
        "b": tokens[1],
    }

    def assemble():
        for r in range(SIDE):
            for c in range(SIDE):
                at = r * SIDE + c
                w_in[c * PART : (c + 1) * PART, r * 288 : (r + 1) * 288] = packs[at, :PART, :288]
                w_out[r * PART : (r + 1) * PART, c * PART : (c + 1) * PART] = packs[at, :PART, 288:]
                tail = packs[at, PART:, :PART].astype(f32)
                w_route[r * 8 : (r + 1) * 8, c * PART : (c + 1) * PART] = tail[:8]
                if r == 0:
                    vecs[:, c * PART : (c + 1) * PART] = tail[8:]

    def attend(m):
        stream = x_ref[m].astype(f32)
        normal, _ = normalize(stream)
        first = (normal * vecs[0:1] + vecs[1:2]).astype(bf16)
        normed_one[m] = first
        triple[m] = dot(first, w_in[...], ((1,), (0,))).astype(bf16)
        for pair in range(HEADS // 2):
            lanes = 2 * HEAD * pair
            queries = triple[m, :, lanes : lanes + 128]
            keys = triple[m, :, D + lanes : D + lanes + 128]
            values = triple[m, :, 2 * D + lanes : 2 * D + lanes + 128]
            parts = []
            for which in range(2):
                prob = softmax_rows(queries, one_half(keys, low, which)).astype(bf16)
                parts.append(dot(prob, values, ((1,), (0,))))
            mixed[m, :, lanes : lanes + 128] = jnp.where(low, parts[0], parts[1]).astype(bf16)
        after = stream + dot(mixed[m], w_out[...], ((1,), (0,)))
        hidden[m] = after
        normal, _ = normalize(after)
        normed_two[m] = (normal * vecs[2:3] + vecs[3:4]).astype(bf16)

    mats = ((eup_ref, up_ref), (edown_ref, down_ref))
    shares = (half,) if paired else (0, 1)

    def into(whole, own, owner):
        return whole.at[own, owner // SIDE, pl.ds(lax.rem(owner, SIDE) * PART, PART), :]

    def fetch(number, mat, own, step):
        blocks, whole = mats[mat]
        to, _ = peer(step)
        return remote(
            blocks.at[own * SHARES + to],
            into(whole, own, rank),
            fetch_send.at[number, mat, step],
            fetch_recv.at[number, mat, step],
            row=to // SIDE,
            col=lax.rem(to, SIDE),
        )

    def arrival(number, mat, own, step):
        _, source = peer(step)
        block = into(mats[mat][1], own, source)
        return remote(
            block,
            block,
            fetch_send.at[number, mat, step],
            fetch_recv.at[number, mat, step],
            row=source // SIDE,
            col=lax.rem(source, SIDE),
        )

    def hand(mat, step):
        blocks, whole = mats[mat]
        _, source = peer(step)
        block = into(whole, half, source)
        src = blocks.at[half * SHARES + rank] if isinstance(step, int) else block
        return remote(src, block, pass_send.at[mat, step], pass_recv.at[mat, step], dp=partner)

    def keep(number, mat, own):
        blocks, whole = mats[mat]
        return pltpu.make_async_copy(
            blocks.at[own * SHARES + rank], into(whole, own, rank), keep_sems.at[number, mat]
        )

    def begin_fetch():
        for number, own in enumerate(shares):
            for mat in range(2):
                keep(number, mat, own).start()
                if paired:
                    hand(mat, 0).start()

    def fetch_some(first, last):
        for number, own in enumerate(shares):

            @pl.loop(first, last)
            def _(step):
                for mat in range(2):
                    fetch(number, mat, own, step).start()

    def pass_some(first, last):
        for number, own in enumerate(shares):

            @pl.loop(first, last)
            def _(step):
                for mat in range(2):
                    arrival(number, mat, own, step).wait_recv()
                    if paired:
                        hand(mat, step).start()

    def have_own():
        for number, own in enumerate(shares):
            for mat in range(2):
                keep(number, mat, own).wait()

    def side_steps(number):
        return (number * SHARES // 2, (number + 1) * SHARES // 2)

    def have_other(number):
        if paired:

            @pl.loop(*side_steps(number))
            def _(step):
                for mat in range(2):
                    hand(mat, step).wait_recv()

    def handed(number):
        if paired:

            @pl.loop(*side_steps(number))
            def _(step):
                for mat in range(2):
                    hand(mat, step).wait_send()

    slot_place = lax.broadcasted_iota(jnp.int32, (SLOTS, LANES), 0).astype(f32)
    names = lax.broadcasted_iota(jnp.int32, (32, LANES), 0)

    def own_routes(m, q):
        mine = rank + SHARES * q
        return (places[m, 0] == mine, places[m, 1] == mine)

    def find_spots():
        load_routes()
        down_lane = lax.broadcasted_iota(jnp.int32, (LANES, LANES), 0)
        lane = lax.broadcasted_iota(jnp.int32, (LANES, LANES), 1)
        upper = jnp.where(down_lane <= lane, 1.0, 0.0).astype(bf16)
        below = lax.broadcasted_iota(jnp.int32, (32, 32), 0)
        above = lax.broadcasted_iota(jnp.int32, (32, 32), 1)
        earlier = jnp.where(below > above, 1.0, 0.0).astype(bf16)
        ones = jnp.ones((LANES, LANES), bf16)
        for m in range(2):
            for q in range(OWN):
                one, two = own_routes(m, q)
                routed = jnp.where(one | two, 1.0, 0.0).astype(bf16)
                within = dot(routed, upper, ((1,), (0,)))
                per_row = dot(routed, ones, ((1,), (0,))).astype(bf16)
                before = dot(earlier, per_row, ((1,), (0,)))
                spots[m, q] = jnp.where(one | two, within + before - 1.0, -1.0)

    def make_pick(m):
        @pl.loop(0, CHUNKS)
        def _(i):
            lanes = pl.ds(pl.multiple_of(i * LANES, LANES), LANES)
            for q in range(OWN):
                hit = spots[m, q, pl.ds(i, 1), :] == slot_place
                pick[m, q * SLOTS : (q + 1) * SLOTS, lanes] = jnp.where(hit, 1.0, 0.0).astype(bf16)

    def take(source, target, m):
        found = dot(pick[m], source[m], ((1,), (0,))).astype(bf16)
        for q in range(OWN):
            target[q, m * SLOTS : (m + 1) * SLOTS, :] = found[q * SLOTS : (q + 1) * SLOTS]

    def make_gates(m):
        logit[...] = dot(w_route[...].astype(bf16), x_all[m], ((1,), (1,)))
        for k in range(TOP):
            gate_rows[k] = jnp.zeros((32, LANES), f32)

        @pl.loop(0, CHUNKS)
        def _(i):
            piece = logit[:, pl.ds(pl.multiple_of(i * LANES, LANES), LANES)]
            for k in range(TOP):
                chosen = places[m, k, pl.ds(i, 1), :] == names
                gate_rows[k, pl.ds(i, 1), :] = jnp.sum(
                    jnp.where(chosen, piece, 0.0), axis=0, keepdims=True
                )

        first, second = gate_rows[0], gate_rows[1]
        top = jnp.maximum(first, second)
        first, second = jnp.exp(first - top), jnp.exp(second - top)
        total = first + second
        first, second = first / total, second / total
        rows = slice(m * SLOTS, (m + 1) * SLOTS)
        for q in range(OWN):
            one, two = own_routes(m, q)
            own_gate[q] = jnp.where(one, first, jnp.where(two, second, 0.0))
            slot_gate[q, rows, :] = jnp.zeros((SLOTS, LANES), f32)

        @pl.loop(0, CHUNKS)
        def _(i):
            for q in range(OWN):
                hit = spots[m, q, pl.ds(i, 1), :] == slot_place
                slot_gate[q, rows, :] += jnp.where(hit, own_gate[q, pl.ds(i, 1), :], 0.0)

        for q in range(OWN):
            slot_gate[q, rows, :] = jnp.broadcast_to(
                jnp.sum(slot_gate[q, rows, :], axis=1, keepdims=True), (SLOTS, LANES)
            )

    def expert(q, number):
        if number == 0:
            out_sum[q] = jnp.zeros((2 * SLOTS, D), f32)
            back_sum[q] = jnp.zeros((2 * SLOTS, D), f32)
            gate_sum[q] = jnp.zeros((2 * SLOTS, LANES), f32)
        near, far = ((row, beside_row), (across_row, corner_row))[number]

        @pl.loop(0, 2)
        def _(turn):
            f = jnp.where(turn == 0, near, far)
            inputs, cots = slot_x[q], slot_g[q]
            up, down = up_ref[q, f], down_ref[q, f]
            pre = dot(inputs, up, ((1,), (0,)))
            grad = dot(cots, down, ((1,), (0,)))
            cdf = 0.5 * (1.0 + lax.erf(pre * sqrt_half))
            act = pre * cdf
            gate = slot_gate[q][:, :1]
            scaled = (gate * act).astype(bf16)
            gate_sum[q] += jnp.broadcast_to(
                jnp.sum(grad * act, axis=1, keepdims=True), (2 * SLOTS, LANES)
            )
            slope = cdf + pre * jnp.exp(-0.5 * pre * pre) * inv_root_tau
            grad_pre = (gate * grad * slope).astype(bf16)
            out_sum[q] += dot(scaled, down, ((1,), (1,)))
            back_sum[q] += dot(grad_pre, up, ((1,), (1,)))
            up_ref[q, f] = dot(inputs, grad_pre, ((0,), (0,))).astype(bf16)
            down_ref[q, f] = dot(cots, scaled, ((0,), (0,))).astype(bf16)

        if number == 1:
            slot_x[q] = out_sum[q].astype(bf16)
            slot_g[q] = back_sum[q].astype(bf16)

    def put(source, target, m):
        rows = slice(m * SLOTS, (m + 1) * SLOTS)
        stacked = jnp.concatenate([source[0, rows, :], source[1, rows, :]], axis=0)

        @pl.loop(0, CHUNKS // 5)
        def _(i):
            there = pl.ds(pl.multiple_of(i * 5 * LANES, 5 * LANES), 5 * LANES)
            target[m, there, :] = dot(pick[m, :, there], stacked, ((0,), (0,))).astype(bf16)

    def gate_back():
        gate_part[...] = jnp.zeros_like(gate_part)
        for m in range(2):
            rows = slice(m * SLOTS, (m + 1) * SLOTS)
            for k in range(TOP):
                gate_out[m, k] = jnp.zeros((32, LANES), f32)

            @pl.loop(0, CHUNKS)
            def _(i):
                for q in range(OWN):
                    hit = spots[m, q, pl.ds(i, 1), :] == slot_place
                    found = jnp.sum(
                        jnp.where(hit, gate_sum[q, rows, :], 0.0), axis=0, keepdims=True
                    )
                    for k in range(TOP):
                        here = places[m, k, pl.ds(i, 1), :] == rank + SHARES * q
                        gate_out[m, k, pl.ds(i, 1), :] += jnp.where(here, found, 0.0)

            for to in range(SHARES):
                first = to * ROWS // LANES
                shift = to * ROWS - first * LANES
                span = -(-(shift + ROWS) // LANES)
                for k in range(TOP):
                    wide = jnp.concatenate(
                        [gate_out[m, k, first + n : first + n + 1, :] for n in range(span)], axis=1
                    )
                    gate_part[to, 2 * m + k : 2 * m + k + 1, :ROWS] = wide[:, shift : shift + ROWS]

    def gate_copy(step):
        to, _ = peer(step)
        return remote(
            gate_part.at[to],
            gate_in.at[rank],
            gate_send.at[step],
            gate_recv.at[step],
            row=to // SIDE,
            col=lax.rem(to, SIDE),
        )

    def gate_wait(step):
        _, source = peer(step)
        return remote(
            gate_part.at[rank],
            gate_in.at[source],
            gate_send.at[step],
            gate_recv.at[step],
            row=source // SIDE,
            col=lax.rem(source, SIDE),
        )

    def start_gates():
        gate_back()
        gate_in[rank] = gate_part[rank]

        @pl.loop(1, SHARES)
        def _(step):
            gate_copy(step).start()

    def wait_gates():
        @pl.loop(1, SHARES)
        def _(step):
            gate_wait(step).wait_recv()

    folds = [
        Fold(
            lambda index, n=n: (dy_all if n < 2 else x_all).at[n % 2, rows_of(index)],
            beside.at[n],
            across.at[n],
            line.at[n],
            fold_sems.at[n],
        )
        for n in range(4)
    ]
    small = Fold(
        lambda index: small_part.at[index], small_beside, small_across, small_line, fold_sems.at[4]
    )

    givers = ((up_ref, up_out), (down_ref, down_out))

    def swap(mat, step):
        to, _ = peer(step)
        return remote(
            into(givers[mat][0], partner, to),
            theirs.at[step, mat],
            swap_send.at[step, mat],
            swap_recv.at[step, mat],
            dp=partner,
        )

    def give(number, mat, q, step):
        to, _ = peer(step)
        return remote(
            into(givers[mat][0], q, to),
            givers[mat][1].at[rank if paired else q * SHARES + rank],
            give_send.at[number, mat, step],
            give_recv.at[number, mat, step],
            row=to // SIDE,
            col=lax.rem(to, SIDE),
        )

    def given(number, mat, q, step):
        _, source = peer(step)
        block = givers[mat][1].at[source if paired else q * SHARES + source]
        return remote(
            block,
            block,
            give_send.at[number, mat, step],
            give_recv.at[number, mat, step],
            row=source // SIDE,
            col=lax.rem(source, SIDE),
        )

    def retain(number, mat, q):
        return pltpu.make_async_copy(
            into(givers[mat][0], q, rank),
            givers[mat][1].at[rank if paired else q * SHARES + rank],
            retain_sems.at[number, mat],
        )

    def start_swap(number):
        if paired:

            @pl.loop(*side_steps(number))
            def _(step):
                for mat in range(2):
                    swap(mat, step).start()

    def give_some(first, last):
        for number, q in enumerate(shares):

            @pl.loop(first, last)
            def _(step):
                for mat in range(2):
                    if paired:
                        swap(mat, step).wait_recv()
                        to, _ = peer(step)
                        block = into(givers[mat][0], half, to)
                        block[...] = (
                            block[...].astype(f32) + theirs[step, mat].astype(f32)
                        ).astype(bf16)

                    @pl.when(step > 0)
                    def _():
                        give(number, mat, q, step).start()

                    @pl.when(step == 0)
                    def _():
                        retain(number, mat, q).start()

    token_names = lax.broadcasted_iota(jnp.int32, (ROWS, 32), 1).astype(f32)
    exact = lax.Precision.HIGHEST

    def clear_sums():
        weight_in[...] = jnp.zeros_like(weight_in)
        weight_out[...] = jnp.zeros_like(weight_out)
        route_sum[...] = jnp.zeros_like(route_sum)
        vec_sum[...] = jnp.zeros_like(vec_sum)

    def norm_back(grad_out, normal, inverse, which):
        scaled = grad_out * vecs[which : which + 1]
        vec_sum[which : which + 1] += jnp.sum(grad_out * normal, axis=0, keepdims=True)
        vec_sum[which + 1 : which + 2] += jnp.sum(grad_out, axis=0, keepdims=True)
        return inverse * (
            scaled
            - jnp.mean(scaled, axis=-1, keepdims=True)
            - normal * jnp.mean(scaled * normal, axis=-1, keepdims=True)
        )

    def attend_back(m):
        folds[m].land()
        grad_norm = folds[m].result().astype(f32)
        router = w_route[...]
        logits = dot(normed_two[m], router.astype(bf16), ((1,), (1,)))
        hits = [
            routes_ref[:, TOP * m + k : TOP * m + k + 1] == token_names for k in range(TOP)
        ]
        picked = [jnp.sum(jnp.where(hit, logits, 0.0), axis=1, keepdims=True) for hit in hits]
        top = jnp.maximum(picked[0], picked[1])
        grown = [jnp.exp(v - top) for v in picked]
        total = grown[0] + grown[1]
        gates = [v / total for v in grown]
        columns = jnp.transpose(jnp.sum(gate_in[...], axis=0))[:ROWS]
        grads = [columns[:, 2 * m + k : 2 * m + k + 1] for k in range(TOP)]
        mean_grad = gates[0] * grads[0] + gates[1] * grads[1]
        dense = jnp.zeros((ROWS, 32), f32)
        for k in range(TOP):
            dense = dense + jnp.where(hits[k], gates[k] * (grads[k] - mean_grad), 0.0)
        route_sum[...] += lax.dot_general(
            dense,
            normed_two[m].astype(f32),
            (((0,), (0,)), ((), ())),
            preferred_element_type=f32,
            precision=exact,
        )
        grad_norm = grad_norm + lax.dot_general(
            dense, router, (((1,), (0,)), ((), ())), preferred_element_type=f32, precision=exact
        )
        normal, inverse = normalize(hidden[m])
        into_hidden = dy_ref[m].astype(f32) + norm_back(grad_norm, normal, inverse, 2)
        grad_hidden[m] = into_hidden
        grad_attn = into_hidden.astype(bf16)
        weight_out[...] += dot(mixed[m], grad_attn, ((0,), (0,)))
        grad_mixed = dot(grad_attn, w_out[...], ((1,), (1,))).astype(bf16)
        grad_triple[m, :, :D] = grad_mixed

        @pl.loop(0, HEADS // 2)
        def _(pair):
            def lanes(n):
                return pl.ds(pl.multiple_of(n * D + pair * 128, 128), 128)

            queries, keys, values = (triple[m, :, lanes(n)] for n in range(3))
            cots = grad_triple[m, :, lanes(0)]
            parts = []
            for which in range(2):
                prob = softmax_rows(queries, one_half(keys, low, which))
                weights = prob.astype(bf16)
                grad_prob = dot(cots, one_half(values, low, which), ((1,), (1,)))
                grad_scores = prob * (
                    grad_prob - jnp.sum(prob * grad_prob, axis=-1, keepdims=True)
                )
                grad_scores = grad_scores.astype(bf16)
                parts.append(
                    (
                        dot(grad_scores, keys, ((1,), (0,))) * HEAD ** (-0.5),
                        dot(grad_scores, queries, ((0,), (0,))) * HEAD ** (-0.5),
                        dot(weights, cots, ((0,), (0,))),
                    )
                )
            for n in range(3):
                grad_triple[m, :, lanes(n)] = jnp.where(
                    low, parts[0][n], parts[1][n]
                ).astype(bf16)

        weight_in[...] += dot(normed_one[m], grad_triple[m], ((0,), (0,)))
        grad_norm = dot(grad_triple[m], w_in[...], ((1,), (1,)))
        normal, inverse = normalize(x_ref[m].astype(f32))
        grad_hidden[m] += norm_back(grad_norm, normal, inverse, 0)

    def write_grad(m):
        input_grad[:, m, :] = grad_hidden[m][:SEQ]

    def gather_small():
        for r in range(SIDE):
            for c in range(SIDE):
                at = r * SIDE + c
                small_part[at, :PART, :288] = weight_in[
                    c * PART : (c + 1) * PART, r * 288 : (r + 1) * 288
                ].astype(bf16)
                small_part[at, :PART, 288:] = weight_out[
                    r * PART : (r + 1) * PART, c * PART : (c + 1) * PART
                ].astype(bf16)
                tail = jnp.concatenate([route_sum[r * 8 : (r + 1) * 8, :], vec_sum[...]], axis=0)
                small_part[at, PART:, :PART] = tail[:, c * PART : (c + 1) * PART].astype(bf16)
                small_part[at, PART:, PART:] = jnp.zeros((16, D - PART), bf16)

    pair = None
    if paired:
        pair = remote(
            small_pair.at[0], small_pair.at[1], pair_sems.at[0], pair_sems.at[1], dp=partner
        )

    def end_small():
        small.land()
        if paired:
            small_pair[0] = small.result()
            pair.start()

    def finish_small():
        if paired:
            pair.wait_recv()
            small_out[...] = small.result().astype(f32) + small_pair[1].astype(f32)
            pair.wait_send()
        else:
            small_out[...] = small.result().astype(f32)

    def finish_branch(m):
        folds[2 + m].land()
        block_out[m] = (hidden[m] + folds[2 + m].result().astype(f32)).astype(bf16)[:SEQ]

    limits = {"f": SHARES // 2, "y": SHARES, "h": SHARES // 2, "j": SHARES, "g": SHARES // 2, "k": SHARES}
    at = {"f": 1, "y": SHARES // 2, "h": 1, "j": SHARES // 2, "g": 0, "k": SHARES // 2}
    ranged = {
        "f": fetch_some,
        "y": fetch_some,
        "h": pass_some,
        "j": pass_some,
        "g": give_some,
        "k": give_some,
    }
    plain = {
        "own": begin_fetch,
        "asm": assemble,
        "spot": find_spots,
        "mine": have_own,
        "gates": start_gates,
        "wait": wait_gates,
        "clear": clear_sums,
        "sums": end_small,
    }
    numbered = {
        "other": have_other,
        "sent": handed,
        "swap": start_swap,
        "image": attend,
        "pick": make_pick,
        "gate": make_gates,
        "takex": lambda m: take(x_all, slot_x, m),
        "takeg": lambda m: take(dy_all, slot_g, m),
        "putx": lambda m: put(slot_x, x_all, m),
        "putg": lambda m: put(slot_g, dy_all, m),
        "unimage": attend_back,
        "out": write_grad,
        "done": finish_branch,
    }
    for step in BLOCK_ORDER:
        name, number = step[:-1], int(step[-1], 16)
        if name in ranged:
            last = min(at[name] + number, limits[name])
            ranged[name](at[name], last)
            at[name] = last
        elif name in plain:
            plain[name]()
        elif name in numbered:
            numbered[name](number)
        elif name == "ex":
            expert(number // 2 if half is None else (half, partner)[number // 2], number % 2)
        elif name == "small":
            gather_small()
            small.start()
        elif name[0] in spreads:
            act = spreads[name[0]]
            if name[1:] == "":
                act.start()
            elif name[1:] == "r":
                act.relay(number)
            elif name[1:] == "x":
                act.cross(number)
            elif name[1:] == "f":
                act.landed()
            elif name[1:] == "s":
                act.finish()
        else:
            fold = small if name[0] == "s" else folds[int(name[0])]
            if name[1:] == "b":
                fold.start()
            elif name[1:] == "f":
                fold.fold_side(1)
            elif name[1:] == "n":
                fold.fold_side(0)
            else:
                fold.fold_line(number)
    finish_small()

    for fold in folds:
        fold.finish()
    small.finish()

    @pl.loop(1, SHARES)
    def _(step):
        gate_copy(step).wait_send()

    for number, q in enumerate(shares):
        for mat in range(2):
            retain(number, mat, q).wait()

        @pl.loop(1, SHARES)
        def _(step):
            for mat in range(2):
                fetch(number, mat, q, step).wait_send()

        for mat in range(2):

            @pl.loop(1, SHARES)
            def _(step):
                given(number, mat, q, step).wait_recv()
                give(number, mat, q, step).wait_send()

    if paired:

        @pl.loop(0, SHARES)
        def _(step):
            for mat in range(2):
                swap(mat, step).wait_send()


def block_call(paired, *operands):
    block, small = (ROWS, D), (PACK, D)
    experts = SHARES if paired else OWN * SHARES
    numbers = 1 if paired else 2
    outputs = [
        ((2, SEQ, D), bf16, VMEM),
        ((SEQ, 2, D), f32, VMEM),
        (small, f32, VMEM),
        ((experts, PART, FPART), bf16, ANY),
        ((experts, PART, FPART), bf16, ANY),
    ]
    scratch = [
        ((2,) + block, bf16),
        ((2,) + block, bf16),
        (small, bf16),
        ((8, TOKENS), jnp.int32),
        ((2, TOP, 32, LANES), jnp.int32),
        ((ROWS, 8), f32),
        ((SHARES,) + small, bf16),
        ((D, WIDE), bf16),
        ((D, D), bf16),
        ((32, D), f32),
        ((8, D), f32),
        ((2,) + block, bf16),
        ((2, ROWS, WIDE), bf16),
        ((2,) + block, bf16),
        ((2,) + block, f32),
        ((2,) + block, bf16),
        ((2, TOKENS, D), bf16),
        ((2, TOKENS, D), bf16),
        ((OWN, SIDE, D, FPART), bf16),
        ((OWN, SIDE, D, FPART), bf16),
        ((2, OWN * SLOTS, TOKENS), bf16),
        ((32, TOKENS), f32),
        ((TOP, 32, LANES), f32),
        ((OWN, 32, LANES), f32),
        ((2, OWN, 32, LANES), f32),
        ((OWN, 2 * SLOTS, LANES), f32),
        ((OWN, 2 * SLOTS, D), bf16),
        ((OWN, 2 * SLOTS, D), bf16),
        ((OWN, 2 * SLOTS, D), f32),
        ((OWN, 2 * SLOTS, D), f32),
        ((OWN, 2 * SLOTS, LANES), f32),
        ((2, TOP, 32, LANES), f32),
        ((SHARES, 8, 256), f32),
        ((SHARES, 8, 256), f32),
        ((4, 2, SIDE) + block, bf16),
        ((4, SIDE) + block, bf16),
        ((4, 2 * SIDE) + block, bf16),
        ((SHARES,) + small, bf16),
        ((2, SIDE) + small, bf16),
        ((SIDE,) + small, bf16),
        ((2 * SIDE,) + small, bf16),
        ((2,) + small, bf16),
        ((D, WIDE), f32),
        ((D, D), f32),
        ((32, D), f32),
        ((8, D), f32),
        ((2,) + block, f32),
        ((2, ROWS, WIDE), bf16),
        ((SHARES, 2, PART, FPART) if paired else (1, 2, 16, LANES), bf16),
    ]
    semaphores = [
        (4, Spread.COUNT),
        (numbers, 2, SHARES),
        (numbers, 2, SHARES),
        (2, SHARES),
        (2, SHARES),
        (numbers, 2),
        (5, Fold.COUNT),
        (SHARES,),
        (SHARES,),
        (SHARES, 2),
        (SHARES, 2),
        (numbers, 2, SHARES),
        (numbers, 2, SHARES),
        (numbers, 2),
        (2,),
    ]
    return pl.pallas_call(
        functools.partial(block_kernel, paired),
        out_shape=[jax.ShapeDtypeStruct(shape, kind) for shape, kind, _ in outputs],
        in_specs=[VMEM] * 9 + [ANY, ANY, VMEM],
        out_specs=[space for _, _, space in outputs],
        scratch_shapes=[pltpu.VMEM(shape, kind) for shape, kind in scratch]
        + [DMA(shape) for shape in semaphores],
        compiler_params=pltpu.CompilerParams(
            collective_id=0, has_side_effects=True, vmem_limit_bytes=63 << 20
        ),
        name="block",
    )(*operands)


def final_kernel(
    output, grad, small, up, down, output_rows, grad_rows, g_in, g_out, *rest
):
    *g_vecs, g_router, g_up, g_down = rest
    g_up[...] = up[...].astype(f32)
    g_down[...] = down[...].astype(f32)

    step = pl.program_id(0)
    for m in range(2):

        @pl.when(step == m)
        def _(m=m):
            output_rows[:, m, :] = output[m]

    @pl.when(step == 2)
    def _():
        grad_rows[...] = grad[...]

    @pl.when(step == 0)
    def _():
        g_in[...] = small[:PART, :288]
        g_out[...] = small[:PART, 288:]
        g_router[...] = small[PART : PART + 8, :PART]
        for n in range(4):
            g_vecs[n][...] = small[PART + 8 + n : PART + 9 + n, :PART]


def final_call(output, grad, small, up, down):
    steps = 4
    rows = up.shape[0] * PART // steps
    shape = up.shape
    up, down = (v.reshape(-1, FPART) for v in (up, down))
    blocks = pl.BlockSpec((rows, FPART), lambda i: (i, 0))

    def whole(*shape):
        return pl.BlockSpec(shape, lambda i: (0,) * len(shape))

    sizes = [
        ((SEQ, 2, D), bf16),
        ((SEQ, 2, D), f32),
        ((PART, 288), f32),
        ((PART, PART), f32),
        ((1, PART), f32),
        ((1, PART), f32),
        ((1, PART), f32),
        ((1, PART), f32),
        ((8, PART), f32),
        (up.shape, f32),
        (up.shape, f32),
    ]
    *rest, g_up, g_down = pl.pallas_call(
        final_kernel,
        grid=(steps,),
        out_shape=[jax.ShapeDtypeStruct(shape, kind) for shape, kind in sizes],
        in_specs=[whole(2, SEQ, D), whole(SEQ, 2, D), whole(PACK, D), blocks, blocks],
        out_specs=[whole(*shape) for shape, _ in sizes[:9]] + [blocks, blocks],
        name="final",
    )(output, grad, small, up, down)
    return (*rest, g_up.reshape(shape), g_down.reshape(shape))


def on_device(
    block_input,
    first_gain,
    first_bias,
    project_in,
    project_out,
    second_gain,
    second_bias,
    router_weight,
    expert_up,
    expert_down,
    routes,
    out_grad,
):
    paired = lax.axis_size("dp") == 2
    block_output, input_grad, small, up_sum, down_sum = block_call(
        paired,
        block_input.transpose(1, 0, 2),
        out_grad.transpose(1, 0, 2),
        project_in,
        project_out,
        router_weight.T,
        first_gain[None],
        first_bias[None],
        second_gain[None],
        second_bias[None],
        expert_up,
        expert_down,
        routes.transpose(0, 2, 1),
    )
    if not paired:
        small = lax.psum(small, "dp")
        up_sum = lax.psum_scatter(up_sum, "dp", scatter_dimension=0, tiled=True)
        down_sum = lax.psum_scatter(down_sum, "dp", scatter_dimension=0, tiled=True)
    output, grad, g_in, g_out, *g_vecs, g_router, g_up, g_down = final_call(
        block_output, input_grad, small, up_sum, down_sum
    )
    return (
        output.transpose(1, 0, 2),
        grad.transpose(1, 0, 2),
        g_vecs[0][0],
        g_vecs[1][0],
        g_in,
        g_out,
        g_vecs[2][0],
        g_vecs[3][0],
        g_router.T,
        g_up,
        g_down,
    )


def solution(mesh):
    in_specs = (
        P(None, ("dp", "row", "col"), None),
        P("col"),
        P("col"),
        P("col", "row"),
        P("row", "col"),
        P("col"),
        P("col"),
        P("col", "row"),
        P(None, "col", "row"),
        P(None, "col", "row"),
        P(None, "dp", None),
        P(None, ("dp", "row", "col"), None),
    )
    out_specs = (
        P(None, ("dp", "row", "col"), None),
        P(None, ("dp", "row", "col"), None),
        P("col"),
        P("col"),
        P("col", "row"),
        P("row", "col"),
        P("col"),
        P("col"),
        P("col", "row"),
        P("dp", "col", "row"),
        P("dp", "col", "row"),
    )
    return jax.shard_map(
        on_device, mesh=mesh, in_specs=in_specs, out_specs=out_specs, check_vma=False
    )
```
